32 devices in a mesh: fsdp: 8 (over y, x, core), seq: 4 (over z).
Axes of the slice: x: 2, y: 2, z: 4, core: 2. Of those that a mesh axis runs over, the one named last changes fastest.
Arguments:
- inputs: bfloat16 [8, 1568, 1024], P('fsdp', 'seq'), may hold values from -6 to 6
- clip_mask: int32 [8], P('fsdp'), may hold values 0 or 1
- ln1_gain: float32 [1024], replicated, may hold values from 0.5 to 1.5
- ln1_bias: float32 [1024], replicated, may hold values from -1 to 1
- w_query: bfloat16 [1024, 1024], P('fsdp'), may hold values from -0.1875 to 0.1875
- b_query: float32 [1024], replicated, may hold values from -1 to 1
- w_key: bfloat16 [1024, 1024], P('fsdp'), may hold values from -0.1875 to 0.1875
- w_value: bfloat16 [1024, 1024], P('fsdp'), may hold values from -0.1875 to 0.1875
- b_value: float32 [1024], replicated, may hold values from -1 to 1
- w_out: bfloat16 [1024, 1024], P('fsdp'), may hold values from -3 to 3
- b_out: float32 [1024], replicated, may hold values from -1 to 1
- ln2_gain: float32 [1024], replicated, may hold values from 0.5 to 1.5
- ln2_bias: float32 [1024], replicated, may hold values from -1 to 1
- w_fc1: bfloat16 [1024, 4096], P('fsdp'), may hold values from -0.1875 to 0.1875
- b_fc1: float32 [4096], replicated, may hold values from -1 to 1
- w_fc2: bfloat16 [4096, 1024], P('fsdp'), may hold values from -0.09375 to 0.09375
- b_fc2: float32 [1024], replicated, may hold values from -1 to 1
- cotangent: bfloat16 [8, 1568, 1024], P('fsdp', 'seq'), may hold values from -6 to 6
Outputs:
- output: bfloat16 [8, 1568, 1024], P('fsdp', 'seq')
- grad_inputs: float32 [8, 1568, 1024], P('fsdp', 'seq')
- grad_ln1_gain: float32 [1024], P(('fsdp', 'seq'))
- grad_ln1_bias: float32 [1024], P(('fsdp', 'seq'))
- grad_w_query: float32 [1024, 1024], P(('fsdp', 'seq'))
- grad_b_query: float32 [1024], P(('fsdp', 'seq'))
- grad_w_key: float32 [1024, 1024], P(('fsdp', 'seq'))
- grad_w_value: float32 [1024, 1024], P(('fsdp', 'seq'))
- grad_b_value: float32 [1024], P(('fsdp', 'seq'))
- grad_w_out: float32 [1024, 1024], P(('fsdp', 'seq'))
- grad_b_out: float32 [1024], P(('fsdp', 'seq'))
- grad_ln2_gain: float32 [1024], P(('fsdp', 'seq'))
- grad_ln2_bias: float32 [1024], P(('fsdp', 'seq'))
- grad_w_fc1: float32 [1024, 4096], P(('fsdp', 'seq'))
- grad_b_fc1: float32 [4096], P(('fsdp', 'seq'))
- grad_w_fc2: float32 [4096, 1024], P(('fsdp', 'seq'))
- grad_b_fc2: float32 [1024], P(('fsdp', 'seq'))
The draws below stay inside these ranges and needn't reach their ends.
Inputs may be any that keep to these rules, and one draw needn't show every extreme that they name: `clip_mask`: 1 where the clip's slot holds a clip, 0 where it holds none.
All inputs are finite; a program needn't handle non-finite values. No bound on the sum of `clip_mask` on one device may be relied on, other than what follows from the above.
Results may differ from the reference program's by a relative error of at most 0.011.
Values may be sent and summed in bfloat16 or wider, within the bound.
No kernel may reach another device: no remote copies, remote signals or barrier semaphores. Data moves between devices by JAX's collectives and lax.ppermute only.
A program may use at most 256 MiB of HBM per device.

```python
from functools import partial
import jax
import jax.numpy as jnp
from jax import lax

D = 1024
HEADS = 16
HD = 64
FF = 4096
L = 1568
CLIPS = 8


def touch_ends(values, rng, low, high):
    place = [jax.random.randint(jax.random.fold_in(rng, axis), (), 0, length) for axis, length in enumerate(values.shape)]
    longest = values.shape.index(max(values.shape))
    next_to = place[:longest] + [(place[longest] + 1) % values.shape[longest]] + place[longest + 1:]
    return values.at[tuple(place)].set(low).at[tuple(next_to)].set(high)


def shard_levels(stream_key, dims, pieces, least, largest):
    factor_of = 1.0
    for position, shards_of in pieces:
        draws = jax.random.uniform(jax.random.fold_in(jax.random.fold_in(stream_key, 6), position), (shards_of,), jnp.float32, least / len(pieces), largest / len(pieces))
        factor_of = factor_of * jnp.repeat(jnp.exp(draws), dims[position] // shards_of).reshape((-1,) + (1,) * (len(dims) - 1 - position))
    return factor_of


def centred(own_key, extent, scale, limit, shards=(), dtype=jnp.bfloat16):
    values = scale * jax.random.normal(own_key, extent, jnp.float32)
    if shards:
        values = values * shard_levels(own_key, extent, shards, -0.22, 0.18)
    return jnp.clip(values, -limit, limit).astype(dtype)


def setup_inputs(seed: int = 0) -> dict:
    arg_keys = jax.random.split(jax.random.key(seed), 19)
    return {
        "inputs": centred(arg_keys[0], (CLIPS, L, D), 1.0, 6.0, ((0, 8), (1, 4))),
        "clip_mask": touch_ends((jax.random.randint(arg_keys[1], (CLIPS,), 0, 4) < 3).astype(jnp.int32), jax.random.fold_in(arg_keys[1], 1), 0, 1),
        "ln1_gain": jnp.clip(1.0 + 0.1 * jax.random.normal(arg_keys[2], (D,), jnp.float32), 0.5, 1.5),
        "ln1_bias": centred(arg_keys[3], (D,), 0.2, 1.0, (), jnp.float32),
        "w_query": centred(arg_keys[4], (D, D), D ** -0.5, 0.1875, ((0, 8),)),
        "b_query": centred(arg_keys[5], (D,), 0.2, 1.0, (), jnp.float32),
        "w_key": centred(arg_keys[6], (D, D), D ** -0.5, 0.1875, ((0, 8),)),
        "w_value": centred(arg_keys[7], (D, D), D ** -0.5, 0.1875, ((0, 8),)),
        "b_value": centred(arg_keys[8], (D,), 0.2, 1.0, (), jnp.float32),
        "w_out": centred(arg_keys[9], (D, D), (max(D // 256, 1)) ** -0.5, 3.0, ((0, 8),)),
        "b_out": centred(arg_keys[10], (D,), 0.2, 1.0, (), jnp.float32),
        "ln2_gain": jnp.clip(1.0 + 0.1 * jax.random.normal(arg_keys[11], (D,), jnp.float32), 0.5, 1.5),
        "ln2_bias": centred(arg_keys[12], (D,), 0.2, 1.0, (), jnp.float32),
        "w_fc1": centred(arg_keys[13], (D, FF), D ** -0.5, 0.1875, ((0, 8),)),
        "b_fc1": centred(arg_keys[14], (FF,), 0.2, 1.0, (), jnp.float32),
        "w_fc2": centred(arg_keys[15], (FF, D), FF ** -0.5, 0.09375, ((0, 8),)),
        "b_fc2": centred(arg_keys[16], (D,), 0.2, 1.0, (), jnp.float32),
        "cotangent": centred(arg_keys[17], (CLIPS, L, D), 1.0, 6.0, ((0, 8), (1, 4))),
    }


@jax.custom_vjp
def low(v):
    return lax.optimization_barrier(v.astype(jnp.bfloat16)).astype(jnp.float32)

@jax.custom_vjp
def low_back(v):
    return v

def low_keep(v):
    return (low(v), None)

def low_pass(kept, grad):
    return (grad,)

def back_keep(v):
    return (v, None)

def back_low(kept, grad):
    return (low(grad),)
low.defvjp(low_keep, low_pass)
low_back.defvjp(back_keep, back_low)
EPSILON = 1e-06
HIGHEST = lax.Precision.HIGHEST

def matmul(left, right):
    return jnp.dot(left, right, precision=HIGHEST)

def normalize(rows, gain, shift):
    center = rows - lax.optimization_barrier(jnp.mean(rows, -1, keepdims=True))
    inverse = lax.rsqrt(lax.optimization_barrier(jnp.mean(center * center, -1, keepdims=True)) + EPSILON)
    return center * inverse * gain + shift

def clip_layer(params, blocks):
    rows, present = blocks
    ln1_gain, ln1_bias, w_query, b_query, w_key, w_value, b_value, w_out, b_out, ln2_gain, ln2_bias, w_fc1, b_fc1, w_fc2, b_fc2 = params
    tokens = rows.shape[0]
    first_in = low(normalize(rows, ln1_gain, ln1_bias))
    query = low(low_back(matmul(first_in, w_query) + b_query)).reshape(tokens, HEADS, HD)
    keys = low(low_back(matmul(first_in, w_key))).reshape(tokens, HEADS, HD)
    values = low(low_back(matmul(first_in, w_value) + b_value)).reshape(tokens, HEADS, HD)
    scores = low_back(jnp.einsum('qhd,khd->hqk', query, keys, precision=HIGHEST) * HD ** (-0.5))
    probs = low(jax.nn.softmax(scores, axis=-1))
    mixed = low(low_back(jnp.einsum('hqk,khd->qhd', probs, values, precision=HIGHEST)))
    mixed = mixed.reshape(tokens, HEADS * HD)
    branch = low_back(matmul(mixed, w_out) + b_out)
    middle = rows + branch
    second_in = low(normalize(middle, ln2_gain, ln2_bias))
    hidden = low_back(matmul(second_in, w_fc1) + b_fc1)
    activ = low(jax.nn.gelu(hidden, approximate=False))
    final = low_back(matmul(activ, w_fc2) + b_fc2)
    return (middle + final) * present

def reference(inputs, clip_mask, ln1_gain, ln1_bias, w_query, b_query, w_key, w_value, b_value, w_out, b_out, ln2_gain, ln2_bias, w_fc1, b_fc1, w_fc2, b_fc2, cotangent):
    present = clip_mask.astype(jnp.float32)
    params = tuple((p.astype(jnp.float32) for p in (ln1_gain, ln1_bias, w_query, b_query, w_key, w_value, b_value, w_out, b_out, ln2_gain, ln2_bias, w_fc1, b_fc1, w_fc2, b_fc2)))

    def forward(source, weights):
        return lax.map(jax.checkpoint(partial(clip_layer, weights)), (source, present))
    result, pull = jax.vjp(forward, inputs.astype(jnp.float32), params)
    grad_x, grads = pull(cotangent.astype(jnp.float32))
    return (result.astype(jnp.bfloat16), grad_x, grads[0], grads[1], grads[2], grads[3], grads[4], grads[5], grads[6], grads[7], grads[8], grads[9], grads[10], grads[11], grads[12], grads[13], grads[14])
```

```python
import functools
import math

import jax
import jax.numpy as jnp
from jax import lax
from jax.experimental import pallas as pl
from jax.experimental.pallas import tpu as pltpu
from jax.sharding import PartitionSpec as P

HD = 64
PAIR = 2 * HD
EPSILON = 1e-06
LOG2E = math.log2(math.e)
BF16 = jnp.bfloat16
F32 = jnp.float32
NT = (((1,), (1,)), ((), ()))
NN = (((1,), (0,)), ((), ()))
TN = (((0,), (0,)), ((), ()))


def dot(a, b, dims=NN):
    return lax.dot_general(a, b, dims, preferred_element_type=F32)


def normalize(rows, gain, shift):
    center = rows - jnp.mean(rows, -1, keepdims=True)
    inverse = lax.rsqrt(jnp.mean(center * center, -1, keepdims=True) + EPSILON)
    normed = center * inverse
    return (normed * gain + shift, normed, inverse)


def norm_grad(grad, normed, inverse, gain):
    scaled = grad * gain
    inner = (
        scaled
        - jnp.mean(scaled, -1, keepdims=True)
        - normed * jnp.mean(scaled * normed, -1, keepdims=True)
    )
    return inner * inverse


def forward_kernel(scale, q_ref, k_ref, v_ref, mixed_ref, exact_ref, lse_ref, value_sc):
    @pl.when(pl.program_id(1) == 0)
    def _():
        value_sc[:, :PAIR] = v_ref[...]
        value_sc[:, PAIR:] = jnp.ones((value_sc.shape[0], PAIR), value_sc.dtype)

    query = q_ref[...]
    keys = k_ref[...]
    first = lax.broadcasted_iota(jnp.int32, query.shape, 1) < HD
    outs, sums = [], []
    for head in range(2):
        mine = first if head == 0 else jnp.logical_not(first)
        scores = dot(jnp.where(mine, query, jnp.zeros_like(query)), keys, NT)
        peak = jnp.max(scores, -1, keepdims=True)
        expo = jnp.exp2((scores - peak) * scale).astype(BF16)
        both = dot(expo, value_sc[...])
        total = both[:, PAIR:]
        outs.append(both[:, :PAIR] / total)
        sums.append(peak * scale + jnp.log2(total[:, :1]))
    exact = jnp.where(first, outs[0], outs[1])
    exact_ref[...] = exact
    mixed_ref[...] = exact.astype(BF16)
    lse_ref[...] = jnp.concatenate(sums, 1)


def attention_forward(qkv, rows):
    length, width = qkv.shape[0], qkv.shape[1] // 3
    pairs = width // PAIR
    return pl.pallas_call(
        functools.partial(forward_kernel, HD**-0.5 * LOG2E),
        grid=(pairs, length // rows),
        in_specs=[
            pl.BlockSpec((rows, PAIR), lambda p, i: (i, p)),
            pl.BlockSpec((length, PAIR), lambda p, i: (0, pairs + p)),
            pl.BlockSpec((length, PAIR), lambda p, i: (0, 2 * pairs + p)),
        ],
        out_specs=[
            pl.BlockSpec((rows, PAIR), lambda p, i: (i, p)),
            pl.BlockSpec((rows, PAIR), lambda p, i: (i, p)),
            pl.BlockSpec((None, rows, 2), lambda p, i: (p, i, 0)),
        ],
        out_shape=[
            jax.ShapeDtypeStruct((length, width), BF16),
            jax.ShapeDtypeStruct((length, width), F32),
            jax.ShapeDtypeStruct((pairs, length, 2), F32),
        ],
        scratch_shapes=[pltpu.VMEM((length, 2 * PAIR), BF16)],
        compiler_params=pltpu.CompilerParams(vmem_limit_bytes=48 << 20),
        cost_estimate=pl.CostEstimate(
            flops=16 * length * length * width,
            transcendentals=length * length * width // HD,
            bytes_accessed=14 * length * width,
        ),
        name="attention_forward",
    )(qkv, qkv, qkv)


def backward_kernel(
    scale, q_ref, k_ref, v_ref, do_ref, exact_ref, lse_ref, dq_ref, dk_ref, dv_ref, dk_sc, dv_sc
):
    step = pl.program_id(1)

    @pl.when(step == 0)
    def _():
        dk_sc[...] = jnp.zeros_like(dk_sc)
        dv_sc[...] = jnp.zeros_like(dv_sc)

    query, keys, values, grad = q_ref[...], k_ref[...], v_ref[...], do_ref[...]
    first = lax.broadcasted_iota(jnp.int32, query.shape, 1) < HD
    product = grad.astype(F32) * exact_ref[...]
    dqs = []
    for head in range(2):
        mine = first if head == 0 else jnp.logical_not(first)
        zero = jnp.zeros_like(query)
        q_one = jnp.where(mine, query, zero)
        g_one = jnp.where(mine, grad, zero)
        inner = jnp.sum(jnp.where(mine, product, 0.0), -1, keepdims=True)
        probs = jnp.exp2(dot(q_one, keys, NT) * (scale * LOG2E) - lse_ref[:, head : head + 1])
        grad_scores = (probs * (dot(g_one, values, NT) - inner)).astype(BF16)
        dqs.append(dot(grad_scores, keys))
        dv_sc[...] += dot(g_one, probs.astype(BF16), TN)
        dk_sc[...] += dot(q_one, grad_scores, TN)
    dq_ref[...] = (jnp.where(first, dqs[0], dqs[1]) * scale).astype(BF16)

    @pl.when(step == pl.num_programs(1) - 1)
    def _():
        dk_ref[...] = (dk_sc[...] * scale).T.astype(BF16)
        dv_ref[...] = dv_sc[...].T.astype(BF16)


def attention_backward(qkv, grad, exact, lse, rows):
    length, width = qkv.shape[0], qkv.shape[1] // 3
    pairs = width // PAIR
    row = pl.BlockSpec((rows, PAIR), lambda p, i: (i, p))
    full = pl.BlockSpec((length, PAIR), lambda p, i: (0, p))
    return pl.pallas_call(
        functools.partial(backward_kernel, HD**-0.5),
        grid=(pairs, length // rows),
        in_specs=[
            row,
            pl.BlockSpec((length, PAIR), lambda p, i: (0, pairs + p)),
            pl.BlockSpec((length, PAIR), lambda p, i: (0, 2 * pairs + p)),
            row,
            row,
            pl.BlockSpec((None, rows, 2), lambda p, i: (p, i, 0)),
        ],
        out_specs=[row, full, full],
        out_shape=[jax.ShapeDtypeStruct((length, width), BF16)] * 3,
        scratch_shapes=[pltpu.VMEM((PAIR, length), F32)] * 2,
        compiler_params=pltpu.CompilerParams(vmem_limit_bytes=48 << 20),
        cost_estimate=pl.CostEstimate(
            flops=40 * length * length * width,
            transcendentals=length * length * width // HD,
            bytes_accessed=18 * length * width,
        ),
        name="attention_backward",
    )(qkv, qkv, qkv, grad, exact, lse)


def flip(array, bit, size):
    return lax.ppermute(array, "fsdp", [(i, i ^ (1 << bit)) for i in range(size)])


def shift(array, by, size):
    return lax.ppermute(array, "seq", [(i, (i + by) % size) for i in range(size)])


def gather_rows(shard, size):
    if size != 8:
        return lax.all_gather(shard, "fsdp", axis=0, tiled=True)
    half = shard.shape[0] // 2
    one, two = flip(shard, 1, size), flip(shard, 2, size)
    top, low = flip(one[:half], 2, size), flip(two[half:], 1, size)
    pieces = [shard, one, two, top, low]
    other = [flip(piece, 0, size) for piece in pieces]
    me = lax.axis_index("fsdp")
    rows, columns = shard.shape
    whole = jnp.zeros((size * rows, columns), shard.dtype)
    for near, group in enumerate((pieces, other)):
        for far, start, piece in zip((0, 2, 4, 6, 6), (0, 0, 0, 0, half), group):
            place = (me ^ (far + near)) * rows + start
            whole = lax.dynamic_update_slice(whole, piece, (place, 0))
    return whole


def reduce_rows(left, right, size):
    tokens, height = left.shape
    bits = size.bit_length() - 1
    me = lax.axis_index("fsdp")
    rest = height // size
    split = left.reshape(tokens, size // 2, 2, rest)

    def half_of(which):
        return lax.dynamic_index_in_dim(split, which, 2, False).reshape(tokens, height // 2)

    mine = me & 1
    away = dot(half_of(1 - mine), right, TN).astype(BF16)
    arrived = flip(away, 0, size)
    kept = dot(half_of(mine), right, TN)
    block = (kept + arrived.astype(F32)).astype(BF16)
    columns = right.shape[1]
    block = block.reshape((2,) * (bits - 1) + (rest, columns))
    order = list(range(1, bits))
    parts = []
    for part, way in ((block[..., : columns // 2], order), (block[..., columns // 2 :], order[::-1])):
        left_over = list(range(bits - 1, 0, -1))
        for bit in way:
            axis = left_over.index(bit)
            left_over.remove(bit)
            mine = (me >> bit) & 1
            away = lax.dynamic_index_in_dim(part, 1 - mine, axis, False)
            kept = lax.dynamic_index_in_dim(part, mine, axis, False)
            arrived = flip(away, bit, size)
            part = (kept.astype(F32) + arrived.astype(F32)).astype(BF16)
        parts.append(part)
    return jnp.concatenate(parts, 1)


def reduce_seq(block, size):
    me = lax.axis_index("seq")
    parts = block.reshape(size, block.shape[0] // size, block.shape[1])
    total = lax.dynamic_index_in_dim(parts, me, 0, False).astype(F32)
    for by in range(1, size):
        away = lax.dynamic_index_in_dim(parts, (me + by) % size, 0, False)
        total = total + shift(away, by, size).astype(F32)
    return total


def swap_seq(pieces, size):
    me = lax.axis_index("seq")
    came = [pieces[0]] + [shift(pieces[by], by, size) for by in range(1, size)]
    came = came[::-1]
    return lax.dynamic_slice_in_dim(jnp.stack(came + came), (size - 1 - me) % size, size, 0)


def reduce_vectors(vectors, fsdp, seq):
    me = lax.axis_index("fsdp")
    bits = fsdp.bit_length() - 1
    sizes = [v.shape[0] // (fsdp * seq) for v in vectors]
    block = jnp.concatenate([v.reshape(fsdp, seq, -1) for v in vectors], 2)
    block = block.reshape((2,) * bits + (seq, sum(sizes)))
    for bit in range(bits):
        axis = bits - 1 - bit
        mine = (me >> bit) & 1
        away = lax.dynamic_index_in_dim(block, 1 - mine, axis, False)
        block = lax.dynamic_index_in_dim(block, mine, axis, False) + flip(away, bit, fsdp)
    total = reduce_seq(block, seq)[0]
    return jnp.split(total, [sum(sizes[: i + 1]) for i in range(len(sizes) - 1)])


def on_device(
    fsdp,
    seq,
    inputs,
    clip_mask,
    ln1_gain,
    ln1_bias,
    w_query,
    b_query,
    w_key,
    w_value,
    b_value,
    w_out,
    b_out,
    ln2_gain,
    ln2_bias,
    w_fc1,
    b_fc1,
    w_fc2,
    b_fc2,
    cotangent,
):
    clips, local, width = inputs.shape
    assert clips == 1
    me = lax.axis_index("seq")
    own = width // seq
    present = clip_mask[0].astype(F32)

    def columns(array, axis):
        return lax.dynamic_slice_in_dim(array, me * own, own, axis)

    w_heads = gather_rows(
        jnp.concatenate([columns(w, 1) for w in (w_query, w_key, w_value)], 1), fsdp
    )
    b_heads = jnp.concatenate([columns(b_query, 0), jnp.zeros((own,), F32), columns(b_value, 0)])

    tokens = [inputs[0]] + [shift(inputs[0], -by, seq) for by in range(1, seq)]
    first_parts, qkv_parts = [], []
    for part in tokens:
        normed, _, _ = normalize(part.astype(F32), ln1_gain, ln1_bias)
        first_parts.append(normed.astype(BF16))
        qkv_parts.append((dot(first_parts[-1], w_heads) + b_heads).astype(BF16))
    first_in = jnp.concatenate(first_parts, 0)
    qkv = jnp.concatenate(qkv_parts, 0)
    mixed, exact, lse = attention_forward(qkv, 2 * local)

    full_out = gather_rows(w_out, fsdp)
    full_fc1 = gather_rows(w_fc1, fsdp)
    full_fc2 = gather_rows(w_fc2, fsdp)

    attended = swap_seq([mixed[j * local : (j + 1) * local] for j in range(seq)], seq)
    attended = attended.transpose(1, 0, 2).reshape(local, width)
    rows = inputs[0].astype(F32)
    middle = rows + dot(attended, full_out) + b_out
    normed2, hat2, inv2 = normalize(middle, ln2_gain, ln2_bias)
    second_in = normed2.astype(BF16)
    hidden = dot(second_in, full_fc1) + b_fc1
    cdf = 0.5 * (1.0 + lax.erf(hidden * (0.5**0.5)))
    activ = (hidden * cdf).astype(BF16)
    slope = cdf + hidden * jnp.exp(-0.5 * hidden * hidden) * ((2.0 * math.pi) ** -0.5)
    output = ((middle + dot(activ, full_fc2) + b_fc2) * present).astype(BF16)

    grad_rows = cotangent[0].astype(F32) * present
    grad_low = grad_rows.astype(BF16)
    part_fc2 = reduce_rows(activ, grad_low, fsdp)
    grad_hidden = (dot(grad_low, full_fc2, NT) * slope).astype(BF16)
    part_fc1 = reduce_rows(second_in, grad_hidden, fsdp)
    grad_second = dot(grad_hidden, full_fc1, NT)
    grad_middle = grad_rows + norm_grad(grad_second, hat2, inv2, ln2_gain)
    grad_branch = grad_middle.astype(BF16)
    grad_mixed = dot(grad_branch, full_out, NT).astype(BF16)

    grad_parts = [columns(grad_mixed, 1)]
    for by in range(1, seq):
        theirs = lax.dynamic_slice_in_dim(grad_mixed, ((me - by) % seq) * own, own, 1)
        grad_parts.append(shift(theirs, -by, seq))
    part_out = reduce_rows(attended, grad_branch, fsdp)
    dq, dk, dv = attention_backward(qkv, jnp.concatenate(grad_parts, 0), exact, lse, 2 * local)
    dqkv = jnp.concatenate([dq, dk, dv], 1)

    full_query = gather_rows(w_query, fsdp)
    full_key = gather_rows(w_key, fsdp)
    full_value = gather_rows(w_value, fsdp)
    back = swap_seq([dqkv[j * local : (j + 1) * local] for j in range(seq)], seq)
    back = back.reshape(seq, local, 3, own).transpose(2, 1, 0, 3).reshape(3, local, width)
    grad_first = (
        dot(back[0], full_query, NT) + dot(back[1], full_key, NT) + dot(back[2], full_value, NT)
    )
    _, hat1, inv1 = normalize(rows, ln1_gain, ln1_bias)
    grad_inputs = grad_middle + norm_grad(grad_first, hat1, inv1, ln1_gain)

    part_heads = reduce_rows(first_in, dqkv, fsdp)
    strip = part_heads.shape[0] // seq
    sent = [
        lax.dynamic_slice_in_dim(part_heads, ((me + j) % seq) * strip, strip, 0)
        for j in range(seq)
    ]
    heads = swap_seq(sent, seq).astype(F32)
    heads = heads.reshape(seq, strip, 3, own).transpose(2, 1, 0, 3).reshape(3, strip, width)

    def spread(vector):
        return lax.dynamic_update_slice(jnp.zeros((width,), F32), vector, (me * own,))

    sums = reduce_vectors(
        [
            jnp.sum(grad_first * hat1, 0),
            jnp.sum(grad_first, 0),
            spread(jnp.sum(dq.astype(F32), 0)),
            spread(jnp.sum(dv.astype(F32), 0)),
            jnp.sum(grad_branch.astype(F32), 0),
            jnp.sum(grad_second * hat2, 0),
            jnp.sum(grad_second, 0),
            jnp.sum(grad_hidden.astype(F32), 0),
            jnp.sum(grad_rows, 0),
        ],
        fsdp,
        seq,
    )
    return (
        output[None],
        grad_inputs[None],
        sums[0],
        sums[1],
        heads[0],
        sums[2],
        heads[1],
        heads[2],
        sums[3],
        reduce_seq(part_out, seq),
        sums[4],
        sums[5],
        sums[6],
        reduce_seq(part_fc1, seq),
        sums[7],
        reduce_seq(part_fc2, seq),
        sums[8],
    )


def solution(mesh):
    rows, both = P("fsdp", None), P(("fsdp", "seq"))
    tokens = P("fsdp", "seq", None)
    matrix = P(("fsdp", "seq"), None)
    return jax.shard_map(
        functools.partial(on_device, mesh.shape["fsdp"], mesh.shape["seq"]),
        mesh=mesh,
        in_specs=(
            tokens,
            P("fsdp"),
            P(),
            P(),
            rows,
            P(),
            rows,
            rows,
            P(),
            rows,
            P(),
            P(),
            P(),
            rows,
            P(),
            rows,
            P(),
            tokens,
        ),
        out_specs=(
            tokens,
            tokens,
            both,
            both,
            matrix,
            both,
            matrix,
            matrix,
            both,
            matrix,
            both,
            both,
            both,
            matrix,
            both,
            matrix,
            both,
        ),
        check_vma=False,
    )
```

```python
import functools
import math

import jax
import jax.numpy as jnp
from jax import lax
from jax.experimental import pallas as pl
from jax.experimental.pallas import tpu as pltpu
from jax.sharding import PartitionSpec as P

HD = 64
PAIR = 2 * HD
EPSILON = 1e-06
LOG2E = math.log2(math.e)
BF16 = jnp.bfloat16
F32 = jnp.float32
NT = (((1,), (1,)), ((), ()))
NN = (((1,), (0,)), ((), ()))
TN = (((0,), (0,)), ((), ()))
ANY = pl.BlockSpec(memory_space=pl.ANY)
SCALARS = pl.BlockSpec(memory_space=pltpu.SMEM)


def dot(a, b, dims=NN):
    return lax.dot_general(a, b, dims, preferred_element_type=F32)


def like(shape, dtype):
    return pltpu.HBM(shape, dtype)


def placed(*arrays):
    return [pltpu.with_memory_space_constraint(a, pltpu.HBM) for a in arrays]


def standard(rows):
    center = rows - jnp.mean(rows, -1, keepdims=True)
    inverse = lax.rsqrt(jnp.mean(center * center, -1, keepdims=True) + EPSILON)
    return center * inverse, inverse


def norm_grad(grad, normed, inverse, gain):
    scaled = grad * gain
    inner = (
        scaled
        - jnp.mean(scaled, -1, keepdims=True)
        - normed * jnp.mean(scaled * normed, -1, keepdims=True)
    )
    return inner * inverse


def params(mib):
    return pltpu.CompilerParams(vmem_limit_bytes=mib << 20)


def cost(flops, moved, special=0):
    return pl.CostEstimate(flops=flops // 64, bytes_accessed=moved // 64, transcendentals=0)


def piece_table(size):
    if size != 8:
        return [(None, None)]
    return [(far + near, half) for near in (0, 1) for far, half in
            ((0, None), (2, None), (4, None), (6, 0), (6, 1))]


def flip(array, bit, size):
    return lax.ppermute(array, "fsdp", [(i, i ^ (1 << bit)) for i in range(size)])


def shift(array, by, size):
    return lax.ppermute(array, "seq", [(i, (i + by) % size) for i in range(size)])


def gather_near(shard, size):
    return (flip(shard, 1, size), flip(shard, 2, size)) if size == 8 else ()


def gather_pieces(shard, near, size):
    if size != 8:
        return [lax.all_gather(shard, "fsdp", axis=0, tiled=True)]
    half = shard.shape[0] // 2
    one, two = near
    top, low = flip(one[:half], 2, size), flip(two[half:], 1, size)
    pieces = [shard, one, two, top, low]
    return pieces + [flip(piece, 0, size) for piece in pieces]


def piece_copies(table, me, refs, first, target, sems):
    width = target.shape[1]
    copies = []
    for i, ((rel, half), ref) in enumerate(zip(table, refs)):
        count = ref.shape[0]
        if rel is None:
            start = 0
        elif half is None:
            start = jnp.bitwise_xor(me, rel) * count
        else:
            start = jnp.bitwise_xor(me, rel) * (2 * count) + half * count
        source = ref.at[:, pl.ds(first, width)]
        place = target.at[pl.ds(start, count), :]
        copies.append(pltpu.make_async_copy(source, place, sems.at[i]))
    return copies


def block_copies(ref, first, target, sems):
    count = sems.shape[0]
    rows, width = target.shape[0] // count, target.shape[1]
    return [
        pltpu.make_async_copy(
            ref.at[pl.ds(i * rows, rows), pl.ds(first, width)],
            target.at[pl.ds(i * rows, rows), :],
            sems.at[i],
        )
        for i in range(count)
    ]


def project_kernel(seq, table, where_ref, *refs):
    own_ref, down_refs, up_refs = refs[0], refs[1:seq], refs[seq : 2 * seq - 1]
    refs = refs[2 * seq - 1 :]
    w_refs, refs = refs[: len(table)], refs[len(table) :]
    gain_ref, shift_ref, bias_ref, first_ref, qkv_ref, x_sc, w_sc, x_sem, w_sem = refs
    step = pl.program_id(0)
    copies = piece_copies(table, where_ref[0], w_refs, 0, w_sc, w_sem)

    @pl.when(step == 0)
    def _():
        for copy in copies:
            copy.start()
        pltpu.make_async_copy(own_ref, x_sc.at[0], x_sem.at[0]).start()
        for j in range(1, seq):
            inside = where_ref[1] + j < seq

            @pl.when(inside)
            def _(j=j):
                pltpu.make_async_copy(down_refs[j - 1], x_sc.at[j], x_sem.at[j]).start()

            @pl.when(jnp.logical_not(inside))
            def _(j=j):
                pltpu.make_async_copy(up_refs[seq - j - 1], x_sc.at[j], x_sem.at[j]).start()

        for copy in copies:
            copy.wait()

    pltpu.make_async_copy(own_ref, x_sc.at[step], x_sem.at[step]).wait()
    hat, _ = standard(x_sc[step].astype(F32))
    first = (hat * gain_ref[...] + shift_ref[...]).astype(BF16)
    first_ref[...] = first
    qkv_ref[...] = (dot(first, w_sc[...]) + bias_ref[...]).astype(BF16)


def project(where, seq, table, tokens, pieces, gain, shift_by, bias):
    local, width = tokens[0].shape
    columns = pieces[0].shape[1]
    vector = pl.BlockSpec((1, width), lambda i: (0, 0))
    return pl.pallas_call(
        functools.partial(project_kernel, seq, table),
        grid=(seq,),
        in_specs=[SCALARS] + [ANY] * (len(tokens) + len(pieces))
        + [vector, vector, pl.BlockSpec((1, columns), lambda i: (0, 0))],
        out_specs=[
            pl.BlockSpec((local, width), lambda i: (i, 0)),
            pl.BlockSpec((local, columns), lambda i: (i, 0)),
        ],
        out_shape=[
            like((seq * local, width), BF16),
            jax.ShapeDtypeStruct((seq * local, columns), BF16),
        ],
        scratch_shapes=[
            pltpu.VMEM((seq, local, width), BF16),
            pltpu.VMEM((width, columns), BF16),
            pltpu.SemaphoreType.DMA((seq,)),
            pltpu.SemaphoreType.DMA((len(table),)),
        ],
        compiler_params=params(32),
        cost_estimate=cost(2 * seq * local * width * columns, 6 * seq * local * width),
        name="project",
    )(where, *placed(*tokens, *pieces), gain[None], shift_by[None], bias[None])


def forward_kernel(scale, seq, q_ref, k_ref, v_ref, *refs):
    mixed_refs, (exact_ref, lse_ref, value_sc) = refs[:seq], refs[seq:]
    step = pl.program_id(0)

    @pl.when(step == 0)
    def _():
        value_sc[:, :PAIR] = v_ref[...]
        value_sc[:, PAIR:] = jnp.ones((value_sc.shape[0], PAIR), value_sc.dtype)

    query = q_ref[...]
    keys = k_ref[...]
    first = lax.broadcasted_iota(jnp.int32, query.shape, 1) < HD
    outs, sums = [], []
    for head in range(2):
        mine = first if head == 0 else jnp.logical_not(first)
        scores = dot(jnp.where(mine, query, jnp.zeros_like(query)), keys, NT)
        peak = jnp.max(scores, -1, keepdims=True)
        expo = jnp.exp2((scores - peak) * scale).astype(BF16)
        both = dot(expo, value_sc[...])
        total = both[:, PAIR:]
        outs.append(both[:, :PAIR] / total)
        sums.append(peak * scale + jnp.log2(total[:, :1]))
    exact = jnp.where(first, outs[0], outs[1])
    exact_ref[...] = exact
    lse_ref[...] = jnp.concatenate(sums, 1)
    for j in range(seq):

        @pl.when(step == j)
        def _(j=j):
            mixed_refs[j][...] = exact.astype(BF16)


def attention_forward(qkv, pair, pairs, seq):
    length = qkv.shape[0]
    rows = length // seq
    row = pl.BlockSpec((rows, PAIR), lambda i: (i, 0))
    return pl.pallas_call(
        functools.partial(forward_kernel, HD**-0.5 * LOG2E, seq),
        grid=(seq,),
        in_specs=[
            pl.BlockSpec((rows, PAIR), lambda i: (i, pair)),
            pl.BlockSpec((length, PAIR), lambda i: (0, pairs + pair)),
            pl.BlockSpec((length, PAIR), lambda i: (0, 2 * pairs + pair)),
        ],
        out_specs=[pl.BlockSpec((rows, PAIR), lambda i: (0, 0))] * seq
        + [row, pl.BlockSpec((rows, 2), lambda i: (i, 0))],
        out_shape=[like((rows, PAIR), BF16)] * seq
        + [like((length, PAIR), F32), like((length, 2), F32)],
        scratch_shapes=[pltpu.VMEM((length, 2 * PAIR), BF16)],
        compiler_params=params(32),
        cost_estimate=cost(
            16 * length * length * PAIR, 14 * length * PAIR, 2 * length * length
        ),
        name="attention_forward",
    )(qkv, qkv, qkv)


def backward_kernel(scale, seq, q_ref, k_ref, v_ref, *refs):
    grad_refs, (exact_ref, lse_ref), refs = refs[:seq], refs[seq : seq + 2], refs[seq + 2 :]
    out_refs, (dk_sc, dv_sc, grad_sc) = refs[:seq], refs[seq:]
    step = pl.program_id(0)

    @pl.when(step == 0)
    def _():
        dk_sc[...] = jnp.zeros_like(dk_sc)
        dv_sc[...] = jnp.zeros_like(dv_sc)

    for j in range(seq):

        @pl.when(step == j)
        def _(j=j):
            grad_sc[...] = grad_refs[j][...]

    query, keys, values, grad = q_ref[...], k_ref[...], v_ref[...], grad_sc[...]
    first = lax.broadcasted_iota(jnp.int32, query.shape, 1) < HD
    product = grad.astype(F32) * exact_ref[...]
    dqs = []
    for head in range(2):
        mine = first if head == 0 else jnp.logical_not(first)
        zero = jnp.zeros_like(query)
        q_one = jnp.where(mine, query, zero)
        g_one = jnp.where(mine, grad, zero)
        inner = jnp.sum(jnp.where(mine, product, 0.0), -1, keepdims=True)
        probs = jnp.exp2(dot(q_one, keys, NT) * (scale * LOG2E) - lse_ref[:, head : head + 1])
        grad_scores = (probs * (dot(g_one, values, NT) - inner)).astype(BF16)
        dqs.append(dot(grad_scores, keys))
        dv_sc[...] += dot(g_one, probs.astype(BF16), TN)
        dk_sc[...] += dot(q_one, grad_scores, TN)
    dq = (jnp.where(first, dqs[0], dqs[1]) * scale).astype(BF16)
    for j in range(seq):

        @pl.when(step == j)
        def _(j=j):
            out_refs[j][:, :PAIR] = dq

    @pl.when(step == pl.num_programs(0) - 1)
    def _():
        dk = (dk_sc[...] * scale).T.astype(BF16)
        dv = dv_sc[...].T.astype(BF16)
        rows = dk.shape[0] // seq
        for j in range(seq):
            out_refs[j][:, PAIR : 2 * PAIR] = dk[j * rows : (j + 1) * rows]
            out_refs[j][:, 2 * PAIR :] = dv[j * rows : (j + 1) * rows]


def attention_backward(qkv, grads, exact, lse, pair, pairs, seq):
    length = qkv.shape[0]
    rows = length // seq
    row = pl.BlockSpec((rows, PAIR), lambda i: (i, 0))
    return pl.pallas_call(
        functools.partial(backward_kernel, HD**-0.5, seq),
        grid=(seq,),
        in_specs=[
            pl.BlockSpec((rows, PAIR), lambda i: (i, pair)),
            pl.BlockSpec((length, PAIR), lambda i: (0, pairs + pair)),
            pl.BlockSpec((length, PAIR), lambda i: (0, 2 * pairs + pair)),
        ]
        + [pl.BlockSpec((rows, PAIR), lambda i: (0, pair))] * seq
        + [row, pl.BlockSpec((rows, 2), lambda i: (i, 0))],
        out_specs=[pl.BlockSpec((rows, 3 * PAIR), lambda i: (0, 0))] * seq,
        out_shape=[like((rows, 3 * PAIR), BF16)] * seq,
        scratch_shapes=[pltpu.VMEM((PAIR, length), F32)] * 2 + [pltpu.VMEM((rows, PAIR), BF16)],
        compiler_params=params(32),
        cost_estimate=cost(
            40 * length * length * PAIR, 20 * length * PAIR, 2 * length * length
        ),
        name="attention_backward",
    )(qkv, qkv, qkv, *placed(*grads, exact, lse))


def block_of(where_ref, j, seq):
    return lax.rem(where_ref[1] + (seq - j), seq)


def hidden_kernel(seq, pairs, where_ref, *refs):
    count = seq * pairs
    mixed_refs, w_ref = refs[:count], refs[count]
    (x_ref, bout_ref, gain_ref, shift_ref, bfc1_ref, attended_ref, middle_ref, second_ref,
     activ_ref, slope_ref, att_sc, wout_sc, wfc1_sc, mixed_sem, wout_sem, wfc1_sem) = refs[count + 1 :]
    step = pl.program_id(0)
    width = x_ref.shape[1]

    @pl.when(step == 0)
    def _():
        out_copies = block_copies(w_ref, 0, wout_sc, wout_sem)
        for j in range(seq):
            for p in range(pairs):
                place = (block_of(where_ref, j, seq) * pairs + p) * PAIR
                out_copies.append(
                    pltpu.make_async_copy(
                        mixed_refs[j * pairs + p],
                        att_sc.at[:, pl.ds(pl.multiple_of(place, PAIR), PAIR)],
                        mixed_sem.at[j * pairs + p],
                    )
                )
        fc1_copies = block_copies(w_ref, width, wfc1_sc, wfc1_sem)
        for copy in out_copies + fc1_copies:
            copy.start()
        for copy in out_copies:
            copy.wait()
        attended = att_sc[...]
        attended_ref[...] = attended
        middle = x_ref[...].astype(F32) + (dot(attended, wout_sc[...]) + bout_ref[...])
        middle_ref[...] = middle
        hat, _ = standard(middle)
        second_ref[...] = (hat * gain_ref[...] + shift_ref[...]).astype(BF16)
        for copy in fc1_copies:
            copy.wait()

    block = bfc1_ref.shape[1]
    start = pl.multiple_of(step * block, block)
    hidden = dot(second_ref[...], wfc1_sc[:, pl.ds(start, block)]) + bfc1_ref[...]
    cdf = 0.5 * (1.0 + lax.erf(hidden * (0.5**0.5)))
    activ_ref[...] = (hidden * cdf).astype(BF16)
    slope_ref[...] = cdf + hidden * jnp.exp(-0.5 * hidden * hidden) * ((2.0 * math.pi) ** -0.5)


def hidden_layer(where, seq, mixed, weights, x, b_out, gain, shift_by, b_fc1, block):
    local, width = x.shape
    high = b_fc1.shape[0]
    pairs = len(mixed) // seq
    fixed = lambda i: (0, 0)
    tall = pl.BlockSpec((local, width), fixed)
    vector = pl.BlockSpec((1, width), fixed)
    wide = pl.BlockSpec((local, block), lambda i: (0, i))
    return pl.pallas_call(
        functools.partial(hidden_kernel, seq, pairs),
        grid=(high // block,),
        in_specs=[SCALARS] + [ANY] * (len(mixed) + 1)
        + [tall, vector, vector, vector, pl.BlockSpec((1, block), lambda i: (0, i))],
        out_specs=[tall, tall, tall, wide, wide],
        out_shape=[
            like((local, width), BF16),
            like((local, width), F32),
            like((local, width), BF16),
            like((local, high), BF16),
            like((local, high), F32),
        ],
        scratch_shapes=[
            pltpu.VMEM((local, width), BF16),
            pltpu.VMEM((width, width), BF16),
            pltpu.VMEM((width, high), BF16),
            pltpu.SemaphoreType.DMA((len(mixed),)),
            pltpu.SemaphoreType.DMA((4,)),
            pltpu.SemaphoreType.DMA((4,)),
        ],
        compiler_params=params(40),
        cost_estimate=cost(2 * local * width * (width + high), 8 * local * high, local * high),
        name="hidden_layer",
    )(where, *placed(*mixed, weights, x), b_out[None], gain[None], shift_by[None], b_fc1[None])


def output_kernel(blocks, where_ref, present_ref, w_ref, activ_ref, slope_ref, middle_ref, cot_ref,
                  bfc2_ref, out_ref, ghid_ref, sum_ref, final_sc, glow_sc, w_sc, w_sem):
    step = pl.program_id(0)
    present = present_ref[0]
    copies = block_copies(w_ref, 0, w_sc, w_sem)

    @pl.when(step == 0)
    def _():
        for copy in copies:
            copy.start()
        glow_sc[...] = (cot_ref[...].astype(F32) * present).astype(BF16)
        final_sc[...] = middle_ref[...] + bfc2_ref[...]

    for i in range(blocks):

        @pl.when(step == i)
        def _(i=i):
            copies[i].wait()

    block = activ_ref.shape[1]
    below = w_sc[pl.ds(pl.multiple_of(step * block, block), block), :]
    final_sc[...] += dot(activ_ref[...], below)
    grad_hidden = (dot(glow_sc[...], below, NT) * slope_ref[...]).astype(BF16)
    ghid_ref[...] = grad_hidden
    sum_ref[...] = jnp.sum(grad_hidden.astype(F32), 0, keepdims=True)

    @pl.when(step == blocks - 1)
    def _():
        out_ref[...] = (final_sc[...] * present).astype(BF16)


def output_layer(where, present, weights, activ, slope, middle, cot, b_fc2):
    local, width = middle.shape
    high = activ.shape[1]
    blocks = 8
    fixed = lambda i: (0, 0)
    tall = pl.BlockSpec((local, width), fixed)
    wide = pl.BlockSpec((local, high // blocks), lambda i: (0, i))
    return pl.pallas_call(
        functools.partial(output_kernel, blocks),
        grid=(blocks,),
        in_specs=[SCALARS, SCALARS, ANY, wide, wide, tall, tall, pl.BlockSpec((1, width), fixed)],
        out_specs=[tall, wide, pl.BlockSpec((1, high // blocks), lambda i: (0, i))],
        out_shape=[like((local, width), BF16), like((local, high), BF16), like((1, high), F32)],
        scratch_shapes=[
            pltpu.VMEM((local, width), F32),
            pltpu.VMEM((local, width), BF16),
            pltpu.VMEM((high, width), BF16),
            pltpu.SemaphoreType.DMA((blocks,)),
        ],
        compiler_params=params(40),
        cost_estimate=cost(4 * local * width * high, 12 * local * high),
        name="output_layer",
    )(where, present, *placed(weights, activ, slope, middle, cot), b_fc2[None])


def middle_kernel(seq, blocks, where_ref, present_ref, w_ref, ghid_ref, middle_ref, cot_ref,
                  gain_ref, gmid_ref, gbranch_ref, *refs):
    gmixed_refs, (sums_ref, gsecond_sc, wout_sc, wfc1_sc, wout_sem, wfc1_sem) = refs[:seq], refs[seq:]
    step = pl.program_id(0)
    width = middle_ref.shape[1]
    present = present_ref[0]
    upper = block_copies(w_ref, width, wfc1_sc, wfc1_sem)
    outer = block_copies(w_ref, 0, wout_sc, wout_sem)

    @pl.when(step == 0)
    def _():
        for copy in upper + outer:
            copy.start()
        gsecond_sc[...] = jnp.zeros_like(gsecond_sc)
        for copy in upper:
            copy.wait()

    block = ghid_ref.shape[1]
    start = pl.multiple_of(step * block, block)
    gsecond_sc[...] += dot(ghid_ref[...], wfc1_sc[:, pl.ds(start, block)], NT)

    @pl.when(step == blocks - 1)
    def _():
        for copy in outer:
            copy.wait()
        hat, inverse = standard(middle_ref[...])
        grad_second = gsecond_sc[...]
        grad_rows = cot_ref[...].astype(F32) * present
        grad_middle = grad_rows + norm_grad(grad_second, hat, inverse, gain_ref[...])
        gmid_ref[...] = grad_middle
        grad_branch = grad_middle.astype(BF16)
        gbranch_ref[...] = grad_branch
        sums_ref[...] = jnp.concatenate(
            [
                jnp.sum(grad_branch.astype(F32), 0, keepdims=True),
                jnp.sum(grad_second * hat, 0, keepdims=True),
                jnp.sum(grad_second, 0, keepdims=True),
                jnp.sum(grad_rows, 0, keepdims=True),
            ],
            0,
        )
        own = width // seq
        for j in range(seq):
            rows = pl.multiple_of(block_of(where_ref, j, seq) * own, own)
            gmixed_refs[j][...] = dot(grad_branch, wout_sc[pl.ds(rows, own), :], NT).astype(BF16)


def middle_layer(where, present, seq, weights, grad_hidden, middle, cot, gain):
    local, width = middle.shape
    high = grad_hidden.shape[1]
    blocks = 4
    fixed = lambda i: (0, 0)
    tall = pl.BlockSpec((local, width), fixed)
    own = width // seq
    return pl.pallas_call(
        functools.partial(middle_kernel, seq, blocks),
        grid=(blocks,),
        in_specs=[
            SCALARS,
            SCALARS,
            ANY,
            pl.BlockSpec((local, high // blocks), lambda i: (0, i)),
            tall,
            tall,
            pl.BlockSpec((1, width), fixed),
        ],
        out_specs=[tall, tall]
        + [pl.BlockSpec((local, own), fixed)] * seq
        + [pl.BlockSpec((4, width), fixed)],
        out_shape=[like((local, width), F32), like((local, width), BF16)]
        + [like((local, own), BF16)] * seq
        + [like((4, width), F32)],
        scratch_shapes=[
            pltpu.VMEM((local, width), F32),
            pltpu.VMEM((width, width), BF16),
            pltpu.VMEM((width, high), BF16),
            pltpu.SemaphoreType.DMA((4,)),
            pltpu.SemaphoreType.DMA((4,)),
        ],
        compiler_params=params(40),
        cost_estimate=cost(2 * local * width * (width + high), 12 * local * high),
        name="middle_layer",
    )(where, present, *placed(weights, grad_hidden, middle, cot), gain[None])


def last_kernel(seq, pairs, where_ref, *refs):
    count = seq * pairs
    grad_refs, w_ref = refs[:count], refs[count]
    x_ref, gmid_ref, gain_ref, out_ref, sums_ref, grad_sc, w_sc, grad_sem, w_sem = refs[count + 1 :]
    width = x_ref.shape[1]
    copies = block_copies(w_ref, 0, w_sc, w_sem)
    for j in range(seq):
        for p in range(pairs):
            place = (block_of(where_ref, j, seq) * pairs + p) * PAIR
            for t in range(3):
                copies.append(
                    pltpu.make_async_copy(
                        grad_refs[j * pairs + p].at[:, pl.ds(t * PAIR, PAIR)],
                        grad_sc.at[:, pl.ds(pl.multiple_of(t * width + place, PAIR), PAIR)],
                        grad_sem.at[(j * pairs + p) * 3 + t],
                    )
                )
    for copy in copies:
        copy.start()
    hat, inverse = standard(x_ref[...].astype(F32))
    for copy in copies:
        copy.wait()
    grad_first = dot(grad_sc[...], w_sc[...], NT)
    out_ref[...] = gmid_ref[...] + norm_grad(grad_first, hat, inverse, gain_ref[...])
    sums_ref[...] = jnp.concatenate(
        [jnp.sum(grad_first * hat, 0, keepdims=True), jnp.sum(grad_first, 0, keepdims=True)], 0
    )


def last_layer(where, seq, grads, weights, x, grad_middle, gain):
    local, width = x.shape
    pairs = len(grads) // seq
    whole = pl.BlockSpec(memory_space=pltpu.VMEM)
    return pl.pallas_call(
        functools.partial(last_kernel, seq, pairs),
        in_specs=[SCALARS] + [ANY] * (len(grads) + 1) + [whole] * 3,
        out_specs=[whole, whole],
        out_shape=[like((local, width), F32), like((2, width), F32)],
        scratch_shapes=[
            pltpu.VMEM((local, 3 * width), BF16),
            pltpu.VMEM((width, 3 * width), BF16),
            pltpu.SemaphoreType.DMA((3 * len(grads),)),
            pltpu.SemaphoreType.DMA((4,)),
        ],
        compiler_params=params(56),
        cost_estimate=cost(6 * local * width * width, 6 * width * width),
        name="last_layer",
    )(where, *placed(*grads, weights, x, grad_middle), gain[None])


def product(sides, refs):
    parts = []
    for count in sides:
        left, right_refs, refs = refs[0][...], refs[1 : 1 + count], refs[1 + count :]
        rows = right_refs[0].shape[0]
        groups = left.shape[0] // rows
        total = None
        for g in range(groups):
            blocks = [r[...] for r in right_refs[g::groups]]
            right = blocks[0] if len(blocks) == 1 else jnp.concatenate(blocks, 1)
            term = dot(left[g * rows : (g + 1) * rows], right, TN)
            total = term if total is None else total + term
        parts.append(total)
    return parts[0] if len(parts) == 1 else jnp.concatenate(parts, 1)


def away_kernel(sides, where_ref, *refs):
    refs[-1][0] = product(sides, refs[:-1]).astype(BF16)


def kept_kernel(sides, where_ref, *refs):
    refs, (arrived_ref, far1, keep1, far2, keep2) = refs[:-5], refs[-5:]
    step = pl.program_id(0)
    total = (product(sides, refs) + arrived_ref[0].astype(F32)).astype(BF16)
    half = total.shape[1] // 2

    @pl.when(step % 2 == 1)
    def _():
        far1[0] = total[:, :half]

    @pl.when(step % 2 == 0)
    def _():
        keep1[0] = total[:, :half]

    @pl.when(step >= 2)
    def _():
        far2[0] = total[:, half:]

    @pl.when(step < 2)
    def _():
        keep2[0] = total[:, half:]


def weight_shape(job):
    columns = [sum(r.shape[1] for r in rights) * rights[0].shape[0] // left.shape[0]
               for left, rights in job]
    return job[0][0].shape[1] // 8, sum(columns)


def weight_call(where, job, kernel, odd, more, out_specs, out_shape, name):
    rest, columns = weight_shape(job)
    specs, args = [], []
    for left, rights in job:
        specs.append(
            pl.BlockSpec(
                (left.shape[0], rest), lambda i, w: (0, jnp.bitwise_xor(w[0], 2 * i + odd))
            )
        )
        specs += [pl.BlockSpec(r.shape, lambda i, w: (0, 0)) for r in rights]
        args += [left, *rights]
    return pl.pallas_call(
        functools.partial(kernel, [len(rights) for _, rights in job]),
        grid_spec=pltpu.PrefetchScalarGridSpec(
            num_scalar_prefetch=1,
            grid=(4,),
            in_specs=specs
            + [pl.BlockSpec((1, rest, columns), lambda i, w: (i, 0, 0)) for _ in more],
            out_specs=out_specs,
        ),
        out_shape=out_shape,
        compiler_params=params(48),
        cost_estimate=cost(job[0][0].shape[0] * 8 * rest * columns, 8 * rest * columns),
        name=name,
    )(where, *placed(*args, *more))


def weight_away(where, job):
    rest, columns = weight_shape(job)
    return weight_call(
        where,
        job,
        away_kernel,
        1,
        [],
        pl.BlockSpec((1, rest, columns), lambda i, w: (i, 0, 0)),
        like((4, rest, columns), BF16),
        "weight_away",
    )


def weight_kept(where, job, arrived):
    rest, columns = weight_shape(job)
    two = like((2, rest, columns // 2), BF16)

    def spec(which):
        return pl.BlockSpec((1, rest, columns // 2), lambda i, w: (which(i), 0, 0))

    far1, keep1, far2, keep2 = weight_call(
        where,
        job,
        kept_kernel,
        0,
        [arrived],
        [
            spec(lambda i: i // 2),
            spec(lambda i: i // 2),
            spec(lambda i: jnp.maximum(i - 2, 0)),
            spec(lambda i: jnp.minimum(i, 1)),
        ],
        [two] * 4,
        "weight_kept",
    )
    return (keep1, flip(far1, 1, 8)), (keep2, flip(far2, 2, 8))


def second_kernel(keep1_ref, came1_ref, keep2_ref, came2_ref, *out_refs):
    far1, stay1, far2, stay2 = out_refs
    for keep_ref, came_ref, far, stay in (
        (keep1_ref, came1_ref, far1, stay1),
        (keep2_ref, came2_ref, far2, stay2),
    ):
        total = (keep_ref[...].astype(F32) + came_ref[...].astype(F32)).astype(BF16)
        stay[...] = total[0]
        far[...] = total[1]


def second_sums(first, before, ahead):
    (keep1, came1), (keep2, came2) = first
    keep1 = after(keep1, before)
    _, rest, half = keep1.shape
    rows = rest // 4
    spec = pl.BlockSpec((2, rows, half), lambda i: (0, i, 0))
    out = pl.BlockSpec((rows, half), lambda i: (i, 0))
    far1, stay1, far2, stay2 = pl.pallas_call(
        second_kernel,
        grid=(4,),
        in_specs=[spec] * 4,
        out_specs=[out] * 4,
        out_shape=[like((rest, half), BF16)] * 4,
        compiler_params=params(32),
        cost_estimate=cost(4 * rest * half, 24 * rest * half),
        name="second_sums",
    )(*placed(keep1, came1, keep2, came2))
    far1, far2 = after((far1, far2), ahead)
    return (stay1, flip(far1, 2, 8)), (stay2, flip(far2, 1, 8))


def spread_kernel(seq, where_ref, *refs):
    ins, outs = refs[:-seq], refs[-seq:]
    both = jnp.concatenate(
        [a[...].astype(F32) + b[...].astype(F32) for a, b in zip(ins[0::2], ins[1::2])], 1
    )
    for j, out_ref in enumerate(outs):

        @pl.when(pl.program_id(0) == j)
        def _(out_ref=out_ref):
            out_ref[...] = both.astype(out_ref.dtype)


def seq_spread(where, seconds, seq):
    arrays = [array for second in seconds for part in second for array in part]
    rest = arrays[0].shape[0]
    rows = rest // seq
    columns = sum(a.shape[1] for a in arrays[::2])
    blocks = [
        pl.BlockSpec((rows, a.shape[1]), lambda i, w: (lax.rem(w[1] + i, seq), 0)) for a in arrays
    ]
    out = pl.BlockSpec((rows, columns), lambda i, w: (0, 0))
    return pl.pallas_call(
        functools.partial(spread_kernel, seq),
        grid_spec=pltpu.PrefetchScalarGridSpec(
            num_scalar_prefetch=1, grid=(seq,), in_specs=blocks, out_specs=[out] * seq
        ),
        out_shape=[like((rows, columns), F32)] + [like((rows, columns), BF16)] * (seq - 1),
        compiler_params=params(32),
        cost_estimate=cost(rest * columns, 8 * rest * columns),
        name="seq_spread",
    )(where, *placed(*arrays))


def plain_sums(job, seq):
    blocks = []
    for left, rights in job:
        groups = left.shape[0] // rights[0].shape[0]
        right = jnp.concatenate([jnp.concatenate(rights[g::groups], 1) for g in range(groups)], 0)
        product = dot(left, right, TN)
        blocks.append(lax.psum_scatter(product, "fsdp", scatter_dimension=0, tiled=True))
    me = lax.axis_index("seq")
    parts = jnp.concatenate(blocks, 1)
    parts = parts.reshape(seq, parts.shape[0] // seq, parts.shape[1])
    chunks = [lax.dynamic_index_in_dim(parts, (me + j) % seq, 0, False) for j in range(seq)]
    return [chunks[0]] + [c.astype(BF16) for c in chunks[1:]]


def sum_vectors(vectors, fsdp, seq):
    me = lax.axis_index("fsdp")
    bits = fsdp.bit_length() - 1
    sizes = [v.shape[0] // (fsdp * seq) for v in vectors]
    block = jnp.concatenate([v.reshape(fsdp, seq, -1) for v in vectors], 2)
    block = block.reshape((2,) * bits + (seq, sum(sizes)))
    for bit in range(bits):
        axis = bits - 1 - bit
        mine = (me >> bit) & 1
        away = lax.dynamic_index_in_dim(block, 1 - mine, axis, False)
        block = lax.dynamic_index_in_dim(block, mine, axis, False) + flip(away, bit, fsdp)
    return block, sizes


def split_vectors(block, sizes, seq):
    place = lax.axis_index("seq")
    total = lax.dynamic_index_in_dim(block, place, 0, False)
    for by in range(1, seq):
        away = lax.dynamic_index_in_dim(block, (place + by) % seq, 0, False)
        total = total + shift(away, by, seq)
    return jnp.split(total, [sum(sizes[: i + 1]) for i in range(len(sizes) - 1)])


def after(value, *others):
    return lax.optimization_barrier((value, others))[0]


def spread_pairs(parts, seq):
    arrived = []
    for blocks in parts:
        if arrived:
            blocks = after(blocks, arrived[-1][1:])
        arrived.append([blocks[0]] + [shift(blocks[j], j, seq) for j in range(1, seq)])
    return [pair[j] for j in range(seq) for pair in arrived]


def on_device(
    fsdp,
    seq,
    inputs,
    clip_mask,
    ln1_gain,
    ln1_bias,
    w_query,
    b_query,
    w_key,
    w_value,
    b_value,
    w_out,
    b_out,
    ln2_gain,
    ln2_bias,
    w_fc1,
    b_fc1,
    w_fc2,
    b_fc2,
    cotangent,
):
    clips, local, width = inputs.shape
    assert clips == 1
    me = lax.axis_index("seq")
    where = jnp.stack([lax.axis_index("fsdp"), me]).astype(jnp.int32)
    present = clip_mask.astype(F32)
    own = width // seq
    pairs = own // PAIR
    table = piece_table(fsdp)
    x, cot = inputs[0], cotangent[0]
    grad_low = (cot.astype(F32) * present).astype(BF16)

    def columns(array, axis):
        return lax.dynamic_slice_in_dim(array, me * own, own, axis)

    shard_heads = jnp.concatenate([columns(w, 1) for w in (w_query, w_key, w_value)], 1)
    near_heads = gather_near(shard_heads, fsdp)
    down, up = [x], [x]
    for hop in range(1, seq):
        if hop == 2:
            down[-1], up[-1], near_heads = after((down[-1], up[-1], near_heads))
            w_heads = gather_pieces(shard_heads, near_heads, fsdp)
        if hop == 3:
            down[-1], up[-1] = after((down[-1], up[-1]), w_heads)
        down.append(lax.ppermute(down[-1], "seq", [(i, i - 1) for i in range(1, seq + 1 - hop)]))
        up.append(lax.ppermute(up[-1], "seq", [(i, i + 1) for i in range(hop - 1, seq - 1)]))
    b_heads = jnp.concatenate([columns(b_query, 0), jnp.zeros((own,), F32), columns(b_value, 0)])
    one = lax.all_gather(jnp.concatenate([w_out, w_fc1], 1), "fsdp", axis=0, tiled=True)
    two = lax.all_gather(after(w_fc2, down[1], up[1]), "fsdp", axis=0, tiled=True)
    shard_three = jnp.concatenate([w_query, w_key, w_value], 1)

    first_in, qkv = project(
        where,
        seq,
        table,
        [x] + down[1:] + up[1:],
        w_heads,
        ln1_gain,
        ln1_bias,
        b_heads,
    )
    forward = [attention_forward(qkv, 0, pairs, seq)]
    for p in range(1, pairs):
        forward.append(attention_forward(qkv, p, pairs, seq))
    mixed = spread_pairs([part[:seq] for part in forward], seq)
    attended, middle, second_in, activ, slope = hidden_layer(
        where, seq, mixed, one, x, b_out, ln2_gain, ln2_bias, b_fc1, 512
    )
    parts = {}

    def away(name, job, before):
        if fsdp == 8:
            parts[name] = weight_away(after(where, before), job)
        else:
            parts[name] = plain_sums(job, seq)
        return parts[name]

    def kept(name, job, before, ahead=()):
        if fsdp != 8:
            return ()
        arrived = flip(after(parts[name], ahead), 0, 8)
        parts[name] = weight_kept(after(where, before), job, arrived)
        return parts[name][0][0]

    def second(name, before, ahead=()):
        if fsdp != 8:
            return ()
        parts[name] = second_sums(parts[name], before, ahead)
        return parts[name][0][0]

    def chunks(names, before):
        if fsdp == 8:
            return seq_spread(after(where, before), [parts[n] for n in names], seq)
        return [jnp.concatenate(blocks, 1) for blocks in zip(*[parts[n] for n in names])]

    def came(name):
        return (parts[name][0][1], parts[name][1][1]) if fsdp == 8 else ()

    def send(blocks, ahead):
        if ahead:
            blocks = after(blocks, ahead)
        return [blocks[0]] + [shift(blocks[j], j, seq) for j in range(1, seq)]

    low = [(activ, [grad_low])]
    step = away("low", low, ())
    output, grad_hidden, sum_fc1 = output_layer(
        after(where, step), present, two, activ, slope, middle, cot, b_fc2
    )
    step = kept("low", low, grad_hidden)
    high = [(second_in, [grad_hidden])]
    step = away("high", high, step)
    results = middle_layer(
        after(where, step), present, seq, one, grad_hidden, middle, cot, ln2_gain
    )
    grad_middle, grad_branch = results[:2]
    grad_mixed, sums2 = results[2 : 2 + seq], results[2 + seq]
    grads = [grad_mixed[0]] + [shift(grad_mixed[j], -j, seq) for j in range(1, seq)]
    low_came = came("low")
    step = second("low", grad_branch)
    step = kept("high", high, (step, grads, came("low")), (low_came, grad_branch))
    low_rows = chunks(["low"], step)
    step = low_rows[1]
    low_rows = send(low_rows, ())
    back, home = [], []
    for p in range(pairs):
        exact, lse = forward[p][seq:]
        back.append(attention_backward(qkv, grads, exact, after(lse, step), p, pairs, seq))
        home.append(send(back[-1], home[-1][1:] if home else low_rows[1:]))
        step = back[-1][0]
        if p == 0:
            step = second("high", step, low_rows[1:])
            three = lax.all_gather(after(shard_three, step, low_rows[1:]), "fsdp", axis=0, tiled=True)
    total_low = sum(rows.astype(F32) for rows in low_rows)
    late = [(first_in, [b for pair in back for b in pair]), (attended, [grad_branch])]
    step = away("late", late, (step, came("high")))
    step = kept("late", late, step, home[0])
    step = second("late", step)
    rows = chunks(["late", "high"], step)
    grad_inputs, sums1 = last_layer(
        after(where, rows[0]),
        seq,
        [pair[j] for j in range(seq) for pair in home],
        three,
        x,
        grad_middle,
        ln1_gain,
    )
    def spread(which):
        vector = jnp.concatenate(
            [
                sum(
                    jnp.sum(block[:, which * PAIR : (which + 1) * PAIR].astype(F32), 0)
                    for block in back[p]
                )
                for p in range(pairs)
            ]
        )
        return lax.dynamic_update_slice(jnp.zeros((width,), F32), vector, (me * own,))

    block, sizes = sum_vectors(
        [sums1[0], sums1[1], spread(0), spread(2)] + [sums2[i] for i in range(4)] + [sum_fc1[0]],
        fsdp,
        seq,
    )
    split = 3 * own
    rows = after(send(rows, home[-1][1:]), block)
    total_rows = sum(part[:, split:].astype(F32) for part in rows)
    total_out, total_high = total_rows[:, :width], total_rows[:, width:]
    heads = [part[:, :split].astype(F32) for part in rows[::-1]]
    grad_heads = lax.dynamic_slice_in_dim(jnp.stack(heads + heads), (seq - 1 - me) % seq, seq, 0)
    strip = grad_heads.shape[1]
    grad_heads = grad_heads.reshape(seq, strip, pairs, 3, PAIR).transpose(3, 1, 0, 2, 4)
    grad_heads = grad_heads.reshape(3, strip, width)

    sums = split_vectors(block, sizes, seq)
    return (
        output[None],
        grad_inputs[None],
        sums[0],
        sums[1],
        grad_heads[0],
        sums[2],
        grad_heads[1],
        grad_heads[2],
        sums[3],
        total_out,
        sums[4],
        sums[5],
        sums[6],
        total_high,
        sums[8],
        total_low,
        sums[7],
    )


def solution(mesh):
    rows, both = P("fsdp", None), P(("fsdp", "seq"))
    tokens = P("fsdp", "seq", None)
    matrix = P(("fsdp", "seq"), None)
    return jax.shard_map(
        functools.partial(on_device, mesh.shape["fsdp"], mesh.shape["seq"]),
        mesh=mesh,
        in_specs=(
            tokens,
            P("fsdp"),
            P(),
            P(),
            rows,
            P(),
            rows,
            rows,
            P(),
            rows,
            P(),
            P(),
            P(),
            rows,
            P(),
            rows,
            P(),
            tokens,
        ),
        out_specs=(
            tokens,
            tokens,
            both,
            both,
            matrix,
            both,
            matrix,
            matrix,
            both,
            matrix,
            both,
            both,
            both,
            matrix,
            both,
            matrix,
            both,
        ),
        check_vma=False,
    )
```

```python
import functools
import math

import jax
import jax.numpy as jnp
from jax import lax
from jax.experimental import pallas as pl
from jax.experimental.pallas import tpu as pltpu
from jax.sharding import PartitionSpec as P

HD = 64
PAIR = 2 * HD
EPSILON = 1e-06
LOG2E = math.log2(math.e)
BF16 = jnp.bfloat16
F32 = jnp.float32
NT = (((1,), (1,)), ((), ()))
NN = (((1,), (0,)), ((), ()))
TN = (((0,), (0,)), ((), ()))
ANY = pl.BlockSpec(memory_space=pl.ANY)
SCALARS = pl.BlockSpec(memory_space=pltpu.SMEM)


def dot(a, b, dims=NN):
    return lax.dot_general(a, b, dims, preferred_element_type=F32)


def like(shape, dtype):
    return pltpu.HBM(shape, dtype)


def placed(*arrays):
    return [pltpu.with_memory_space_constraint(a, pltpu.HBM) for a in arrays]


def standard(rows):
    center = rows - jnp.mean(rows, -1, keepdims=True)
    inverse = lax.rsqrt(jnp.mean(center * center, -1, keepdims=True) + EPSILON)
    return center * inverse, inverse


def norm_grad(grad, normed, inverse, gain):
    scaled = grad * gain
    inner = (
        scaled
        - jnp.mean(scaled, -1, keepdims=True)
        - normed * jnp.mean(scaled * normed, -1, keepdims=True)
    )
    return inner * inverse


def params(mib):
    return pltpu.CompilerParams(vmem_limit_bytes=mib << 20)


def cost(flops, moved, special=0):
    return pl.CostEstimate(flops=flops // 64, bytes_accessed=moved // 64, transcendentals=0)


def piece_table(size):
    if size != 8:
        return [(None, None)]
    return [(far + near, half) for near in (0, 1) for far, half in
            ((0, None), (2, None), (4, None), (6, 0), (6, 1))]


def flip(array, bit, size):
    return lax.ppermute(array, "fsdp", [(i, i ^ (1 << bit)) for i in range(size)])


def shift(array, by, size):
    return lax.ppermute(array, "seq", [(i, (i + by) % size) for i in range(size)])


def gather_near(shard, size):
    return (flip(shard, 1, size), flip(shard, 2, size)) if size == 8 else ()


def gather_pieces(shard, near, size):
    if size != 8:
        return [lax.all_gather(shard, "fsdp", axis=0, tiled=True)]
    half = shard.shape[0] // 2
    one, two = near
    top, low = flip(one[:half], 2, size), flip(two[half:], 1, size)
    pieces = [shard, one, two, top, low]
    return pieces + [flip(piece, 0, size) for piece in pieces]


def piece_copies(table, me, refs, first, target, sems):
    width = target.shape[1]
    copies = []
    for i, ((rel, half), ref) in enumerate(zip(table, refs)):
        count = ref.shape[0]
        if rel is None:
            start = 0
        elif half is None:
            start = jnp.bitwise_xor(me, rel) * count
        else:
            start = jnp.bitwise_xor(me, rel) * (2 * count) + half * count
        source = ref.at[:, pl.ds(first, width)]
        place = target.at[pl.ds(start, count), :]
        copies.append(pltpu.make_async_copy(source, place, sems.at[i]))
    return copies


def block_copies(ref, first, target, sems):
    count = sems.shape[0]
    rows, width = target.shape[0] // count, target.shape[1]
    return [
        pltpu.make_async_copy(
            ref.at[pl.ds(i * rows, rows), pl.ds(first, width)],
            target.at[pl.ds(i * rows, rows), :],
            sems.at[i],
        )
        for i in range(count)
    ]


def project_kernel(seq, table, where_ref, *refs):
    own_ref, down_refs, up_refs = refs[0], refs[1:seq], refs[seq : 2 * seq - 1]
    refs = refs[2 * seq - 1 :]
    w_refs, refs = refs[: len(table)], refs[len(table) :]
    gain_ref, shift_ref, bias_ref, first_ref, qkv_ref, x_sc, w_sc, x_sem, w_sem = refs
    step = pl.program_id(0)
    copies = piece_copies(table, where_ref[0], w_refs, 0, w_sc, w_sem)

    @pl.when(step == 0)
    def _():
        for copy in copies:
            copy.start()
        pltpu.make_async_copy(own_ref, x_sc.at[0], x_sem.at[0]).start()
        for j in range(1, seq):
            inside = where_ref[1] + j < seq

            @pl.when(inside)
            def _(j=j):
                pltpu.make_async_copy(down_refs[j - 1], x_sc.at[j], x_sem.at[j]).start()

            @pl.when(jnp.logical_not(inside))
            def _(j=j):
                pltpu.make_async_copy(up_refs[seq - j - 1], x_sc.at[j], x_sem.at[j]).start()

        for copy in copies:
            copy.wait()

    pltpu.make_async_copy(own_ref, x_sc.at[step], x_sem.at[step]).wait()
    hat, _ = standard(x_sc[step].astype(F32))
    first = (hat * gain_ref[...] + shift_ref[...]).astype(BF16)
    first_ref[...] = first
    qkv_ref[...] = (dot(first, w_sc[...]) + bias_ref[...]).astype(BF16)


def project(where, seq, table, tokens, pieces, gain, shift_by, bias):
    local, width = tokens[0].shape
    columns = pieces[0].shape[1]
    vector = pl.BlockSpec((1, width), lambda i: (0, 0))
    return pl.pallas_call(
        functools.partial(project_kernel, seq, table),
        grid=(seq,),
        in_specs=[SCALARS] + [ANY] * (len(tokens) + len(pieces))
        + [vector, vector, pl.BlockSpec((1, columns), lambda i: (0, 0))],
        out_specs=[
            pl.BlockSpec((local, width), lambda i: (i, 0)),
            pl.BlockSpec((local, columns), lambda i: (i, 0)),
        ],
        out_shape=[
            like((seq * local, width), BF16),
            jax.ShapeDtypeStruct((seq * local, columns), BF16),
        ],
        scratch_shapes=[
            pltpu.VMEM((seq, local, width), BF16),
            pltpu.VMEM((width, columns), BF16),
            pltpu.SemaphoreType.DMA((seq,)),
            pltpu.SemaphoreType.DMA((len(table),)),
        ],
        compiler_params=params(32),
        cost_estimate=cost(2 * seq * local * width * columns, 6 * seq * local * width),
        name="project",
    )(where, *placed(*tokens, *pieces), gain[None], shift_by[None], bias[None])


def forward_kernel(scale, seq, q_ref, k_ref, v_ref, *refs):
    mixed_refs, (exact_ref, lse_ref, value_sc) = refs[:seq], refs[seq:]
    step = pl.program_id(0)

    @pl.when(step == 0)
    def _():
        value_sc[:, :PAIR] = v_ref[...]
        value_sc[:, PAIR:] = jnp.ones((value_sc.shape[0], PAIR), value_sc.dtype)

    query = q_ref[...]
    keys = k_ref[...]
    first = lax.broadcasted_iota(jnp.int32, query.shape, 1) < HD
    outs, sums = [], []
    for head in range(2):
        mine = first if head == 0 else jnp.logical_not(first)
        scores = dot(jnp.where(mine, query, jnp.zeros_like(query)), keys, NT)
        peak = jnp.max(scores, -1, keepdims=True)
        expo = jnp.exp2((scores - peak) * scale).astype(BF16)
        both = dot(expo, value_sc[...])
        total = both[:, PAIR:]
        outs.append(both[:, :PAIR] / total)
        sums.append(peak * scale + jnp.log2(total[:, :1]))
    exact = jnp.where(first, outs[0], outs[1])
    exact_ref[...] = exact
    lse_ref[...] = jnp.concatenate(sums, 1)
    for j in range(seq):

        @pl.when(step == j)
        def _(j=j):
            mixed_refs[j][...] = exact.astype(BF16)


def attention_forward(qkv, pair, pairs, seq):
    length = qkv.shape[0]
    rows = length // seq
    row = pl.BlockSpec((rows, PAIR), lambda i: (i, 0))
    return pl.pallas_call(
        functools.partial(forward_kernel, HD**-0.5 * LOG2E, seq),
        grid=(seq,),
        in_specs=[
            pl.BlockSpec((rows, PAIR), lambda i: (i, pair)),
            pl.BlockSpec((length, PAIR), lambda i: (0, pairs + pair)),
            pl.BlockSpec((length, PAIR), lambda i: (0, 2 * pairs + pair)),
        ],
        out_specs=[pl.BlockSpec((rows, PAIR), lambda i: (0, 0))] * seq
        + [row, pl.BlockSpec((rows, 2), lambda i: (i, 0))],
        out_shape=[like((rows, PAIR), BF16)] * seq
        + [like((length, PAIR), F32), like((length, 2), F32)],
        scratch_shapes=[pltpu.VMEM((length, 2 * PAIR), BF16)],
        compiler_params=params(32),
        cost_estimate=cost(
            16 * length * length * PAIR, 14 * length * PAIR, 2 * length * length
        ),
        name="attention_forward",
    )(qkv, qkv, qkv)


def backward_kernel(scale, seq, q_ref, k_ref, v_ref, *refs):
    grad_refs, (exact_ref, lse_ref), refs = refs[:seq], refs[seq : seq + 2], refs[seq + 2 :]
    out_refs, (dk_sc, dv_sc, grad_sc) = refs[:seq], refs[seq:]
    step = pl.program_id(0)

    @pl.when(step == 0)
    def _():
        dk_sc[...] = jnp.zeros_like(dk_sc)
        dv_sc[...] = jnp.zeros_like(dv_sc)

    for j in range(seq):

        @pl.when(step == j)
        def _(j=j):
            grad_sc[...] = grad_refs[j][...]

    query, keys, values, grad = q_ref[...], k_ref[...], v_ref[...], grad_sc[...]
    first = lax.broadcasted_iota(jnp.int32, query.shape, 1) < HD
    product = grad.astype(F32) * exact_ref[...]
    dqs = []
    for head in range(2):
        mine = first if head == 0 else jnp.logical_not(first)
        zero = jnp.zeros_like(query)
        q_one = jnp.where(mine, query, zero)
        g_one = jnp.where(mine, grad, zero)
        inner = jnp.sum(jnp.where(mine, product, 0.0), -1, keepdims=True)
        probs = jnp.exp2(dot(q_one, keys, NT) * (scale * LOG2E) - lse_ref[:, head : head + 1])
        grad_scores = (probs * (dot(g_one, values, NT) - inner)).astype(BF16)
        dqs.append(dot(grad_scores, keys))
        dv_sc[...] += dot(g_one, probs.astype(BF16), TN)
        dk_sc[...] += dot(q_one, grad_scores, TN)
    dq = (jnp.where(first, dqs[0], dqs[1]) * scale).astype(BF16)
    for j in range(seq):

        @pl.when(step == j)
        def _(j=j):
            out_refs[j][:, :PAIR] = dq

    @pl.when(step == pl.num_programs(0) - 1)
    def _():
        dk = (dk_sc[...] * scale).T.astype(BF16)
        dv = dv_sc[...].T.astype(BF16)
        rows = dk.shape[0] // seq
        for j in range(seq):
            out_refs[j][:, PAIR : 2 * PAIR] = dk[j * rows : (j + 1) * rows]
            out_refs[j][:, 2 * PAIR :] = dv[j * rows : (j + 1) * rows]


def attention_backward(qkv, grads, exact, lse, pair, pairs, seq):
    length = qkv.shape[0]
    rows = length // seq
    row = pl.BlockSpec((rows, PAIR), lambda i: (i, 0))
    return pl.pallas_call(
        functools.partial(backward_kernel, HD**-0.5, seq),
        grid=(seq,),
        in_specs=[
            pl.BlockSpec((rows, PAIR), lambda i: (i, pair)),
            pl.BlockSpec((length, PAIR), lambda i: (0, pairs + pair)),
            pl.BlockSpec((length, PAIR), lambda i: (0, 2 * pairs + pair)),
        ]
        + [pl.BlockSpec((rows, PAIR), lambda i: (0, pair))] * seq
        + [row, pl.BlockSpec((rows, 2), lambda i: (i, 0))],
        out_specs=[pl.BlockSpec((rows, 3 * PAIR), lambda i: (0, 0))] * seq,
        out_shape=[like((rows, 3 * PAIR), BF16)] * seq,
        scratch_shapes=[pltpu.VMEM((PAIR, length), F32)] * 2 + [pltpu.VMEM((rows, PAIR), BF16)],
        compiler_params=params(32),
        cost_estimate=cost(
            40 * length * length * PAIR, 20 * length * PAIR, 2 * length * length
        ),
        name="attention_backward",
    )(qkv, qkv, qkv, *placed(*grads, exact, lse))


def block_of(where_ref, j, seq):
    return lax.rem(where_ref[1] + (seq - j), seq)


def hidden_kernel(seq, pairs, where_ref, *refs):
    count = seq * pairs
    mixed_refs, w_ref = refs[:count], refs[count]
    (x_ref, bout_ref, gain_ref, shift_ref, bfc1_ref, attended_ref, middle_ref, second_ref,
     activ_ref, slope_ref, att_sc, wout_sc, wfc1_sc, mixed_sem, wout_sem, wfc1_sem) = refs[count + 1 :]
    step = pl.program_id(0)
    width = x_ref.shape[1]

    @pl.when(step == 0)
    def _():
        out_copies = block_copies(w_ref, 0, wout_sc, wout_sem)
        for j in range(seq):
            for p in range(pairs):
                place = (block_of(where_ref, j, seq) * pairs + p) * PAIR
                out_copies.append(
                    pltpu.make_async_copy(
                        mixed_refs[j * pairs + p],
                        att_sc.at[:, pl.ds(pl.multiple_of(place, PAIR), PAIR)],
                        mixed_sem.at[j * pairs + p],
                    )
                )
        fc1_copies = block_copies(w_ref, width, wfc1_sc, wfc1_sem)
        for copy in out_copies + fc1_copies:
            copy.start()
        for copy in out_copies:
            copy.wait()
        attended = att_sc[...]
        attended_ref[...] = attended
        middle = x_ref[...].astype(F32) + (dot(attended, wout_sc[...]) + bout_ref[...])
        middle_ref[...] = middle
        hat, _ = standard(middle)
        second_ref[...] = (hat * gain_ref[...] + shift_ref[...]).astype(BF16)
        for copy in fc1_copies:
            copy.wait()

    block = bfc1_ref.shape[1]
    start = pl.multiple_of(step * block, block)
    hidden = dot(second_ref[...], wfc1_sc[:, pl.ds(start, block)]) + bfc1_ref[...]
    cdf = 0.5 * (1.0 + lax.erf(hidden * (0.5**0.5)))
    activ_ref[...] = (hidden * cdf).astype(BF16)
    slope_ref[...] = cdf + hidden * jnp.exp(-0.5 * hidden * hidden) * ((2.0 * math.pi) ** -0.5)


def hidden_layer(where, seq, mixed, weights, x, b_out, gain, shift_by, b_fc1, block):
    local, width = x.shape
    high = b_fc1.shape[0]
    pairs = len(mixed) // seq
    fixed = lambda i: (0, 0)
    tall = pl.BlockSpec((local, width), fixed)
    vector = pl.BlockSpec((1, width), fixed)
    wide = pl.BlockSpec((local, block), lambda i: (0, i))
    return pl.pallas_call(
        functools.partial(hidden_kernel, seq, pairs),
        grid=(high // block,),
        in_specs=[SCALARS] + [ANY] * (len(mixed) + 1)
        + [tall, vector, vector, vector, pl.BlockSpec((1, block), lambda i: (0, i))],
        out_specs=[tall, tall, tall, wide, wide],
        out_shape=[
            like((local, width), BF16),
            like((local, width), F32),
            like((local, width), BF16),
            like((local, high), BF16),
            like((local, high), F32),
        ],
        scratch_shapes=[
            pltpu.VMEM((local, width), BF16),
            pltpu.VMEM((width, width), BF16),
            pltpu.VMEM((width, high), BF16),
            pltpu.SemaphoreType.DMA((len(mixed),)),
            pltpu.SemaphoreType.DMA((4,)),
            pltpu.SemaphoreType.DMA((4,)),
        ],
        compiler_params=params(40),
        cost_estimate=cost(2 * local * width * (width + high), 8 * local * high, local * high),
        name="hidden_layer",
    )(where, *placed(*mixed, weights, x), b_out[None], gain[None], shift_by[None], b_fc1[None])


def output_kernel(blocks, where_ref, present_ref, w_ref, activ_ref, slope_ref, middle_ref, cot_ref,
                  bfc2_ref, out_ref, ghid_ref, sum_ref, final_sc, glow_sc, w_sc, w_sem):
    step = pl.program_id(0)
    present = present_ref[0]
    copies = block_copies(w_ref, 0, w_sc, w_sem)

    @pl.when(step == 0)
    def _():
        for copy in copies:
            copy.start()
        glow_sc[...] = (cot_ref[...].astype(F32) * present).astype(BF16)
        final_sc[...] = middle_ref[...] + bfc2_ref[...]

    for i in range(blocks):

        @pl.when(step == i)
        def _(i=i):
            copies[i].wait()

    block = activ_ref.shape[1]
    below = w_sc[pl.ds(pl.multiple_of(step * block, block), block), :]
    final_sc[...] += dot(activ_ref[...], below)
    grad_hidden = (dot(glow_sc[...], below, NT) * slope_ref[...]).astype(BF16)
    ghid_ref[...] = grad_hidden
    sum_ref[...] = jnp.sum(grad_hidden.astype(F32), 0, keepdims=True)

    @pl.when(step == blocks - 1)
    def _():
        out_ref[...] = (final_sc[...] * present).astype(BF16)


def output_layer(where, present, weights, activ, slope, middle, cot, b_fc2):
    local, width = middle.shape
    high = activ.shape[1]
    blocks = 8
    fixed = lambda i: (0, 0)
    tall = pl.BlockSpec((local, width), fixed)
    wide = pl.BlockSpec((local, high // blocks), lambda i: (0, i))
    return pl.pallas_call(
        functools.partial(output_kernel, blocks),
        grid=(blocks,),
        in_specs=[SCALARS, SCALARS, ANY, wide, wide, tall, tall, pl.BlockSpec((1, width), fixed)],
        out_specs=[tall, wide, pl.BlockSpec((1, high // blocks), lambda i: (0, i))],
        out_shape=[like((local, width), BF16), like((local, high), BF16), like((1, high), F32)],
        scratch_shapes=[
            pltpu.VMEM((local, width), F32),
            pltpu.VMEM((local, width), BF16),
            pltpu.VMEM((high, width), BF16),
            pltpu.SemaphoreType.DMA((blocks,)),
        ],
        compiler_params=params(40),
        cost_estimate=cost(4 * local * width * high, 12 * local * high),
        name="output_layer",
    )(where, present, *placed(weights, activ, slope, middle, cot), b_fc2[None])


def middle_kernel(seq, blocks, where_ref, present_ref, w_ref, ghid_ref, middle_ref, cot_ref,
                  gain_ref, gmid_ref, gbranch_ref, *refs):
    gmixed_refs, (sums_ref, gsecond_sc, wout_sc, wfc1_sc, wout_sem, wfc1_sem) = refs[:seq], refs[seq:]
    step = pl.program_id(0)
    width = middle_ref.shape[1]
    present = present_ref[0]
    upper = block_copies(w_ref, width, wfc1_sc, wfc1_sem)
    outer = block_copies(w_ref, 0, wout_sc, wout_sem)

    @pl.when(step == 0)
    def _():
        for copy in upper + outer:
            copy.start()
        gsecond_sc[...] = jnp.zeros_like(gsecond_sc)
        for copy in upper:
            copy.wait()

    block = ghid_ref.shape[1]
    start = pl.multiple_of(step * block, block)
    gsecond_sc[...] += dot(ghid_ref[...], wfc1_sc[:, pl.ds(start, block)], NT)

    @pl.when(step == blocks - 1)
    def _():
        for copy in outer:
            copy.wait()
        hat, inverse = standard(middle_ref[...])
        grad_second = gsecond_sc[...]
        grad_rows = cot_ref[...].astype(F32) * present
        grad_middle = grad_rows + norm_grad(grad_second, hat, inverse, gain_ref[...])
        gmid_ref[...] = grad_middle
        grad_branch = grad_middle.astype(BF16)
        gbranch_ref[...] = grad_branch
        sums_ref[...] = jnp.concatenate(
            [
                jnp.sum(grad_branch.astype(F32), 0, keepdims=True),
                jnp.sum(grad_second * hat, 0, keepdims=True),
                jnp.sum(grad_second, 0, keepdims=True),
                jnp.sum(grad_rows, 0, keepdims=True),
            ],
            0,
        )
        own = width // seq
        for j in range(seq):
            rows = pl.multiple_of(block_of(where_ref, j, seq) * own, own)
            gmixed_refs[j][...] = dot(grad_branch, wout_sc[pl.ds(rows, own), :], NT).astype(BF16)


def middle_layer(where, present, seq, weights, grad_hidden, middle, cot, gain):
    local, width = middle.shape
    high = grad_hidden.shape[1]
    blocks = 4
    fixed = lambda i: (0, 0)
    tall = pl.BlockSpec((local, width), fixed)
    own = width // seq
    return pl.pallas_call(
        functools.partial(middle_kernel, seq, blocks),
        grid=(blocks,),
        in_specs=[
            SCALARS,
            SCALARS,
            ANY,
            pl.BlockSpec((local, high // blocks), lambda i: (0, i)),
            tall,
            tall,
            pl.BlockSpec((1, width), fixed),
        ],
        out_specs=[tall, tall]
        + [pl.BlockSpec((local, own), fixed)] * seq
        + [pl.BlockSpec((4, width), fixed)],
        out_shape=[like((local, width), F32), like((local, width), BF16)]
        + [like((local, own), BF16)] * seq
        + [like((4, width), F32)],
        scratch_shapes=[
            pltpu.VMEM((local, width), F32),
            pltpu.VMEM((width, width), BF16),
            pltpu.VMEM((width, high), BF16),
            pltpu.SemaphoreType.DMA((4,)),
            pltpu.SemaphoreType.DMA((4,)),
        ],
        compiler_params=params(40),
        cost_estimate=cost(2 * local * width * (width + high), 12 * local * high),
        name="middle_layer",
    )(where, present, *placed(weights, grad_hidden, middle, cot), gain[None])


def last_kernel(seq, pairs, where_ref, *refs):
    count = seq * pairs
    grad_refs, w_ref = refs[:count], refs[count]
    x_ref, gmid_ref, gain_ref, out_ref, sums_ref, grad_sc, w_sc, grad_sem, w_sem = refs[count + 1 :]
    width = x_ref.shape[1]
    copies = block_copies(w_ref, 0, w_sc, w_sem)
    for j in range(seq):
        for p in range(pairs):
            place = (block_of(where_ref, j, seq) * pairs + p) * PAIR
            for t in range(3):
                copies.append(
                    pltpu.make_async_copy(
                        grad_refs[j * pairs + p].at[:, pl.ds(t * PAIR, PAIR)],
                        grad_sc.at[:, pl.ds(pl.multiple_of(t * width + place, PAIR), PAIR)],
                        grad_sem.at[(j * pairs + p) * 3 + t],
                    )
                )
    for copy in copies:
        copy.start()
    hat, inverse = standard(x_ref[...].astype(F32))
    for copy in copies:
        copy.wait()
    grad_first = dot(grad_sc[...], w_sc[...], NT)
    out_ref[...] = gmid_ref[...] + norm_grad(grad_first, hat, inverse, gain_ref[...])
    sums_ref[...] = jnp.concatenate(
        [jnp.sum(grad_first * hat, 0, keepdims=True), jnp.sum(grad_first, 0, keepdims=True)], 0
    )


def last_layer(where, seq, grads, weights, x, grad_middle, gain):
    local, width = x.shape
    pairs = len(grads) // seq
    whole = pl.BlockSpec(memory_space=pltpu.VMEM)
    return pl.pallas_call(
        functools.partial(last_kernel, seq, pairs),
        in_specs=[SCALARS] + [ANY] * (len(grads) + 1) + [whole] * 3,
        out_specs=[whole, whole],
        out_shape=[like((local, width), F32), like((2, width), F32)],
        scratch_shapes=[
            pltpu.VMEM((local, 3 * width), BF16),
            pltpu.VMEM((width, 3 * width), BF16),
            pltpu.SemaphoreType.DMA((3 * len(grads),)),
            pltpu.SemaphoreType.DMA((4,)),
        ],
        compiler_params=params(56),
        cost_estimate=cost(6 * local * width * width, 6 * width * width),
        name="last_layer",
    )(where, *placed(*grads, weights, x, grad_middle), gain[None])


def product(sides, refs):
    parts = []
    for count in sides:
        left, right_refs, refs = refs[0][...], refs[1 : 1 + count], refs[1 + count :]
        rows = right_refs[0].shape[0]
        groups = left.shape[0] // rows
        total = None
        for g in range(groups):
            blocks = [r[...] for r in right_refs[g::groups]]
            right = blocks[0] if len(blocks) == 1 else jnp.concatenate(blocks, 1)
            term = dot(left[g * rows : (g + 1) * rows], right, TN)
            total = term if total is None else total + term
        parts.append(total)
    return parts[0] if len(parts) == 1 else jnp.concatenate(parts, 1)


def away_kernel(sides, where_ref, *refs):
    refs[-1][0] = product(sides, refs[:-1]).astype(BF16)


def kept_kernel(sides, where_ref, *refs):
    refs, (arrived_ref, far1, keep1, far2, keep2) = refs[:-5], refs[-5:]
    step = pl.program_id(0)
    total = (product(sides, refs) + arrived_ref[0].astype(F32)).astype(BF16)
    half = total.shape[1] // 2

    @pl.when(step % 2 == 1)
    def _():
        far1[0] = total[:, :half]

    @pl.when(step % 2 == 0)
    def _():
        keep1[0] = total[:, :half]

    @pl.when(step >= 2)
    def _():
        far2[0] = total[:, half:]

    @pl.when(step < 2)
    def _():
        keep2[0] = total[:, half:]


def weight_shape(job):
    columns = [sum(r.shape[1] for r in rights) * rights[0].shape[0] // left.shape[0]
               for left, rights in job]
    return job[0][0].shape[1] // 8, sum(columns)


def weight_call(where, job, kernel, odd, more, out_specs, out_shape, name):
    rest, columns = weight_shape(job)
    specs, args = [], []
    for left, rights in job:
        specs.append(
            pl.BlockSpec(
                (left.shape[0], rest), lambda i, w: (0, jnp.bitwise_xor(w[0], 2 * i + odd))
            )
        )
        specs += [pl.BlockSpec(r.shape, lambda i, w: (0, 0)) for r in rights]
        args += [left, *rights]
    return pl.pallas_call(
        functools.partial(kernel, [len(rights) for _, rights in job]),
        grid_spec=pltpu.PrefetchScalarGridSpec(
            num_scalar_prefetch=1,
            grid=(4,),
            in_specs=specs
            + [pl.BlockSpec((1, rest, columns), lambda i, w: (i, 0, 0)) for _ in more],
            out_specs=out_specs,
        ),
        out_shape=out_shape,
        compiler_params=params(48),
        cost_estimate=cost(job[0][0].shape[0] * 8 * rest * columns, 8 * rest * columns),
        name=name,
    )(where, *placed(*args, *more))


def weight_away(where, job):
    rest, columns = weight_shape(job)
    return weight_call(
        where,
        job,
        away_kernel,
        1,
        [],
        pl.BlockSpec((1, rest, columns), lambda i, w: (i, 0, 0)),
        like((4, rest, columns), BF16),
        "weight_away",
    )


def weight_kept(where, job, arrived, ahead):
    rest, columns = weight_shape(job)
    two = like((2, rest, columns // 2), BF16)

    def spec(which):
        return pl.BlockSpec((1, rest, columns // 2), lambda i, w: (which(i), 0, 0))

    far1, keep1, far2, keep2 = weight_call(
        where,
        job,
        kept_kernel,
        0,
        [arrived],
        [
            spec(lambda i: i // 2),
            spec(lambda i: i // 2),
            spec(lambda i: jnp.maximum(i - 2, 0)),
            spec(lambda i: jnp.minimum(i, 1)),
        ],
        [two] * 4,
        "weight_kept",
    )
    if ahead:
        far1, far2 = after((far1, far2), ahead)
    return (keep1, flip(far1, 1, 8)), (keep2, flip(far2, 2, 8))


def second_kernel(keep1_ref, came1_ref, keep2_ref, came2_ref, *out_refs):
    far1, stay1, far2, stay2 = out_refs
    for keep_ref, came_ref, far, stay in (
        (keep1_ref, came1_ref, far1, stay1),
        (keep2_ref, came2_ref, far2, stay2),
    ):
        total = (keep_ref[...].astype(F32) + came_ref[...].astype(F32)).astype(BF16)
        stay[...] = total[0]
        far[...] = total[1]


def second_sums(first, before, ahead):
    (keep1, came1), (keep2, came2) = first
    keep1 = after(keep1, before)
    _, rest, half = keep1.shape
    rows = rest // 4
    spec = pl.BlockSpec((2, rows, half), lambda i: (0, i, 0))
    out = pl.BlockSpec((rows, half), lambda i: (i, 0))
    far1, stay1, far2, stay2 = pl.pallas_call(
        second_kernel,
        grid=(4,),
        in_specs=[spec] * 4,
        out_specs=[out] * 4,
        out_shape=[like((rest, half), BF16)] * 4,
        compiler_params=params(32),
        cost_estimate=cost(4 * rest * half, 24 * rest * half),
        name="second_sums",
    )(*placed(keep1, came1, keep2, came2))
    far1, far2 = after((far1, far2), ahead)
    return (stay1, flip(far1, 2, 8)), (stay2, flip(far2, 1, 8))


def spread_kernel(seq, where_ref, *refs):
    ins, outs = refs[:-seq], refs[-seq:]
    both = jnp.concatenate(
        [a[...].astype(F32) + b[...].astype(F32) for a, b in zip(ins[0::2], ins[1::2])], 1
    )
    for j, out_ref in enumerate(outs):

        @pl.when(pl.program_id(0) == j)
        def _(out_ref=out_ref):
            out_ref[...] = both.astype(out_ref.dtype)


def seq_spread(where, seconds, seq):
    arrays = [array for second in seconds for part in second for array in part]
    rest = arrays[0].shape[0]
    rows = rest // seq
    columns = sum(a.shape[1] for a in arrays[::2])
    blocks = [
        pl.BlockSpec((rows, a.shape[1]), lambda i, w: (lax.rem(w[1] + i, seq), 0)) for a in arrays
    ]
    out = pl.BlockSpec((rows, columns), lambda i, w: (0, 0))
    return pl.pallas_call(
        functools.partial(spread_kernel, seq),
        grid_spec=pltpu.PrefetchScalarGridSpec(
            num_scalar_prefetch=1, grid=(seq,), in_specs=blocks, out_specs=[out] * seq
        ),
        out_shape=[like((rows, columns), F32)] + [like((rows, columns), BF16)] * (seq - 1),
        compiler_params=params(32),
        cost_estimate=cost(rest * columns, 8 * rest * columns),
        name="seq_spread",
    )(where, *placed(*arrays))


def plain_sums(job, seq):
    blocks = []
    for left, rights in job:
        groups = left.shape[0] // rights[0].shape[0]
        right = jnp.concatenate([jnp.concatenate(rights[g::groups], 1) for g in range(groups)], 0)
        product = dot(left, right, TN)
        blocks.append(lax.psum_scatter(product, "fsdp", scatter_dimension=0, tiled=True))
    me = lax.axis_index("seq")
    parts = jnp.concatenate(blocks, 1)
    parts = parts.reshape(seq, parts.shape[0] // seq, parts.shape[1])
    chunks = [lax.dynamic_index_in_dim(parts, (me + j) % seq, 0, False) for j in range(seq)]
    return [chunks[0]] + [c.astype(BF16) for c in chunks[1:]]


def sum_vectors(vectors, fsdp, seq):
    me = lax.axis_index("fsdp")
    bits = fsdp.bit_length() - 1
    sizes = [v.shape[0] // (fsdp * seq) for v in vectors]
    block = jnp.concatenate([v.reshape(fsdp, seq, -1) for v in vectors], 2)
    block = block.reshape((2,) * bits + (seq, sum(sizes)))
    for bit in range(bits):
        axis = bits - 1 - bit
        mine = (me >> bit) & 1
        away = lax.dynamic_index_in_dim(block, 1 - mine, axis, False)
        block = lax.dynamic_index_in_dim(block, mine, axis, False) + flip(away, bit, fsdp)
    return block, sizes


def split_vectors(block, sizes, seq):
    place = lax.axis_index("seq")
    total = lax.dynamic_index_in_dim(block, place, 0, False)
    for by in range(1, seq):
        away = lax.dynamic_index_in_dim(block, (place + by) % seq, 0, False)
        total = total + shift(away, by, seq)
    return jnp.split(total, [sum(sizes[: i + 1]) for i in range(len(sizes) - 1)])


def after(value, *others):
    return lax.optimization_barrier((value, others))[0]


def spread_pairs(parts, seq):
    arrived = []
    for blocks in parts:
        if arrived:
            blocks = after(blocks, arrived[-1][1:])
        arrived.append([blocks[0]] + [shift(blocks[j], j, seq) for j in range(1, seq)])
    return [pair[j] for j in range(seq) for pair in arrived]


def on_device(
    fsdp,
    seq,
    inputs,
    clip_mask,
    ln1_gain,
    ln1_bias,
    w_query,
    b_query,
    w_key,
    w_value,
    b_value,
    w_out,
    b_out,
    ln2_gain,
    ln2_bias,
    w_fc1,
    b_fc1,
    w_fc2,
    b_fc2,
    cotangent,
):
    clips, local, width = inputs.shape
    assert clips == 1
    me = lax.axis_index("seq")
    where = jnp.stack([lax.axis_index("fsdp"), me]).astype(jnp.int32)
    present = clip_mask.astype(F32)
    own = width // seq
    pairs = own // PAIR
    table = piece_table(fsdp)
    x, cot = inputs[0], cotangent[0]
    grad_low = (cot.astype(F32) * present).astype(BF16)

    def columns(array, axis):
        return lax.dynamic_slice_in_dim(array, me * own, own, axis)

    shard_heads = jnp.concatenate([columns(w, 1) for w in (w_query, w_key, w_value)], 1)
    near_heads = gather_near(shard_heads, fsdp)
    down, up = [x], [x]
    for hop in range(1, seq):
        if hop == 2:
            down[-1], up[-1], near_heads = after((down[-1], up[-1], near_heads))
            w_heads = gather_pieces(shard_heads, near_heads, fsdp)
        if hop == 3:
            down[-1], up[-1] = after((down[-1], up[-1]), w_heads)
        down.append(lax.ppermute(down[-1], "seq", [(i, i - 1) for i in range(1, seq + 1 - hop)]))
        up.append(lax.ppermute(up[-1], "seq", [(i, i + 1) for i in range(hop - 1, seq - 1)]))
    b_heads = jnp.concatenate([columns(b_query, 0), jnp.zeros((own,), F32), columns(b_value, 0)])
    one = lax.all_gather(jnp.concatenate([w_out, w_fc1], 1), "fsdp", axis=0, tiled=True)
    two = lax.all_gather(after(w_fc2, down[1], up[1]), "fsdp", axis=0, tiled=True)
    shard_three = jnp.concatenate([w_query, w_key, w_value], 1)
    three = lax.all_gather(after(shard_three, down[2], up[2]), "fsdp", axis=0, tiled=True)

    first_in, qkv = project(
        where,
        seq,
        table,
        [x] + down[1:] + up[1:],
        w_heads,
        ln1_gain,
        ln1_bias,
        b_heads,
    )
    forward = [attention_forward(qkv, 0, pairs, seq)]
    for p in range(1, pairs):
        forward.append(attention_forward(qkv, p, pairs, seq))
    mixed = spread_pairs([part[:seq] for part in forward], seq)
    attended, middle, second_in, activ, slope = hidden_layer(
        where, seq, mixed, one, x, b_out, ln2_gain, ln2_bias, b_fc1, 512
    )
    parts = {}

    def away(name, job, before):
        if fsdp == 8:
            parts[name] = weight_away(after(where, before), job)
        else:
            parts[name] = plain_sums(job, seq)
        return parts[name]

    def kept(name, job, before, first=(), ahead=()):
        if fsdp != 8:
            return ()
        arrived = flip(after(parts[name], first), 0, 8)
        parts[name] = weight_kept(after(where, before), job, arrived, ahead)
        return parts[name][0][0]

    def second(name, before, ahead=()):
        if fsdp != 8:
            return ()
        parts[name] = second_sums(parts[name], before, ahead)
        return parts[name][0][0]

    def chunks(names, before):
        if fsdp == 8:
            return seq_spread(after(where, before), [parts[n] for n in names], seq)
        return [jnp.concatenate(blocks, 1) for blocks in zip(*[parts[n] for n in names])]

    def came(name):
        return (parts[name][0][1], parts[name][1][1]) if fsdp == 8 else ()

    def send(blocks, ahead):
        if ahead:
            blocks = after(blocks, ahead)
        return [blocks[0]] + [shift(blocks[j], j, seq) for j in range(1, seq)]

    low = [(activ, [grad_low])]
    step = away("low", low, ())
    output, grad_hidden, sum_fc1 = output_layer(
        after(where, step), present, two, activ, slope, middle, cot, b_fc2
    )
    step = kept("low", low, grad_hidden)
    high = [(second_in, [grad_hidden])]
    step = away("high", high, step)
    results = middle_layer(
        after(where, step, three), present, seq, one, grad_hidden, middle, cot, ln2_gain
    )
    grad_middle, grad_branch = results[:2]
    grad_mixed, sums2 = results[2 : 2 + seq], results[2 + seq]
    grads = [grad_mixed[0]] + [shift(grad_mixed[j], -j, seq) for j in range(1, seq)]
    low_came = came("low")
    step = second("low", grad_branch)
    step = kept("high", high, step, (low_came, grad_branch), grads[1:])
    low_rows = chunks(["low"], step)
    step = low_rows[1]
    low_rows = send(low_rows, grads[1:])
    back, home = [], []
    for p in range(pairs):
        exact, lse = forward[p][seq:]
        back.append(attention_backward(qkv, grads, exact, after(lse, step), p, pairs, seq))
        home.append(send(back[-1], home[-1][1:] if home else low_rows[1:]))
        step = back[-1][0]
    total_low = sum(rows.astype(F32) for rows in low_rows)
    step = second("high", step, home[0][1:])
    late = [(first_in, [b for pair in back for b in pair]), (attended, [grad_branch])]
    step = away("late", late, step)
    step = kept("late", late, step, home[0][1:], home[1][1:])
    high_rows = chunks(["high"], step)
    step = high_rows[1]
    high_rows = send(high_rows, home[1][1:])
    grad_inputs, sums1 = last_layer(
        after(where, step),
        seq,
        [pair[j] for j in range(seq) for pair in home],
        three,
        x,
        grad_middle,
        ln1_gain,
    )
    second("late", sums1)
    late_rows = chunks(["late"], ())

    def spread(which):
        vector = jnp.concatenate(
            [
                sum(
                    jnp.sum(block[:, which * PAIR : (which + 1) * PAIR].astype(F32), 0)
                    for block in back[p]
                )
                for p in range(pairs)
            ]
        )
        return lax.dynamic_update_slice(jnp.zeros((width,), F32), vector, (me * own,))

    sums1 = after(sums1, high_rows[1:], came("late"))
    block, sizes = sum_vectors(
        [sums1[0], sums1[1], spread(0), spread(2)] + [sums2[i] for i in range(4)] + [sum_fc1[0]],
        fsdp,
        seq,
    )
    split = 3 * own
    rows = after(send(late_rows, ()), block)
    total_out = sum(part[:, split:].astype(F32) for part in rows)
    total_high = sum(part.astype(F32) for part in high_rows)
    heads = [part[:, :split].astype(F32) for part in rows[::-1]]
    grad_heads = lax.dynamic_slice_in_dim(jnp.stack(heads + heads), (seq - 1 - me) % seq, seq, 0)
    strip = grad_heads.shape[1]
    grad_heads = grad_heads.reshape(seq, strip, pairs, 3, PAIR).transpose(3, 1, 0, 2, 4)
    grad_heads = grad_heads.reshape(3, strip, width)

    sums = split_vectors(block, sizes, seq)
    return (
        output[None],
        grad_inputs[None],
        sums[0],
        sums[1],
        grad_heads[0],
        sums[2],
        grad_heads[1],
        grad_heads[2],
        sums[3],
        total_out,
        sums[4],
        sums[5],
        sums[6],
        total_high,
        sums[8],
        total_low,
        sums[7],
    )


def solution(mesh):
    rows, both = P("fsdp", None), P(("fsdp", "seq"))
    tokens = P("fsdp", "seq", None)
    matrix = P(("fsdp", "seq"), None)
    return jax.shard_map(
        functools.partial(on_device, mesh.shape["fsdp"], mesh.shape["seq"]),
        mesh=mesh,
        in_specs=(
            tokens,
            P("fsdp"),
            P(),
            P(),
            rows,
            P(),
            rows,
            rows,
            P(),
            rows,
            P(),
            P(),
            P(),
            rows,
            P(),
            rows,
            P(),
            tokens,
        ),
        out_specs=(
            tokens,
            tokens,
            both,
            both,
            matrix,
            both,
            matrix,
            matrix,
            both,
            matrix,
            both,
            both,
            both,
            matrix,
            both,
            matrix,
            both,
        ),
        check_vma=False,
    )
```

```python
import functools
import math

import jax
import jax.numpy as jnp
from jax import lax
from jax.experimental import pallas as pl
from jax.experimental.pallas import tpu as pltpu
from jax.sharding import PartitionSpec as P

HD = 64
PAIR = 2 * HD
EPSILON = 1e-06
LOG2E = math.log2(math.e)
BF16 = jnp.bfloat16
F32 = jnp.float32
NT = (((1,), (1,)), ((), ()))
NN = (((1,), (0,)), ((), ()))
TN = (((0,), (0,)), ((), ()))
ANY = pl.BlockSpec(memory_space=pl.ANY)
SCALARS = pl.BlockSpec(memory_space=pltpu.SMEM)


def dot(a, b, dims=NN):
    return lax.dot_general(a, b, dims, preferred_element_type=F32)


def like(shape, dtype):
    return pltpu.HBM(shape, dtype)


def placed(*arrays):
    return [pltpu.with_memory_space_constraint(a, pltpu.HBM) for a in arrays]


def standard(rows):
    center = rows - jnp.mean(rows, -1, keepdims=True)
    inverse = lax.rsqrt(jnp.mean(center * center, -1, keepdims=True) + EPSILON)
    return center * inverse, inverse


def norm_grad(grad, normed, inverse, gain):
    scaled = grad * gain
    inner = (
        scaled
        - jnp.mean(scaled, -1, keepdims=True)
        - normed * jnp.mean(scaled * normed, -1, keepdims=True)
    )
    return inner * inverse


def params(mib):
    return pltpu.CompilerParams(vmem_limit_bytes=mib << 20)


def cost(flops, moved, special=0):
    return pl.CostEstimate(flops=flops // 64, bytes_accessed=moved // 64, transcendentals=0)


def piece_table(size):
    if size != 8:
        return [(None, None)]
    return [(far + near, half) for near in (0, 1) for far, half in
            ((0, None), (2, None), (4, None), (6, 0), (6, 1))]


def flip(array, bit, size):
    return lax.ppermute(array, "fsdp", [(i, i ^ (1 << bit)) for i in range(size)])


def shift(array, by, size):
    return lax.ppermute(array, "seq", [(i, (i + by) % size) for i in range(size)])


def gather_near(shard, size):
    return (flip(shard, 1, size), flip(shard, 2, size)) if size == 8 else ()


def gather_pieces(shard, near, size):
    if size != 8:
        return [lax.all_gather(shard, "fsdp", axis=0, tiled=True)]
    half = shard.shape[0] // 2
    one, two = near
    top, low = flip(one[:half], 2, size), flip(two[half:], 1, size)
    pieces = [shard, one, two, top, low]
    return pieces + [flip(piece, 0, size) for piece in pieces]


def piece_copies(table, me, refs, first, target, sems):
    width = target.shape[1]
    copies = []
    for i, ((rel, half), ref) in enumerate(zip(table, refs)):
        count = ref.shape[0]
        if rel is None:
            start = 0
        elif half is None:
            start = jnp.bitwise_xor(me, rel) * count
        else:
            start = jnp.bitwise_xor(me, rel) * (2 * count) + half * count
        source = ref.at[:, pl.ds(first, width)]
        place = target.at[pl.ds(start, count), :]
        copies.append(pltpu.make_async_copy(source, place, sems.at[i]))
    return copies


def block_copies(ref, first, target, sems):
    count = sems.shape[0]
    rows, width = target.shape[0] // count, target.shape[1]
    return [
        pltpu.make_async_copy(
            ref.at[pl.ds(i * rows, rows), pl.ds(first, width)],
            target.at[pl.ds(i * rows, rows), :],
            sems.at[i],
        )
        for i in range(count)
    ]


def project_kernel(seq, table, where_ref, *refs):
    own_ref, down_refs, up_refs = refs[0], refs[1:seq], refs[seq : 2 * seq - 1]
    refs = refs[2 * seq - 1 :]
    w_refs, refs = refs[: len(table)], refs[len(table) :]
    gain_ref, shift_ref, bias_ref, first_ref, qkv_ref, x_sc, w_sc, x_sem, w_sem = refs
    step = pl.program_id(0)
    copies = piece_copies(table, where_ref[0], w_refs, 0, w_sc, w_sem)

    @pl.when(step == 0)
    def _():
        for copy in copies:
            copy.start()
        pltpu.make_async_copy(own_ref, x_sc.at[0], x_sem.at[0]).start()
        for j in range(1, seq):
            inside = where_ref[1] + j < seq

            @pl.when(inside)
            def _(j=j):
                pltpu.make_async_copy(down_refs[j - 1], x_sc.at[j], x_sem.at[j]).start()

            @pl.when(jnp.logical_not(inside))
            def _(j=j):
                pltpu.make_async_copy(up_refs[seq - j - 1], x_sc.at[j], x_sem.at[j]).start()

        for copy in copies:
            copy.wait()

    pltpu.make_async_copy(own_ref, x_sc.at[step], x_sem.at[step]).wait()
    hat, _ = standard(x_sc[step].astype(F32))
    first = (hat * gain_ref[...] + shift_ref[...]).astype(BF16)
    first_ref[...] = first
    qkv_ref[...] = (dot(first, w_sc[...]) + bias_ref[...]).astype(BF16)


def project(where, seq, table, tokens, pieces, gain, shift_by, bias):
    local, width = tokens[0].shape
    columns = pieces[0].shape[1]
    vector = pl.BlockSpec((1, width), lambda i: (0, 0))
    return pl.pallas_call(
        functools.partial(project_kernel, seq, table),
        grid=(seq,),
        in_specs=[SCALARS] + [ANY] * (len(tokens) + len(pieces))
        + [vector, vector, pl.BlockSpec((1, columns), lambda i: (0, 0))],
        out_specs=[
            pl.BlockSpec((local, width), lambda i: (i, 0)),
            pl.BlockSpec((local, columns), lambda i: (i, 0)),
        ],
        out_shape=[
            like((seq * local, width), BF16),
            jax.ShapeDtypeStruct((seq * local, columns), BF16),
        ],
        scratch_shapes=[
            pltpu.VMEM((seq, local, width), BF16),
            pltpu.VMEM((width, columns), BF16),
            pltpu.SemaphoreType.DMA((seq,)),
            pltpu.SemaphoreType.DMA((len(table),)),
        ],
        compiler_params=params(32),
        cost_estimate=cost(2 * seq * local * width * columns, 6 * seq * local * width),
        name="project",
    )(where, *placed(*tokens, *pieces), gain[None], shift_by[None], bias[None])


def forward_kernel(scale, seq, q_ref, k_ref, v_ref, *refs):
    mixed_refs, (exact_ref, lse_ref, value_sc) = refs[:seq], refs[seq:]
    step = pl.program_id(0)

    @pl.when(step == 0)
    def _():
        value_sc[:, :PAIR] = v_ref[...]
        value_sc[:, PAIR:] = jnp.ones((value_sc.shape[0], PAIR), value_sc.dtype)

    query = q_ref[...]
    keys = k_ref[...]
    first = lax.broadcasted_iota(jnp.int32, query.shape, 1) < HD
    outs, sums = [], []
    for head in range(2):
        mine = first if head == 0 else jnp.logical_not(first)
        scores = dot(jnp.where(mine, query, jnp.zeros_like(query)), keys, NT)
        peak = jnp.max(scores, -1, keepdims=True)
        expo = jnp.exp2((scores - peak) * scale).astype(BF16)
        both = dot(expo, value_sc[...])
        total = both[:, PAIR:]
        outs.append(both[:, :PAIR] / total)
        sums.append(peak * scale + jnp.log2(total[:, :1]))
    exact = jnp.where(first, outs[0], outs[1])
    exact_ref[...] = exact
    lse_ref[...] = jnp.concatenate(sums, 1)
    for j in range(seq):

        @pl.when(step == j)
        def _(j=j):
            mixed_refs[j][...] = exact.astype(BF16)


def attention_forward(qkv, pair, pairs, seq):
    length = qkv.shape[0]
    rows = length // seq
    row = pl.BlockSpec((rows, PAIR), lambda i: (i, 0))
    return pl.pallas_call(
        functools.partial(forward_kernel, HD**-0.5 * LOG2E, seq),
        grid=(seq,),
        in_specs=[
            pl.BlockSpec((rows, PAIR), lambda i: (i, pair)),
            pl.BlockSpec((length, PAIR), lambda i: (0, pairs + pair)),
            pl.BlockSpec((length, PAIR), lambda i: (0, 2 * pairs + pair)),
        ],
        out_specs=[pl.BlockSpec((rows, PAIR), lambda i: (0, 0))] * seq
        + [row, pl.BlockSpec((rows, 2), lambda i: (i, 0))],
        out_shape=[like((rows, PAIR), BF16)] * seq
        + [like((length, PAIR), F32), like((length, 2), F32)],
        scratch_shapes=[pltpu.VMEM((length, 2 * PAIR), BF16)],
        compiler_params=params(32),
        cost_estimate=cost(
            16 * length * length * PAIR, 14 * length * PAIR, 2 * length * length
        ),
        name="attention_forward",
    )(qkv, qkv, qkv)


def backward_kernel(scale, seq, q_ref, k_ref, v_ref, *refs):
    grad_refs, (exact_ref, lse_ref), refs = refs[:seq], refs[seq : seq + 2], refs[seq + 2 :]
    out_refs, (dk_sc, dv_sc, grad_sc) = refs[:seq], refs[seq:]
    step = pl.program_id(0)

    @pl.when(step == 0)
    def _():
        dk_sc[...] = jnp.zeros_like(dk_sc)
        dv_sc[...] = jnp.zeros_like(dv_sc)

    for j in range(seq):

        @pl.when(step == j)
        def _(j=j):
            grad_sc[...] = grad_refs[j][...]

    query, keys, values, grad = q_ref[...], k_ref[...], v_ref[...], grad_sc[...]
    first = lax.broadcasted_iota(jnp.int32, query.shape, 1) < HD
    product = grad.astype(F32) * exact_ref[...]
    dqs = []
    for head in range(2):
        mine = first if head == 0 else jnp.logical_not(first)
        zero = jnp.zeros_like(query)
        q_one = jnp.where(mine, query, zero)
        g_one = jnp.where(mine, grad, zero)
        inner = jnp.sum(jnp.where(mine, product, 0.0), -1, keepdims=True)
        probs = jnp.exp2(dot(q_one, keys, NT) * (scale * LOG2E) - lse_ref[:, head : head + 1])
        grad_scores = (probs * (dot(g_one, values, NT) - inner)).astype(BF16)
        dqs.append(dot(grad_scores, keys))
        dv_sc[...] += dot(g_one, probs.astype(BF16), TN)
        dk_sc[...] += dot(q_one, grad_scores, TN)
    dq = (jnp.where(first, dqs[0], dqs[1]) * scale).astype(BF16)
    for j in range(seq):

        @pl.when(step == j)
        def _(j=j):
            out_refs[j][:, :PAIR] = dq

    @pl.when(step == pl.num_programs(0) - 1)
    def _():
        dk = (dk_sc[...] * scale).T.astype(BF16)
        dv = dv_sc[...].T.astype(BF16)
        rows = dk.shape[0] // seq
        for j in range(seq):
            out_refs[j][:, PAIR : 2 * PAIR] = dk[j * rows : (j + 1) * rows]
            out_refs[j][:, 2 * PAIR :] = dv[j * rows : (j + 1) * rows]


def attention_backward(qkv, grads, exact, lse, pair, pairs, seq):
    length = qkv.shape[0]
    rows = length // seq
    row = pl.BlockSpec((rows, PAIR), lambda i: (i, 0))
    return pl.pallas_call(
        functools.partial(backward_kernel, HD**-0.5, seq),
        grid=(seq,),
        in_specs=[
            pl.BlockSpec((rows, PAIR), lambda i: (i, pair)),
            pl.BlockSpec((length, PAIR), lambda i: (0, pairs + pair)),
            pl.BlockSpec((length, PAIR), lambda i: (0, 2 * pairs + pair)),
        ]
        + [pl.BlockSpec((rows, PAIR), lambda i: (0, pair))] * seq
        + [row, pl.BlockSpec((rows, 2), lambda i: (i, 0))],
        out_specs=[pl.BlockSpec((rows, 3 * PAIR), lambda i: (0, 0))] * seq,
        out_shape=[like((rows, 3 * PAIR), BF16)] * seq,
        scratch_shapes=[pltpu.VMEM((PAIR, length), F32)] * 2 + [pltpu.VMEM((rows, PAIR), BF16)],
        compiler_params=params(32),
        cost_estimate=cost(
            40 * length * length * PAIR, 20 * length * PAIR, 2 * length * length
        ),
        name="attention_backward",
    )(qkv, qkv, qkv, *placed(*grads, exact, lse))


def block_of(where_ref, j, seq):
    return lax.rem(where_ref[1] + (seq - j), seq)


def hidden_kernel(seq, pairs, where_ref, *refs):
    count = seq * pairs
    mixed_refs, w_ref = refs[:count], refs[count]
    (x_ref, bout_ref, gain_ref, shift_ref, bfc1_ref, attended_ref, middle_ref, second_ref,
     activ_ref, slope_ref, att_sc, wout_sc, wfc1_sc, mixed_sem, wout_sem, wfc1_sem) = refs[count + 1 :]
    step = pl.program_id(0)
    width = x_ref.shape[1]

    @pl.when(step == 0)
    def _():
        out_copies = block_copies(w_ref, 0, wout_sc, wout_sem)
        for j in range(seq):
            for p in range(pairs):
                place = (block_of(where_ref, j, seq) * pairs + p) * PAIR
                out_copies.append(
                    pltpu.make_async_copy(
                        mixed_refs[j * pairs + p],
                        att_sc.at[:, pl.ds(pl.multiple_of(place, PAIR), PAIR)],
                        mixed_sem.at[j * pairs + p],
                    )
                )
        fc1_copies = block_copies(w_ref, width, wfc1_sc, wfc1_sem)
        for copy in out_copies + fc1_copies:
            copy.start()
        for copy in out_copies:
            copy.wait()
        attended = att_sc[...]
        attended_ref[...] = attended
        middle = x_ref[...].astype(F32) + (dot(attended, wout_sc[...]) + bout_ref[...])
        middle_ref[...] = middle
        hat, _ = standard(middle)
        second_ref[...] = (hat * gain_ref[...] + shift_ref[...]).astype(BF16)
        for copy in fc1_copies:
            copy.wait()

    block = bfc1_ref.shape[1]
    start = pl.multiple_of(step * block, block)
    hidden = dot(second_ref[...], wfc1_sc[:, pl.ds(start, block)]) + bfc1_ref[...]
    cdf = 0.5 * (1.0 + lax.erf(hidden * (0.5**0.5)))
    activ_ref[...] = (hidden * cdf).astype(BF16)
    slope_ref[...] = cdf + hidden * jnp.exp(-0.5 * hidden * hidden) * ((2.0 * math.pi) ** -0.5)


def hidden_layer(where, seq, mixed, weights, x, b_out, gain, shift_by, b_fc1, block):
    local, width = x.shape
    high = b_fc1.shape[0]
    pairs = len(mixed) // seq
    fixed = lambda i: (0, 0)
    tall = pl.BlockSpec((local, width), fixed)
    vector = pl.BlockSpec((1, width), fixed)
    wide = pl.BlockSpec((local, block), lambda i: (0, i))
    return pl.pallas_call(
        functools.partial(hidden_kernel, seq, pairs),
        grid=(high // block,),
        in_specs=[SCALARS] + [ANY] * (len(mixed) + 1)
        + [tall, vector, vector, vector, pl.BlockSpec((1, block), lambda i: (0, i))],
        out_specs=[tall, tall, tall, wide, wide],
        out_shape=[
            like((local, width), BF16),
            like((local, width), F32),
            like((local, width), BF16),
            like((local, high), BF16),
            like((local, high), F32),
        ],
        scratch_shapes=[
            pltpu.VMEM((local, width), BF16),
            pltpu.VMEM((width, width), BF16),
            pltpu.VMEM((width, high), BF16),
            pltpu.SemaphoreType.DMA((len(mixed),)),
            pltpu.SemaphoreType.DMA((4,)),
            pltpu.SemaphoreType.DMA((4,)),
        ],
        compiler_params=params(40),
        cost_estimate=cost(2 * local * width * (width + high), 8 * local * high, local * high),
        name="hidden_layer",
    )(where, *placed(*mixed, weights, x), b_out[None], gain[None], shift_by[None], b_fc1[None])


def output_kernel(blocks, where_ref, present_ref, w_ref, activ_ref, slope_ref, middle_ref, cot_ref,
                  bfc2_ref, out_ref, ghid_ref, sum_ref, final_sc, glow_sc, w_sc, w_sem):
    step = pl.program_id(0)
    present = present_ref[0]
    copies = block_copies(w_ref, 0, w_sc, w_sem)

    @pl.when(step == 0)
    def _():
        for copy in copies:
            copy.start()
        glow_sc[...] = (cot_ref[...].astype(F32) * present).astype(BF16)
        final_sc[...] = middle_ref[...] + bfc2_ref[...]

    for i in range(blocks):

        @pl.when(step == i)
        def _(i=i):
            copies[i].wait()

    block = activ_ref.shape[1]
    below = w_sc[pl.ds(pl.multiple_of(step * block, block), block), :]
    final_sc[...] += dot(activ_ref[...], below)
    grad_hidden = (dot(glow_sc[...], below, NT) * slope_ref[...]).astype(BF16)
    ghid_ref[...] = grad_hidden
    sum_ref[...] = jnp.sum(grad_hidden.astype(F32), 0, keepdims=True)

    @pl.when(step == blocks - 1)
    def _():
        out_ref[...] = (final_sc[...] * present).astype(BF16)


def output_layer(where, present, weights, activ, slope, middle, cot, b_fc2):
    local, width = middle.shape
    high = activ.shape[1]
    blocks = 8
    fixed = lambda i: (0, 0)
    tall = pl.BlockSpec((local, width), fixed)
    wide = pl.BlockSpec((local, high // blocks), lambda i: (0, i))
    return pl.pallas_call(
        functools.partial(output_kernel, blocks),
        grid=(blocks,),
        in_specs=[SCALARS, SCALARS, ANY, wide, wide, tall, tall, pl.BlockSpec((1, width), fixed)],
        out_specs=[tall, wide, pl.BlockSpec((1, high // blocks), lambda i: (0, i))],
        out_shape=[like((local, width), BF16), like((local, high), BF16), like((1, high), F32)],
        scratch_shapes=[
            pltpu.VMEM((local, width), F32),
            pltpu.VMEM((local, width), BF16),
            pltpu.VMEM((high, width), BF16),
            pltpu.SemaphoreType.DMA((blocks,)),
        ],
        compiler_params=params(40),
        cost_estimate=cost(4 * local * width * high, 12 * local * high),
        name="output_layer",
    )(where, present, *placed(weights, activ, slope, middle, cot), b_fc2[None])


def middle_kernel(seq, blocks, where_ref, present_ref, w_ref, ghid_ref, middle_ref, cot_ref,
                  gain_ref, gmid_ref, gbranch_ref, *refs):
    gmixed_refs, (sums_ref, gsecond_sc, wout_sc, wfc1_sc, wout_sem, wfc1_sem) = refs[:seq], refs[seq:]
    step = pl.program_id(0)
    width = middle_ref.shape[1]
    present = present_ref[0]
    upper = block_copies(w_ref, width, wfc1_sc, wfc1_sem)
    outer = block_copies(w_ref, 0, wout_sc, wout_sem)

    @pl.when(step == 0)
    def _():
        for copy in upper + outer:
            copy.start()
        gsecond_sc[...] = jnp.zeros_like(gsecond_sc)
        for copy in upper:
            copy.wait()

    block = ghid_ref.shape[1]
    start = pl.multiple_of(step * block, block)
    gsecond_sc[...] += dot(ghid_ref[...], wfc1_sc[:, pl.ds(start, block)], NT)

    @pl.when(step == blocks - 1)
    def _():
        for copy in outer:
            copy.wait()
        hat, inverse = standard(middle_ref[...])
        grad_second = gsecond_sc[...]
        grad_rows = cot_ref[...].astype(F32) * present
        grad_middle = grad_rows + norm_grad(grad_second, hat, inverse, gain_ref[...])
        gmid_ref[...] = grad_middle
        grad_branch = grad_middle.astype(BF16)
        gbranch_ref[...] = grad_branch
        sums_ref[...] = jnp.concatenate(
            [
                jnp.sum(grad_branch.astype(F32), 0, keepdims=True),
                jnp.sum(grad_second * hat, 0, keepdims=True),
                jnp.sum(grad_second, 0, keepdims=True),
                jnp.sum(grad_rows, 0, keepdims=True),
            ],
            0,
        )
        own = width // seq
        for j in range(seq):
            rows = pl.multiple_of(block_of(where_ref, j, seq) * own, own)
            gmixed_refs[j][...] = dot(grad_branch, wout_sc[pl.ds(rows, own), :], NT).astype(BF16)


def middle_layer(where, present, seq, weights, grad_hidden, middle, cot, gain):
    local, width = middle.shape
    high = grad_hidden.shape[1]
    blocks = 4
    fixed = lambda i: (0, 0)
    tall = pl.BlockSpec((local, width), fixed)
    own = width // seq
    return pl.pallas_call(
        functools.partial(middle_kernel, seq, blocks),
        grid=(blocks,),
        in_specs=[
            SCALARS,
            SCALARS,
            ANY,
            pl.BlockSpec((local, high // blocks), lambda i: (0, i)),
            tall,
            tall,
            pl.BlockSpec((1, width), fixed),
        ],
        out_specs=[tall, tall]
        + [pl.BlockSpec((local, own), fixed)] * seq
        + [pl.BlockSpec((4, width), fixed)],
        out_shape=[like((local, width), F32), like((local, width), BF16)]
        + [like((local, own), BF16)] * seq
        + [like((4, width), F32)],
        scratch_shapes=[
            pltpu.VMEM((local, width), F32),
            pltpu.VMEM((width, width), BF16),
            pltpu.VMEM((width, high), BF16),
            pltpu.SemaphoreType.DMA((4,)),
            pltpu.SemaphoreType.DMA((4,)),
        ],
        compiler_params=params(40),
        cost_estimate=cost(2 * local * width * (width + high), 12 * local * high),
        name="middle_layer",
    )(where, present, *placed(weights, grad_hidden, middle, cot), gain[None])


def last_kernel(seq, pairs, where_ref, *refs):
    count = seq * pairs
    grad_refs, w_ref = refs[:count], refs[count]
    x_ref, gmid_ref, gain_ref, out_ref, sums_ref, grad_sc, w_sc, grad_sem, w_sem = refs[count + 1 :]
    width = x_ref.shape[1]
    copies = block_copies(w_ref, 0, w_sc, w_sem)
    for j in range(seq):
        for p in range(pairs):
            place = (block_of(where_ref, j, seq) * pairs + p) * PAIR
            for t in range(3):
                copies.append(
                    pltpu.make_async_copy(
                        grad_refs[j * pairs + p].at[:, pl.ds(t * PAIR, PAIR)],
                        grad_sc.at[:, pl.ds(pl.multiple_of(t * width + place, PAIR), PAIR)],
                        grad_sem.at[(j * pairs + p) * 3 + t],
                    )
                )
    for copy in copies:
        copy.start()
    hat, inverse = standard(x_ref[...].astype(F32))
    for copy in copies:
        copy.wait()
    grad_first = dot(grad_sc[...], w_sc[...], NT)
    out_ref[...] = gmid_ref[...] + norm_grad(grad_first, hat, inverse, gain_ref[...])
    sums_ref[...] = jnp.concatenate(
        [jnp.sum(grad_first * hat, 0, keepdims=True), jnp.sum(grad_first, 0, keepdims=True)], 0
    )


def last_layer(where, seq, grads, weights, x, grad_middle, gain):
    local, width = x.shape
    pairs = len(grads) // seq
    whole = pl.BlockSpec(memory_space=pltpu.VMEM)
    return pl.pallas_call(
        functools.partial(last_kernel, seq, pairs),
        in_specs=[SCALARS] + [ANY] * (len(grads) + 1) + [whole] * 3,
        out_specs=[whole, whole],
        out_shape=[like((local, width), F32), like((2, width), F32)],
        scratch_shapes=[
            pltpu.VMEM((local, 3 * width), BF16),
            pltpu.VMEM((width, 3 * width), BF16),
            pltpu.SemaphoreType.DMA((3 * len(grads),)),
            pltpu.SemaphoreType.DMA((4,)),
        ],
        compiler_params=params(56),
        cost_estimate=cost(6 * local * width * width, 6 * width * width),
        name="last_layer",
    )(where, *placed(*grads, weights, x, grad_middle), gain[None])


def product(sides, refs):
    parts = []
    for count in sides:
        left, right_refs, refs = refs[0][...], refs[1 : 1 + count], refs[1 + count :]
        rows = right_refs[0].shape[0]
        groups = left.shape[0] // rows
        total = None
        for g in range(groups):
            blocks = [r[...] for r in right_refs[g::groups]]
            right = blocks[0] if len(blocks) == 1 else jnp.concatenate(blocks, 1)
            term = dot(left[g * rows : (g + 1) * rows], right, TN)
            total = term if total is None else total + term
        parts.append(total)
    return parts[0] if len(parts) == 1 else jnp.concatenate(parts, 1)


def away_kernel(sides, where_ref, *refs):
    refs[-1][0] = product(sides, refs[:-1]).astype(BF16)


def kept_kernel(sides, where_ref, *refs):
    refs, (arrived_ref, far1, keep1, far2, keep2) = refs[:-5], refs[-5:]
    step = pl.program_id(0)
    total = (product(sides, refs) + arrived_ref[0].astype(F32)).astype(BF16)
    half = total.shape[1] // 2

    @pl.when(step % 2 == 1)
    def _():
        far1[0] = total[:, :half]

    @pl.when(step % 2 == 0)
    def _():
        keep1[0] = total[:, :half]

    @pl.when(step >= 2)
    def _():
        far2[0] = total[:, half:]

    @pl.when(step < 2)
    def _():
        keep2[0] = total[:, half:]


def weight_shape(job):
    columns = [sum(r.shape[1] for r in rights) * rights[0].shape[0] // left.shape[0]
               for left, rights in job]
    return job[0][0].shape[1] // 8, sum(columns)


def weight_call(where, job, kernel, odd, more, out_specs, out_shape, name):
    rest, columns = weight_shape(job)
    specs, args = [], []
    for left, rights in job:
        specs.append(
            pl.BlockSpec(
                (left.shape[0], rest), lambda i, w: (0, jnp.bitwise_xor(w[0], 2 * i + odd))
            )
        )
        specs += [pl.BlockSpec(r.shape, lambda i, w: (0, 0)) for r in rights]
        args += [left, *rights]
    return pl.pallas_call(
        functools.partial(kernel, [len(rights) for _, rights in job]),
        grid_spec=pltpu.PrefetchScalarGridSpec(
            num_scalar_prefetch=1,
            grid=(4,),
            in_specs=specs
            + [pl.BlockSpec((1, rest, columns), lambda i, w: (i, 0, 0)) for _ in more],
            out_specs=out_specs,
        ),
        out_shape=out_shape,
        compiler_params=params(48),
        cost_estimate=cost(job[0][0].shape[0] * 8 * rest * columns, 8 * rest * columns),
        name=name,
    )(where, *placed(*args, *more))


def weight_away(where, job):
    rest, columns = weight_shape(job)
    return weight_call(
        where,
        job,
        away_kernel,
        1,
        [],
        pl.BlockSpec((1, rest, columns), lambda i, w: (i, 0, 0)),
        like((4, rest, columns), BF16),
        "weight_away",
    )


def weight_kept(where, job, arrived, ahead):
    rest, columns = weight_shape(job)
    two = like((2, rest, columns // 2), BF16)

    def spec(which):
        return pl.BlockSpec((1, rest, columns // 2), lambda i, w: (which(i), 0, 0))

    far1, keep1, far2, keep2 = weight_call(
        where,
        job,
        kept_kernel,
        0,
        [arrived],
        [
            spec(lambda i: i // 2),
            spec(lambda i: i // 2),
            spec(lambda i: jnp.maximum(i - 2, 0)),
            spec(lambda i: jnp.minimum(i, 1)),
        ],
        [two] * 4,
        "weight_kept",
    )
    if ahead:
        far1, far2 = after((far1, far2), ahead)
    return (keep1, flip(far1, 1, 8)), (keep2, flip(far2, 2, 8))


def second_kernel(keep1_ref, came1_ref, keep2_ref, came2_ref, *out_refs):
    far1, stay1, far2, stay2 = out_refs
    for keep_ref, came_ref, far, stay in (
        (keep1_ref, came1_ref, far1, stay1),
        (keep2_ref, came2_ref, far2, stay2),
    ):
        total = (keep_ref[...].astype(F32) + came_ref[...].astype(F32)).astype(BF16)
        stay[...] = total[0]
        far[...] = total[1]


def second_sums(first, before, ahead):
    (keep1, came1), (keep2, came2) = first
    keep1 = after(keep1, before)
    _, rest, half = keep1.shape
    rows = rest // 4
    spec = pl.BlockSpec((2, rows, half), lambda i: (0, i, 0))
    out = pl.BlockSpec((rows, half), lambda i: (i, 0))
    far1, stay1, far2, stay2 = pl.pallas_call(
        second_kernel,
        grid=(4,),
        in_specs=[spec] * 4,
        out_specs=[out] * 4,
        out_shape=[like((rest, half), BF16)] * 4,
        compiler_params=params(32),
        cost_estimate=cost(4 * rest * half, 24 * rest * half),
        name="second_sums",
    )(*placed(keep1, came1, keep2, came2))
    far1, far2 = after((far1, far2), ahead)
    return (stay1, flip(far1, 2, 8)), (stay2, flip(far2, 1, 8))


def spread_kernel(seq, where_ref, *refs):
    ins, outs = refs[:-seq], refs[-seq:]
    both = jnp.concatenate(
        [a[...].astype(F32) + b[...].astype(F32) for a, b in zip(ins[0::2], ins[1::2])], 1
    )
    for j, out_ref in enumerate(outs):

        @pl.when(pl.program_id(0) == j)
        def _(out_ref=out_ref):
            out_ref[...] = both.astype(out_ref.dtype)


def seq_spread(where, seconds, seq):
    arrays = [array for second in seconds for part in second for array in part]
    rest = arrays[0].shape[0]
    rows = rest // seq
    columns = sum(a.shape[1] for a in arrays[::2])
    blocks = [
        pl.BlockSpec((rows, a.shape[1]), lambda i, w: (lax.rem(w[1] + i, seq), 0)) for a in arrays
    ]
    out = pl.BlockSpec((rows, columns), lambda i, w: (0, 0))
    return pl.pallas_call(
        functools.partial(spread_kernel, seq),
        grid_spec=pltpu.PrefetchScalarGridSpec(
            num_scalar_prefetch=1, grid=(seq,), in_specs=blocks, out_specs=[out] * seq
        ),
        out_shape=[like((rows, columns), F32)] + [like((rows, columns), BF16)] * (seq - 1),
        compiler_params=params(32),
        cost_estimate=cost(rest * columns, 8 * rest * columns),
        name="seq_spread",
    )(where, *placed(*arrays))


def plain_sums(job, seq):
    blocks = []
    for left, rights in job:
        groups = left.shape[0] // rights[0].shape[0]
        right = jnp.concatenate([jnp.concatenate(rights[g::groups], 1) for g in range(groups)], 0)
        product = dot(left, right, TN)
        blocks.append(lax.psum_scatter(product, "fsdp", scatter_dimension=0, tiled=True))
    me = lax.axis_index("seq")
    parts = jnp.concatenate(blocks, 1)
    parts = parts.reshape(seq, parts.shape[0] // seq, parts.shape[1])
    chunks = [lax.dynamic_index_in_dim(parts, (me + j) % seq, 0, False) for j in range(seq)]
    return [chunks[0]] + [c.astype(BF16) for c in chunks[1:]]


def sum_vectors(vectors, fsdp, seq):
    me = lax.axis_index("fsdp")
    bits = fsdp.bit_length() - 1
    sizes = [v.shape[0] // (fsdp * seq) for v in vectors]
    block = jnp.concatenate([v.reshape(fsdp, seq, -1) for v in vectors], 2)
    block = block.reshape((2,) * bits + (seq, sum(sizes)))
    for bit in range(bits):
        axis = bits - 1 - bit
        mine = (me >> bit) & 1
        away = lax.dynamic_index_in_dim(block, 1 - mine, axis, False)
        block = lax.dynamic_index_in_dim(block, mine, axis, False) + flip(away, bit, fsdp)
    return block, sizes


def split_vectors(block, sizes, seq):
    place = lax.axis_index("seq")
    total = lax.dynamic_index_in_dim(block, place, 0, False)
    for by in range(1, seq):
        away = lax.dynamic_index_in_dim(block, (place + by) % seq, 0, False)
        total = total + shift(away, by, seq)
    return jnp.split(total, [sum(sizes[: i + 1]) for i in range(len(sizes) - 1)])


def after(value, *others):
    return lax.optimization_barrier((value, others))[0]


def spread_pairs(parts, seq):
    arrived = []
    for blocks in parts:
        if arrived:
            blocks = after(blocks, arrived[-1][1:])
        arrived.append([blocks[0]] + [shift(blocks[j], j, seq) for j in range(1, seq)])
    return [pair[j] for j in range(seq) for pair in arrived]


def on_device(
    fsdp,
    seq,
    inputs,
    clip_mask,
    ln1_gain,
    ln1_bias,
    w_query,
    b_query,
    w_key,
    w_value,
    b_value,
    w_out,
    b_out,
    ln2_gain,
    ln2_bias,
    w_fc1,
    b_fc1,
    w_fc2,
    b_fc2,
    cotangent,
):
    clips, local, width = inputs.shape
    assert clips == 1
    me = lax.axis_index("seq")
    where = jnp.stack([lax.axis_index("fsdp"), me]).astype(jnp.int32)
    present = clip_mask.astype(F32)
    own = width // seq
    pairs = own // PAIR
    table = piece_table(fsdp)
    x, cot = inputs[0], cotangent[0]
    grad_low = (cot.astype(F32) * present).astype(BF16)

    def columns(array, axis):
        return lax.dynamic_slice_in_dim(array, me * own, own, axis)

    shard_heads = jnp.concatenate([columns(w, 1) for w in (w_query, w_key, w_value)], 1)
    near_heads = gather_near(shard_heads, fsdp)
    down, up = [x], [x]
    for hop in range(1, seq):
        if hop == 2:
            down[-1], up[-1], near_heads = after((down[-1], up[-1], near_heads))
            w_heads = gather_pieces(shard_heads, near_heads, fsdp)
        if hop == 3:
            down[-1], up[-1] = after((down[-1], up[-1]), w_heads)
        down.append(lax.ppermute(down[-1], "seq", [(i, i - 1) for i in range(1, seq + 1 - hop)]))
        up.append(lax.ppermute(up[-1], "seq", [(i, i + 1) for i in range(hop - 1, seq - 1)]))
    b_heads = jnp.concatenate([columns(b_query, 0), jnp.zeros((own,), F32), columns(b_value, 0)])
    one = lax.all_gather(jnp.concatenate([w_out, w_fc1], 1), "fsdp", axis=0, tiled=True)
    two = lax.all_gather(after(w_fc2, down[1], up[1]), "fsdp", axis=0, tiled=True)
    shard_three = jnp.concatenate([w_query, w_key, w_value], 1)
    three = lax.all_gather(after(shard_three, down[2], up[2]), "fsdp", axis=0, tiled=True)

    first_in, qkv = project(
        where,
        seq,
        table,
        [x] + down[1:] + up[1:],
        w_heads,
        ln1_gain,
        ln1_bias,
        b_heads,
    )
    forward = [attention_forward(qkv, 0, pairs, seq)]
    for p in range(1, pairs):
        forward.append(attention_forward(qkv, p, pairs, seq))
    mixed = spread_pairs([part[:seq] for part in forward], seq)
    attended, middle, second_in, activ, slope = hidden_layer(
        where, seq, mixed, one, x, b_out, ln2_gain, ln2_bias, b_fc1, 512
    )
    parts = {}

    def away(name, job, before):
        if fsdp == 8:
            parts[name] = weight_away(after(where, before), job)
        else:
            parts[name] = plain_sums(job, seq)
        return parts[name]

    def kept(name, job, before, first=(), ahead=()):
        if fsdp != 8:
            return ()
        arrived = flip(after(parts[name], first), 0, 8)
        parts[name] = weight_kept(after(where, before), job, arrived, ahead)
        return parts[name][0][0]

    def second(name, before, ahead=()):
        if fsdp != 8:
            return ()
        parts[name] = second_sums(parts[name], before, ahead)
        return parts[name][0][0]

    def chunks(names, before):
        if fsdp == 8:
            return seq_spread(after(where, before), [parts[n] for n in names], seq)
        return [jnp.concatenate(blocks, 1) for blocks in zip(*[parts[n] for n in names])]

    def came(name):
        return (parts[name][0][1], parts[name][1][1]) if fsdp == 8 else ()

    def send(blocks, ahead):
        if ahead:
            blocks = after(blocks, ahead)
        return [blocks[0]] + [shift(blocks[j], j, seq) for j in range(1, seq)]

    low = [(activ, [grad_low])]
    step = away("low", low, ())
    output, grad_hidden, sum_fc1 = output_layer(
        after(where, step), present, two, activ, slope, middle, cot, b_fc2
    )
    step = kept("low", low, grad_hidden)
    high = [(second_in, [grad_hidden])]
    step = away("high", high, step)
    results = middle_layer(
        after(where, step, three), present, seq, one, grad_hidden, middle, cot, ln2_gain
    )
    grad_middle, grad_branch = results[:2]
    grad_mixed, sums2 = results[2 : 2 + seq], results[2 + seq]
    grads = [grad_mixed[0]] + [shift(grad_mixed[j], -j, seq) for j in range(1, seq)]
    low_came = came("low")
    step = second("low", grad_branch)
    step = kept("high", high, step, (low_came, grad_branch), grads[1:])
    low_rows = chunks(["low"], step)
    step = low_rows[1]
    low_rows = send(low_rows, grads[1:])
    back, home = [], []
    for p in range(pairs):
        exact, lse = forward[p][seq:]
        back.append(attention_backward(qkv, grads, exact, after(lse, step), p, pairs, seq))
        home.append(send(back[-1], home[-1][1:] if home else low_rows[1:]))
        step = back[-1][0]
    total_low = sum(rows.astype(F32) for rows in low_rows)
    step = second("high", step, home[0][1:])
    late = [(first_in, [b for pair in back for b in pair]), (attended, [grad_branch])]
    step = away("late", late, step)
    step = kept("late", late, step, home[0][1:], home[1][1:])
    high_rows = chunks(["high"], step)
    step = high_rows[1]
    high_rows = send(high_rows, home[1][1:])
    step = second("late", step)
    grad_inputs, sums1 = last_layer(
        after(where, step),
        seq,
        [pair[j] for j in range(seq) for pair in home],
        three,
        x,
        grad_middle,
        ln1_gain,
    )
    late_rows = chunks(["late"], sums1)

    def spread(which):
        vector = jnp.concatenate(
            [
                sum(
                    jnp.sum(block[:, which * PAIR : (which + 1) * PAIR].astype(F32), 0)
                    for block in back[p]
                )
                for p in range(pairs)
            ]
        )
        return lax.dynamic_update_slice(jnp.zeros((width,), F32), vector, (me * own,))

    sums1 = after(sums1, high_rows[1:], late_rows[1])
    block, sizes = sum_vectors(
        [sums1[0], sums1[1], spread(0), spread(2)] + [sums2[i] for i in range(4)] + [sum_fc1[0]],
        fsdp,
        seq,
    )
    split = 3 * own
    sent = send(late_rows, high_rows[1:])
    rows = after(sent, block)
    total_out = sum(part[:, split:].astype(F32) for part in rows)
    total_high = sum(part.astype(F32) for part in high_rows)
    heads = [part[:, :split].astype(F32) for part in rows[::-1]]
    grad_heads = lax.dynamic_slice_in_dim(jnp.stack(heads + heads), (seq - 1 - me) % seq, seq, 0)
    strip = grad_heads.shape[1]
    grad_heads = grad_heads.reshape(seq, strip, pairs, 3, PAIR).transpose(3, 1, 0, 2, 4)
    grad_heads = grad_heads.reshape(3, strip, width)

    sums = split_vectors(after(block, sent[1:]), sizes, seq)
    return (
        output[None],
        grad_inputs[None],
        sums[0],
        sums[1],
        grad_heads[0],
        sums[2],
        grad_heads[1],
        grad_heads[2],
        sums[3],
        total_out,
        sums[4],
        sums[5],
        sums[6],
        total_high,
        sums[8],
        total_low,
        sums[7],
    )


def solution(mesh):
    rows, both = P("fsdp", None), P(("fsdp", "seq"))
    tokens = P("fsdp", "seq", None)
    matrix = P(("fsdp", "seq"), None)
    return jax.shard_map(
        functools.partial(on_device, mesh.shape["fsdp"], mesh.shape["seq"]),
        mesh=mesh,
        in_specs=(
            tokens,
            P("fsdp"),
            P(),
            P(),
            rows,
            P(),
            rows,
            rows,
            P(),
            rows,
            P(),
            P(),
            P(),
            rows,
            P(),
            rows,
            P(),
            tokens,
        ),
        out_specs=(
            tokens,
            tokens,
            both,
            both,
            matrix,
            both,
            matrix,
            matrix,
            both,
            matrix,
            both,
            both,
            both,
            matrix,
            both,
            matrix,
            both,
        ),
        check_vma=False,
    )
```

```python
import functools
import math

import jax
import jax.numpy as jnp
from jax import lax
from jax.experimental import pallas as pl
from jax.experimental.pallas import tpu as pltpu
from jax.sharding import PartitionSpec as P

HD = 64
PAIR = 2 * HD
EPSILON = 1e-06
LOG2E = math.log2(math.e)
BF16 = jnp.bfloat16
F32 = jnp.float32
NT = (((1,), (1,)), ((), ()))
NN = (((1,), (0,)), ((), ()))
TN = (((0,), (0,)), ((), ()))
ANY = pl.BlockSpec(memory_space=pl.ANY)
SCALARS = pl.BlockSpec(memory_space=pltpu.SMEM)


def dot(a, b, dims=NN):
    return lax.dot_general(a, b, dims, preferred_element_type=F32)


def like(shape, dtype):
    return pltpu.HBM(shape, dtype)


def placed(*arrays):
    return [pltpu.with_memory_space_constraint(a, pltpu.HBM) for a in arrays]


def standard(rows):
    center = rows - jnp.mean(rows, -1, keepdims=True)
    inverse = lax.rsqrt(jnp.mean(center * center, -1, keepdims=True) + EPSILON)
    return center * inverse, inverse


def norm_grad(grad, normed, inverse, gain):
    scaled = grad * gain
    inner = (
        scaled
        - jnp.mean(scaled, -1, keepdims=True)
        - normed * jnp.mean(scaled * normed, -1, keepdims=True)
    )
    return inner * inverse


def params(mib):
    return pltpu.CompilerParams(vmem_limit_bytes=mib << 20)


def cost(flops, moved, special=0):
    return pl.CostEstimate(flops=flops // 64, bytes_accessed=moved // 64, transcendentals=0)


def piece_table(size):
    if size != 8:
        return [(None, None)]
    return [(far + near, half) for near in (0, 1) for far, half in
            ((0, None), (2, None), (4, None), (6, 0), (6, 1))]


def flip(array, bit, size):
    return lax.ppermute(array, "fsdp", [(i, i ^ (1 << bit)) for i in range(size)])


def shift(array, by, size):
    return lax.ppermute(array, "seq", [(i, (i + by) % size) for i in range(size)])


def gather_near(shard, size):
    return (flip(shard, 1, size), flip(shard, 2, size)) if size == 8 else ()


def gather_pieces(shard, near, size):
    if size != 8:
        return [lax.all_gather(shard, "fsdp", axis=0, tiled=True)]
    half = shard.shape[0] // 2
    one, two = near
    top, low = flip(one[:half], 2, size), flip(two[half:], 1, size)
    pieces = [shard, one, two, top, low]
    return pieces + [flip(piece, 0, size) for piece in pieces]


def piece_copies(table, me, refs, first, target, sems):
    width = target.shape[1]
    copies = []
    for i, ((rel, half), ref) in enumerate(zip(table, refs)):
        count = ref.shape[0]
        if rel is None:
            start = 0
        elif half is None:
            start = jnp.bitwise_xor(me, rel) * count
        else:
            start = jnp.bitwise_xor(me, rel) * (2 * count) + half * count
        source = ref.at[:, pl.ds(first, width)]
        place = target.at[pl.ds(start, count), :]
        copies.append(pltpu.make_async_copy(source, place, sems.at[i]))
    return copies


def block_copies(ref, first, target, sems):
    count = sems.shape[0]
    rows, width = target.shape[0] // count, target.shape[1]
    return [
        pltpu.make_async_copy(
            ref.at[pl.ds(i * rows, rows), pl.ds(first, width)],
            target.at[pl.ds(i * rows, rows), :],
            sems.at[i],
        )
        for i in range(count)
    ]


def last_block(me, seq):
    return jnp.where(2 * me < seq, seq - 1 - me, seq - me)


def project_kernel(seq, table, rest, where_ref, *refs):
    own_ref, down_refs, up_refs = refs[0], refs[1:seq], refs[seq : 2 * seq - 1]
    refs = refs[2 * seq - 1 :]
    w_refs, refs = refs[: len(table)], refs[len(table) :]
    gain_ref, shift_ref, bias_ref, first_ref, qkv_ref, x_sc, w_sc, x_sem, w_sem = (
        refs[:3] + refs[3 + 2 * rest :]
    )
    step = pl.program_id(0)
    me = where_ref[1]
    late = last_block(me, seq)
    copies = piece_copies(table, where_ref[0], w_refs, 0, w_sc, w_sem)

    @pl.when(step == 0)
    def _():
        for copy in copies:
            copy.start()
        if not rest:
            pltpu.make_async_copy(own_ref, x_sc.at[0], x_sem.at[0]).start()
        for j in range(1, seq):
            wanted = (late == j) if rest else (late != j)
            inside = me + j < seq
            if rest or j < seq - 1:

                @pl.when(jnp.logical_and(wanted, inside))
                def _(j=j):
                    pltpu.make_async_copy(down_refs[j - 1], x_sc.at[j], x_sem.at[j]).start()

            if rest or j > 1:

                @pl.when(jnp.logical_and(wanted, jnp.logical_not(inside)))
                def _(j=j):
                    pltpu.make_async_copy(up_refs[seq - j - 1], x_sc.at[j], x_sem.at[j]).start()

        for copy in copies:
            copy.wait()

    block = late if rest else step + jnp.where(step >= late, 1, 0)
    pltpu.make_async_copy(own_ref, x_sc.at[block], x_sem.at[block]).wait()
    hat, _ = standard(x_sc[block].astype(F32))
    first = (hat * gain_ref[...] + shift_ref[...]).astype(BF16)
    first_ref[...] = first
    qkv_ref[...] = (dot(first, w_sc[...]) + bias_ref[...]).astype(BF16)


def project(where, seq, table, tokens, pieces, gain, shift_by, bias, before=None):
    local, width = tokens[0].shape
    columns = pieces[0].shape[1]
    rest = before is not None

    def fixed(i, w):
        return (0, 0)

    def turn(i, w):
        late = last_block(w[1], seq)
        return (late if rest else i + jnp.where(i >= late, 1, 0), 0)

    vector = pl.BlockSpec((1, width), fixed)
    count = len(tokens) + len(pieces) + 4
    return pl.pallas_call(
        functools.partial(project_kernel, seq, table, rest),
        grid_spec=pltpu.PrefetchScalarGridSpec(
            num_scalar_prefetch=1,
            grid=(1 if rest else seq - 1,),
            in_specs=[ANY] * (len(tokens) + len(pieces))
            + [vector, vector, pl.BlockSpec((1, columns), fixed)]
            + [ANY] * (2 * rest),
            out_specs=[pl.BlockSpec((local, width), turn), pl.BlockSpec((local, columns), turn)],
            scratch_shapes=[
                pltpu.VMEM((seq, local, width), BF16),
                pltpu.VMEM((width, columns), BF16),
                pltpu.SemaphoreType.DMA((seq,)),
                pltpu.SemaphoreType.DMA((len(table),)),
            ],
        ),
        out_shape=[
            like((seq * local, width), BF16),
            jax.ShapeDtypeStruct((seq * local, columns), BF16),
        ],
        input_output_aliases={count: 0, count + 1: 1} if rest else {},
        compiler_params=params(32),
        cost_estimate=cost(2 * seq * local * width * columns, 6 * seq * local * width),
        name="project",
    )(
        where,
        *placed(*tokens, *pieces),
        gain[None],
        shift_by[None],
        bias[None],
        *(before if rest else ()),
    )


def forward_kernel(scale, seq, q_ref, k_ref, v_ref, *refs):
    mixed_refs, (exact_ref, lse_ref, value_sc) = refs[:seq], refs[seq:]
    step = pl.program_id(0)

    @pl.when(step == 0)
    def _():
        value_sc[:, :PAIR] = v_ref[...]
        value_sc[:, PAIR:] = jnp.ones((value_sc.shape[0], PAIR), value_sc.dtype)

    query = q_ref[...]
    keys = k_ref[...]
    first = lax.broadcasted_iota(jnp.int32, query.shape, 1) < HD
    outs, sums = [], []
    for head in range(2):
        mine = first if head == 0 else jnp.logical_not(first)
        scores = dot(jnp.where(mine, query, jnp.zeros_like(query)), keys, NT)
        peak = jnp.max(scores, -1, keepdims=True)
        expo = jnp.exp2((scores - peak) * scale).astype(BF16)
        both = dot(expo, value_sc[...])
        total = both[:, PAIR:]
        outs.append(both[:, :PAIR] / total)
        sums.append(peak * scale + jnp.log2(total[:, :1]))
    exact = jnp.where(first, outs[0], outs[1])
    exact_ref[...] = exact
    lse_ref[...] = jnp.concatenate(sums, 1)
    for j in range(seq):

        @pl.when(step == j)
        def _(j=j):
            mixed_refs[j][...] = exact.astype(BF16)


def attention_forward(qkv, pair, pairs, seq):
    length = qkv.shape[0]
    rows = length // seq
    row = pl.BlockSpec((rows, PAIR), lambda i: (i, 0))
    return pl.pallas_call(
        functools.partial(forward_kernel, HD**-0.5 * LOG2E, seq),
        grid=(seq,),
        in_specs=[
            pl.BlockSpec((rows, PAIR), lambda i: (i, pair)),
            pl.BlockSpec((length, PAIR), lambda i: (0, pairs + pair)),
            pl.BlockSpec((length, PAIR), lambda i: (0, 2 * pairs + pair)),
        ],
        out_specs=[pl.BlockSpec((rows, PAIR), lambda i: (0, 0))] * seq
        + [row, pl.BlockSpec((rows, 2), lambda i: (i, 0))],
        out_shape=[like((rows, PAIR), BF16)] * seq
        + [like((length, PAIR), F32), like((length, 2), F32)],
        scratch_shapes=[pltpu.VMEM((length, 2 * PAIR), BF16)],
        compiler_params=params(32),
        cost_estimate=cost(
            16 * length * length * PAIR, 14 * length * PAIR, 2 * length * length
        ),
        name="attention_forward",
    )(qkv, qkv, qkv)


def backward_kernel(scale, seq, q_ref, k_ref, v_ref, *refs):
    grad_refs, (exact_ref, lse_ref), refs = refs[:seq], refs[seq : seq + 2], refs[seq + 2 :]
    out_refs, (dk_sc, dv_sc, grad_sc) = refs[:seq], refs[seq:]
    step = pl.program_id(0)

    @pl.when(step == 0)
    def _():
        dk_sc[...] = jnp.zeros_like(dk_sc)
        dv_sc[...] = jnp.zeros_like(dv_sc)

    for j in range(seq):

        @pl.when(step == j)
        def _(j=j):
            grad_sc[...] = grad_refs[j][...]

    query, keys, values, grad = q_ref[...], k_ref[...], v_ref[...], grad_sc[...]
    first = lax.broadcasted_iota(jnp.int32, query.shape, 1) < HD
    product = grad.astype(F32) * exact_ref[...]
    dqs = []
    for head in range(2):
        mine = first if head == 0 else jnp.logical_not(first)
        zero = jnp.zeros_like(query)
        q_one = jnp.where(mine, query, zero)
        g_one = jnp.where(mine, grad, zero)
        inner = jnp.sum(jnp.where(mine, product, 0.0), -1, keepdims=True)
        probs = jnp.exp2(dot(q_one, keys, NT) * (scale * LOG2E) - lse_ref[:, head : head + 1])
        grad_scores = (probs * (dot(g_one, values, NT) - inner)).astype(BF16)
        dqs.append(dot(grad_scores, keys))
        dv_sc[...] += dot(g_one, probs.astype(BF16), TN)
        dk_sc[...] += dot(q_one, grad_scores, TN)
    dq = (jnp.where(first, dqs[0], dqs[1]) * scale).astype(BF16)
    for j in range(seq):

        @pl.when(step == j)
        def _(j=j):
            out_refs[j][:, :PAIR] = dq

    @pl.when(step == pl.num_programs(0) - 1)
    def _():
        dk = (dk_sc[...] * scale).T.astype(BF16)
        dv = dv_sc[...].T.astype(BF16)
        rows = dk.shape[0] // seq
        for j in range(seq):
            out_refs[j][:, PAIR : 2 * PAIR] = dk[j * rows : (j + 1) * rows]
            out_refs[j][:, 2 * PAIR :] = dv[j * rows : (j + 1) * rows]


def attention_backward(qkv, grads, exact, lse, pair, pairs, seq):
    length = qkv.shape[0]
    rows = length // seq
    row = pl.BlockSpec((rows, PAIR), lambda i: (i, 0))
    return pl.pallas_call(
        functools.partial(backward_kernel, HD**-0.5, seq),
        grid=(seq,),
        in_specs=[
            pl.BlockSpec((rows, PAIR), lambda i: (i, pair)),
            pl.BlockSpec((length, PAIR), lambda i: (0, pairs + pair)),
            pl.BlockSpec((length, PAIR), lambda i: (0, 2 * pairs + pair)),
        ]
        + [pl.BlockSpec((rows, PAIR), lambda i: (0, pair))] * seq
        + [row, pl.BlockSpec((rows, 2), lambda i: (i, 0))],
        out_specs=[pl.BlockSpec((rows, 3 * PAIR), lambda i: (0, 0))] * seq,
        out_shape=[like((rows, 3 * PAIR), BF16)] * seq,
        scratch_shapes=[pltpu.VMEM((PAIR, length), F32)] * 2 + [pltpu.VMEM((rows, PAIR), BF16)],
        compiler_params=params(32),
        cost_estimate=cost(
            40 * length * length * PAIR, 20 * length * PAIR, 2 * length * length
        ),
        name="attention_backward",
    )(qkv, qkv, qkv, *placed(*grads, exact, lse))


def block_of(where_ref, j, seq):
    return lax.rem(where_ref[1] + (seq - j), seq)


def hidden_kernel(seq, pairs, where_ref, *refs):
    count = seq * pairs
    mixed_refs, w_ref = refs[:count], refs[count]
    (x_ref, bout_ref, gain_ref, shift_ref, bfc1_ref, attended_ref, middle_ref, second_ref,
     activ_ref, slope_ref, att_sc, wout_sc, wfc1_sc, mixed_sem, wout_sem, wfc1_sem) = refs[count + 1 :]
    step = pl.program_id(0)
    width = x_ref.shape[1]

    @pl.when(step == 0)
    def _():
        out_copies = block_copies(w_ref, 0, wout_sc, wout_sem)
        for j in range(seq):
            for p in range(pairs):
                place = (block_of(where_ref, j, seq) * pairs + p) * PAIR
                out_copies.append(
                    pltpu.make_async_copy(
                        mixed_refs[j * pairs + p],
                        att_sc.at[:, pl.ds(pl.multiple_of(place, PAIR), PAIR)],
                        mixed_sem.at[j * pairs + p],
                    )
                )
        fc1_copies = block_copies(w_ref, width, wfc1_sc, wfc1_sem)
        for copy in out_copies + fc1_copies:
            copy.start()
        for copy in out_copies:
            copy.wait()
        attended = att_sc[...]
        attended_ref[...] = attended
        middle = x_ref[...].astype(F32) + (dot(attended, wout_sc[...]) + bout_ref[...])
        middle_ref[...] = middle
        hat, _ = standard(middle)
        second_ref[...] = (hat * gain_ref[...] + shift_ref[...]).astype(BF16)
        for copy in fc1_copies:
            copy.wait()

    block = bfc1_ref.shape[1]
    start = pl.multiple_of(step * block, block)
    hidden = dot(second_ref[...], wfc1_sc[:, pl.ds(start, block)]) + bfc1_ref[...]
    cdf = 0.5 * (1.0 + lax.erf(hidden * (0.5**0.5)))
    activ_ref[...] = (hidden * cdf).astype(BF16)
    slope_ref[...] = cdf + hidden * jnp.exp(-0.5 * hidden * hidden) * ((2.0 * math.pi) ** -0.5)


def hidden_layer(where, seq, mixed, weights, x, b_out, gain, shift_by, b_fc1, block):
    local, width = x.shape
    high = b_fc1.shape[0]
    pairs = len(mixed) // seq
    fixed = lambda i: (0, 0)
    tall = pl.BlockSpec((local, width), fixed)
    vector = pl.BlockSpec((1, width), fixed)
    wide = pl.BlockSpec((local, block), lambda i: (0, i))
    return pl.pallas_call(
        functools.partial(hidden_kernel, seq, pairs),
        grid=(high // block,),
        in_specs=[SCALARS] + [ANY] * (len(mixed) + 1)
        + [tall, vector, vector, vector, pl.BlockSpec((1, block), lambda i: (0, i))],
        out_specs=[tall, tall, tall, wide, wide],
        out_shape=[
            like((local, width), BF16),
            like((local, width), F32),
            like((local, width), BF16),
            like((local, high), BF16),
            like((local, high), F32),
        ],
        scratch_shapes=[
            pltpu.VMEM((local, width), BF16),
            pltpu.VMEM((width, width), BF16),
            pltpu.VMEM((width, high), BF16),
            pltpu.SemaphoreType.DMA((len(mixed),)),
            pltpu.SemaphoreType.DMA((4,)),
            pltpu.SemaphoreType.DMA((4,)),
        ],
        compiler_params=params(40),
        cost_estimate=cost(2 * local * width * (width + high), 8 * local * high, local * high),
        name="hidden_layer",
    )(where, *placed(*mixed, weights, x), b_out[None], gain[None], shift_by[None], b_fc1[None])


def output_kernel(blocks, where_ref, present_ref, w_ref, activ_ref, slope_ref, middle_ref, cot_ref,
                  bfc2_ref, out_ref, ghid_ref, sum_ref, final_sc, glow_sc, w_sc, w_sem):
    step = pl.program_id(0)
    present = present_ref[0]
    copies = block_copies(w_ref, 0, w_sc, w_sem)

    @pl.when(step == 0)
    def _():
        for copy in copies:
            copy.start()
        glow_sc[...] = (cot_ref[...].astype(F32) * present).astype(BF16)
        final_sc[...] = middle_ref[...] + bfc2_ref[...]

    for i in range(blocks):

        @pl.when(step == i)
        def _(i=i):
            copies[i].wait()

    block = activ_ref.shape[1]
    below = w_sc[pl.ds(pl.multiple_of(step * block, block), block), :]
    final_sc[...] += dot(activ_ref[...], below)
    grad_hidden = (dot(glow_sc[...], below, NT) * slope_ref[...]).astype(BF16)
    ghid_ref[...] = grad_hidden
    sum_ref[...] = jnp.sum(grad_hidden.astype(F32), 0, keepdims=True)

    @pl.when(step == blocks - 1)
    def _():
        out_ref[...] = (final_sc[...] * present).astype(BF16)


def output_layer(where, present, weights, activ, slope, middle, cot, b_fc2):
    local, width = middle.shape
    high = activ.shape[1]
    blocks = 8
    fixed = lambda i: (0, 0)
    tall = pl.BlockSpec((local, width), fixed)
    wide = pl.BlockSpec((local, high // blocks), lambda i: (0, i))
    return pl.pallas_call(
        functools.partial(output_kernel, blocks),
        grid=(blocks,),
        in_specs=[SCALARS, SCALARS, ANY, wide, wide, tall, tall, pl.BlockSpec((1, width), fixed)],
        out_specs=[tall, wide, pl.BlockSpec((1, high // blocks), lambda i: (0, i))],
        out_shape=[like((local, width), BF16), like((local, high), BF16), like((1, high), F32)],
        scratch_shapes=[
            pltpu.VMEM((local, width), F32),
            pltpu.VMEM((local, width), BF16),
            pltpu.VMEM((high, width), BF16),
            pltpu.SemaphoreType.DMA((blocks,)),
        ],
        compiler_params=params(40),
        cost_estimate=cost(4 * local * width * high, 12 * local * high),
        name="output_layer",
    )(where, present, *placed(weights, activ, slope, middle, cot), b_fc2[None])


def middle_kernel(seq, blocks, where_ref, present_ref, w_ref, ghid_ref, middle_ref, cot_ref,
                  gain_ref, gmid_ref, gbranch_ref, *refs):
    gmixed_refs, (sums_ref, gsecond_sc, wout_sc, wfc1_sc, wout_sem, wfc1_sem) = refs[:seq], refs[seq:]
    step = pl.program_id(0)
    width = middle_ref.shape[1]
    present = present_ref[0]
    upper = block_copies(w_ref, width, wfc1_sc, wfc1_sem)
    outer = block_copies(w_ref, 0, wout_sc, wout_sem)

    @pl.when(step == 0)
    def _():
        for copy in upper + outer:
            copy.start()
        gsecond_sc[...] = jnp.zeros_like(gsecond_sc)
        for copy in upper:
            copy.wait()

    block = ghid_ref.shape[1]
    start = pl.multiple_of(step * block, block)
    gsecond_sc[...] += dot(ghid_ref[...], wfc1_sc[:, pl.ds(start, block)], NT)

    @pl.when(step == blocks - 1)
    def _():
        for copy in outer:
            copy.wait()
        hat, inverse = standard(middle_ref[...])
        grad_second = gsecond_sc[...]
        grad_rows = cot_ref[...].astype(F32) * present
        grad_middle = grad_rows + norm_grad(grad_second, hat, inverse, gain_ref[...])
        gmid_ref[...] = grad_middle
        grad_branch = grad_middle.astype(BF16)
        gbranch_ref[...] = grad_branch
        sums_ref[...] = jnp.concatenate(
            [
                jnp.sum(grad_branch.astype(F32), 0, keepdims=True),
                jnp.sum(grad_second * hat, 0, keepdims=True),
                jnp.sum(grad_second, 0, keepdims=True),
                jnp.sum(grad_rows, 0, keepdims=True),
            ],
            0,
        )
        own = width // seq
        for j in range(seq):
            rows = pl.multiple_of(block_of(where_ref, j, seq) * own, own)
            gmixed_refs[j][...] = dot(grad_branch, wout_sc[pl.ds(rows, own), :], NT).astype(BF16)


def middle_layer(where, present, seq, weights, grad_hidden, middle, cot, gain):
    local, width = middle.shape
    high = grad_hidden.shape[1]
    blocks = 4
    fixed = lambda i: (0, 0)
    tall = pl.BlockSpec((local, width), fixed)
    own = width // seq
    return pl.pallas_call(
        functools.partial(middle_kernel, seq, blocks),
        grid=(blocks,),
        in_specs=[
            SCALARS,
            SCALARS,
            ANY,
            pl.BlockSpec((local, high // blocks), lambda i: (0, i)),
            tall,
            tall,
            pl.BlockSpec((1, width), fixed),
        ],
        out_specs=[tall, tall]
        + [pl.BlockSpec((local, own), fixed)] * seq
        + [pl.BlockSpec((4, width), fixed)],
        out_shape=[like((local, width), F32), like((local, width), BF16)]
        + [like((local, own), BF16)] * seq
        + [like((4, width), F32)],
        scratch_shapes=[
            pltpu.VMEM((local, width), F32),
            pltpu.VMEM((width, width), BF16),
            pltpu.VMEM((width, high), BF16),
            pltpu.SemaphoreType.DMA((4,)),
            pltpu.SemaphoreType.DMA((4,)),
        ],
        compiler_params=params(40),
        cost_estimate=cost(2 * local * width * (width + high), 12 * local * high),
        name="middle_layer",
    )(where, present, *placed(weights, grad_hidden, middle, cot), gain[None])


def last_kernel(seq, pairs, where_ref, *refs):
    count = seq * pairs
    grad_refs, w_ref = refs[:count], refs[count]
    x_ref, gmid_ref, gain_ref, out_ref, sums_ref, grad_sc, w_sc, grad_sem, w_sem = refs[count + 1 :]
    width = x_ref.shape[1]
    copies = block_copies(w_ref, 0, w_sc, w_sem)
    for j in range(seq):
        for p in range(pairs):
            place = (block_of(where_ref, j, seq) * pairs + p) * PAIR
            for t in range(3):
                copies.append(
                    pltpu.make_async_copy(
                        grad_refs[j * pairs + p].at[:, pl.ds(t * PAIR, PAIR)],
                        grad_sc.at[:, pl.ds(pl.multiple_of(t * width + place, PAIR), PAIR)],
                        grad_sem.at[(j * pairs + p) * 3 + t],
                    )
                )
    for copy in copies:
        copy.start()
    hat, inverse = standard(x_ref[...].astype(F32))
    for copy in copies:
        copy.wait()
    grad_first = dot(grad_sc[...], w_sc[...], NT)
    out_ref[...] = gmid_ref[...] + norm_grad(grad_first, hat, inverse, gain_ref[...])
    sums_ref[...] = jnp.concatenate(
        [jnp.sum(grad_first * hat, 0, keepdims=True), jnp.sum(grad_first, 0, keepdims=True)], 0
    )


def last_layer(where, seq, grads, weights, x, grad_middle, gain):
    local, width = x.shape
    pairs = len(grads) // seq
    whole = pl.BlockSpec(memory_space=pltpu.VMEM)
    return pl.pallas_call(
        functools.partial(last_kernel, seq, pairs),
        in_specs=[SCALARS] + [ANY] * (len(grads) + 1) + [whole] * 3,
        out_specs=[whole, whole],
        out_shape=[like((local, width), F32), like((2, width), F32)],
        scratch_shapes=[
            pltpu.VMEM((local, 3 * width), BF16),
            pltpu.VMEM((width, 3 * width), BF16),
            pltpu.SemaphoreType.DMA((3 * len(grads),)),
            pltpu.SemaphoreType.DMA((4,)),
        ],
        compiler_params=params(56),
        cost_estimate=cost(6 * local * width * width, 6 * width * width),
        name="last_layer",
    )(where, *placed(*grads, weights, x, grad_middle), gain[None])


def product(sides, refs):
    parts = []
    for count in sides:
        left, right_refs, refs = refs[0][...], refs[1 : 1 + count], refs[1 + count :]
        rows = right_refs[0].shape[0]
        groups = left.shape[0] // rows
        total = None
        for g in range(groups):
            blocks = [r[...] for r in right_refs[g::groups]]
            right = blocks[0] if len(blocks) == 1 else jnp.concatenate(blocks, 1)
            term = dot(left[g * rows : (g + 1) * rows], right, TN)
            total = term if total is None else total + term
        parts.append(total)
    return parts[0] if len(parts) == 1 else jnp.concatenate(parts, 1)


def away_kernel(sides, where_ref, *refs):
    refs[-1][0] = product(sides, refs[:-1]).astype(BF16)


def kept_kernel(sides, where_ref, *refs):
    refs, (arrived_ref, far1, keep1, far2, keep2) = refs[:-5], refs[-5:]
    step = pl.program_id(0)
    total = (product(sides, refs) + arrived_ref[0].astype(F32)).astype(BF16)
    half = total.shape[1] // 2

    @pl.when(step % 2 == 1)
    def _():
        far1[0] = total[:, :half]

    @pl.when(step % 2 == 0)
    def _():
        keep1[0] = total[:, :half]

    @pl.when(step >= 2)
    def _():
        far2[0] = total[:, half:]

    @pl.when(step < 2)
    def _():
        keep2[0] = total[:, half:]


def weight_shape(job):
    columns = [sum(r.shape[1] for r in rights) * rights[0].shape[0] // left.shape[0]
               for left, rights in job]
    return job[0][0].shape[1] // 8, sum(columns)


def weight_call(where, job, kernel, odd, more, out_specs, out_shape, name):
    rest, columns = weight_shape(job)
    specs, args = [], []
    for left, rights in job:
        specs.append(
            pl.BlockSpec(
                (left.shape[0], rest), lambda i, w: (0, jnp.bitwise_xor(w[0], 2 * i + odd))
            )
        )
        specs += [pl.BlockSpec(r.shape, lambda i, w: (0, 0)) for r in rights]
        args += [left, *rights]
    return pl.pallas_call(
        functools.partial(kernel, [len(rights) for _, rights in job]),
        grid_spec=pltpu.PrefetchScalarGridSpec(
            num_scalar_prefetch=1,
            grid=(4,),
            in_specs=specs
            + [pl.BlockSpec((1, rest, columns), lambda i, w: (i, 0, 0)) for _ in more],
            out_specs=out_specs,
        ),
        out_shape=out_shape,
        compiler_params=params(48),
        cost_estimate=cost(job[0][0].shape[0] * 8 * rest * columns, 8 * rest * columns),
        name=name,
    )(where, *placed(*args, *more))


def weight_away(where, job):
    rest, columns = weight_shape(job)
    return weight_call(
        where,
        job,
        away_kernel,
        1,
        [],
        pl.BlockSpec((1, rest, columns), lambda i, w: (i, 0, 0)),
        like((4, rest, columns), BF16),
        "weight_away",
    )


def weight_kept(where, job, arrived, ahead):
    rest, columns = weight_shape(job)
    two = like((2, rest, columns // 2), BF16)

    def spec(which):
        return pl.BlockSpec((1, rest, columns // 2), lambda i, w: (which(i), 0, 0))

    far1, keep1, far2, keep2 = weight_call(
        where,
        job,
        kept_kernel,
        0,
        [arrived],
        [
            spec(lambda i: i // 2),
            spec(lambda i: i // 2),
            spec(lambda i: jnp.maximum(i - 2, 0)),
            spec(lambda i: jnp.minimum(i, 1)),
        ],
        [two] * 4,
        "weight_kept",
    )
    if ahead:
        far1, far2 = after((far1, far2), ahead)
    return (keep1, flip(far1, 1, 8)), (keep2, flip(far2, 2, 8))


def second_kernel(keep1_ref, came1_ref, keep2_ref, came2_ref, *out_refs):
    far1, stay1, far2, stay2 = out_refs
    for keep_ref, came_ref, far, stay in (
        (keep1_ref, came1_ref, far1, stay1),
        (keep2_ref, came2_ref, far2, stay2),
    ):
        total = (keep_ref[...].astype(F32) + came_ref[...].astype(F32)).astype(BF16)
        stay[...] = total[0]
        far[...] = total[1]


def second_sums(first, before, ahead):
    (keep1, came1), (keep2, came2) = first
    keep1 = after(keep1, before)
    _, rest, half = keep1.shape
    rows = rest // 4
    spec = pl.BlockSpec((2, rows, half), lambda i: (0, i, 0))
    out = pl.BlockSpec((rows, half), lambda i: (i, 0))
    far1, stay1, far2, stay2 = pl.pallas_call(
        second_kernel,
        grid=(4,),
        in_specs=[spec] * 4,
        out_specs=[out] * 4,
        out_shape=[like((rest, half), BF16)] * 4,
        compiler_params=params(32),
        cost_estimate=cost(4 * rest * half, 24 * rest * half),
        name="second_sums",
    )(*placed(keep1, came1, keep2, came2))
    far1, far2 = after((far1, far2), ahead)
    return (stay1, flip(far1, 2, 8)), (stay2, flip(far2, 1, 8))


def spread_kernel(seq, where_ref, *refs):
    ins, outs = refs[:-seq], refs[-seq:]
    both = jnp.concatenate(
        [a[...].astype(F32) + b[...].astype(F32) for a, b in zip(ins[0::2], ins[1::2])], 1
    )
    for j, out_ref in enumerate(outs):

        @pl.when(pl.program_id(0) == j)
        def _(out_ref=out_ref):
            out_ref[...] = both.astype(out_ref.dtype)


def seq_spread(where, seconds, seq):
    arrays = [array for second in seconds for part in second for array in part]
    rest = arrays[0].shape[0]
    rows = rest // seq
    columns = sum(a.shape[1] for a in arrays[::2])
    blocks = [
        pl.BlockSpec((rows, a.shape[1]), lambda i, w: (lax.rem(w[1] + i, seq), 0)) for a in arrays
    ]
    out = pl.BlockSpec((rows, columns), lambda i, w: (0, 0))
    return pl.pallas_call(
        functools.partial(spread_kernel, seq),
        grid_spec=pltpu.PrefetchScalarGridSpec(
            num_scalar_prefetch=1, grid=(seq,), in_specs=blocks, out_specs=[out] * seq
        ),
        out_shape=[like((rows, columns), F32)] + [like((rows, columns), BF16)] * (seq - 1),
        compiler_params=params(32),
        cost_estimate=cost(rest * columns, 8 * rest * columns),
        name="seq_spread",
    )(where, *placed(*arrays))


def plain_sums(job, seq):
    blocks = []
    for left, rights in job:
        groups = left.shape[0] // rights[0].shape[0]
        right = jnp.concatenate([jnp.concatenate(rights[g::groups], 1) for g in range(groups)], 0)
        product = dot(left, right, TN)
        blocks.append(lax.psum_scatter(product, "fsdp", scatter_dimension=0, tiled=True))
    me = lax.axis_index("seq")
    parts = jnp.concatenate(blocks, 1)
    parts = parts.reshape(seq, parts.shape[0] // seq, parts.shape[1])
    chunks = [lax.dynamic_index_in_dim(parts, (me + j) % seq, 0, False) for j in range(seq)]
    return [chunks[0]] + [c.astype(BF16) for c in chunks[1:]]


def sum_vectors(vectors, fsdp, seq):
    me = lax.axis_index("fsdp")
    bits = fsdp.bit_length() - 1
    sizes = [v.shape[0] // (fsdp * seq) for v in vectors]
    block = jnp.concatenate([v.reshape(fsdp, seq, -1) for v in vectors], 2)
    block = block.reshape((2,) * bits + (seq, sum(sizes)))
    for bit in range(bits):
        axis = bits - 1 - bit
        mine = (me >> bit) & 1
        away = lax.dynamic_index_in_dim(block, 1 - mine, axis, False)
        block = lax.dynamic_index_in_dim(block, mine, axis, False) + flip(away, bit, fsdp)
    return block, sizes


def split_vectors(block, sizes, seq):
    place = lax.axis_index("seq")
    total = lax.dynamic_index_in_dim(block, place, 0, False)
    for by in range(1, seq):
        away = lax.dynamic_index_in_dim(block, (place + by) % seq, 0, False)
        total = total + shift(away, by, seq)
    return jnp.split(total, [sum(sizes[: i + 1]) for i in range(len(sizes) - 1)])


def after(value, *others):
    return lax.optimization_barrier((value, others))[0]


def spread_pairs(parts, seq):
    arrived = []
    for blocks in parts:
        if arrived:
            blocks = after(blocks, arrived[-1][1:])
        arrived.append([blocks[0]] + [shift(blocks[j], j, seq) for j in range(1, seq)])
    return [pair[j] for j in range(seq) for pair in arrived]


def on_device(
    fsdp,
    seq,
    inputs,
    clip_mask,
    ln1_gain,
    ln1_bias,
    w_query,
    b_query,
    w_key,
    w_value,
    b_value,
    w_out,
    b_out,
    ln2_gain,
    ln2_bias,
    w_fc1,
    b_fc1,
    w_fc2,
    b_fc2,
    cotangent,
):
    clips, local, width = inputs.shape
    assert clips == 1
    me = lax.axis_index("seq")
    where = jnp.stack([lax.axis_index("fsdp"), me]).astype(jnp.int32)
    present = clip_mask.astype(F32)
    own = width // seq
    pairs = own // PAIR
    table = piece_table(fsdp)
    x, cot = inputs[0], cotangent[0]
    grad_low = (cot.astype(F32) * present).astype(BF16)

    def columns(array, axis):
        return lax.dynamic_slice_in_dim(array, me * own, own, axis)

    shard_heads = jnp.concatenate([columns(w, 1) for w in (w_query, w_key, w_value)], 1)
    near_heads = gather_near(shard_heads, fsdp)
    down, up = [x], [x]
    for hop in range(1, seq):
        if hop == 2:
            down[-1], up[-1], near_heads = after((down[-1], up[-1], near_heads))
            w_heads = gather_pieces(shard_heads, near_heads, fsdp)
        if hop == 3:
            down[-1], up[-1] = after((down[-1], up[-1]), w_heads)
        down.append(lax.ppermute(down[-1], "seq", [(i, i - 1) for i in range(1, seq + 1 - hop)]))
        up.append(lax.ppermute(up[-1], "seq", [(i, i + 1) for i in range(hop - 1, seq - 1)]))
    b_heads = jnp.concatenate([columns(b_query, 0), jnp.zeros((own,), F32), columns(b_value, 0)])
    one = lax.all_gather(jnp.concatenate([w_out, w_fc1], 1), "fsdp", axis=0, tiled=True)
    two = lax.all_gather(after(w_fc2, down[1], up[1]), "fsdp", axis=0, tiled=True)
    shard_three = jnp.concatenate([w_query, w_key, w_value], 1)
    three = lax.all_gather(after(shard_three, down[2], up[2]), "fsdp", axis=0, tiled=True)

    norms = (ln1_gain, ln1_bias, b_heads)
    early = [x] + down[1:-1] + [x] + up[1:-1] + [x]
    first_in, qkv = project(where, seq, table, early, w_heads, *norms)
    first_in, qkv = project(
        where, seq, table, [x] + down[1:] + up[1:], w_heads, *norms, (first_in, qkv)
    )
    forward = [attention_forward(qkv, 0, pairs, seq)]
    for p in range(1, pairs):
        forward.append(attention_forward(qkv, p, pairs, seq))
    mixed = spread_pairs([part[:seq] for part in forward], seq)
    attended, middle, second_in, activ, slope = hidden_layer(
        where, seq, mixed, one, x, b_out, ln2_gain, ln2_bias, b_fc1, 512
    )
    parts = {}

    def away(name, job, before):
        if fsdp == 8:
            parts[name] = weight_away(after(where, before), job)
        else:
            parts[name] = plain_sums(job, seq)
        return parts[name]

    def kept(name, job, before, first=(), ahead=()):
        if fsdp != 8:
            return ()
        arrived = flip(after(parts[name], first), 0, 8)
        parts[name] = weight_kept(after(where, before), job, arrived, ahead)
        return parts[name][0][0]

    def second(name, before, ahead=()):
        if fsdp != 8:
            return ()
        parts[name] = second_sums(parts[name], before, ahead)
        return parts[name][0][0]

    def chunks(names, before):
        if fsdp == 8:
            return seq_spread(after(where, before), [parts[n] for n in names], seq)
        return [jnp.concatenate(blocks, 1) for blocks in zip(*[parts[n] for n in names])]

    def came(name):
        return (parts[name][0][1], parts[name][1][1]) if fsdp == 8 else ()

    def send(blocks, ahead):
        if ahead:
            blocks = after(blocks, ahead)
        return [blocks[0]] + [shift(blocks[j], j, seq) for j in range(1, seq)]

    low = [(activ, [grad_low])]
    step = away("low", low, ())
    output, grad_hidden, sum_fc1 = output_layer(
        after(where, step), present, two, activ, slope, middle, cot, b_fc2
    )
    step = kept("low", low, grad_hidden)
    high = [(second_in, [grad_hidden])]
    step = away("high", high, step)
    results = middle_layer(
        after(where, step), present, seq, one, grad_hidden, middle, cot, ln2_gain
    )
    grad_middle, grad_branch = results[:2]
    grad_mixed, sums2 = results[2 : 2 + seq], results[2 + seq]
    grads = [grad_mixed[0]] + [shift(grad_mixed[j], -j, seq) for j in range(1, seq)]
    low_came = came("low")
    step = second("low", (grad_branch, three))
    step = kept("high", high, step, (low_came, grad_branch), grads[1:])
    low_rows = chunks(["low"], step)
    step = low_rows[1]
    low_rows = send(low_rows, grads[1:])
    back, home = [], []
    for p in range(pairs):
        exact, lse = forward[p][seq:]
        back.append(attention_backward(qkv, grads, exact, after(lse, step), p, pairs, seq))
        home.append(send(back[-1], () if home else low_rows[1:]))
        step = back[-1][0]
    total_low = sum(rows.astype(F32) for rows in low_rows)
    step = second("high", step, home[0][1:])
    late = [(first_in, [b for pair in back for b in pair]), (attended, [grad_branch])]
    step = away("late", late, step)
    step = kept("late", late, step, home[0][1:], home[1][1:])
    high_rows = chunks(["high"], step)
    step = high_rows[1]
    high_rows = send(high_rows, home[1][1:])
    step = second("late", step)
    grad_inputs, sums1 = last_layer(
        after(where, step),
        seq,
        [pair[j] for j in range(seq) for pair in home],
        three,
        x,
        grad_middle,
        ln1_gain,
    )
    late_rows = chunks(["late"], sums1)

    def spread(which):
        vector = jnp.concatenate(
            [
                sum(
                    jnp.sum(block[:, which * PAIR : (which + 1) * PAIR].astype(F32), 0)
                    for block in back[p]
                )
                for p in range(pairs)
            ]
        )
        return lax.dynamic_update_slice(jnp.zeros((width,), F32), vector, (me * own,))

    sums1 = after(sums1, high_rows[1:], late_rows[1])
    block, sizes = sum_vectors(
        [sums1[0], sums1[1], spread(0), spread(2)] + [sums2[i] for i in range(4)] + [sum_fc1[0]],
        fsdp,
        seq,
    )
    split = 3 * own
    sent = send(late_rows, high_rows[1:])
    rows = after(sent, block)
    total_out = sum(part[:, split:].astype(F32) for part in rows)
    total_high = sum(part.astype(F32) for part in high_rows)
    heads = [part[:, :split].astype(F32) for part in rows[::-1]]
    grad_heads = lax.dynamic_slice_in_dim(jnp.stack(heads + heads), (seq - 1 - me) % seq, seq, 0)
    strip = grad_heads.shape[1]
    grad_heads = grad_heads.reshape(seq, strip, pairs, 3, PAIR).transpose(3, 1, 0, 2, 4)
    grad_heads = grad_heads.reshape(3, strip, width)

    sums = split_vectors(after(block, sent[1:]), sizes, seq)
    return (
        output[None],
        grad_inputs[None],
        sums[0],
        sums[1],
        grad_heads[0],
        sums[2],
        grad_heads[1],
        grad_heads[2],
        sums[3],
        total_out,
        sums[4],
        sums[5],
        sums[6],
        total_high,
        sums[8],
        total_low,
        sums[7],
    )


def solution(mesh):
    rows, both = P("fsdp", None), P(("fsdp", "seq"))
    tokens = P("fsdp", "seq", None)
    matrix = P(("fsdp", "seq"), None)
    return jax.shard_map(
        functools.partial(on_device, mesh.shape["fsdp"], mesh.shape["seq"]),
        mesh=mesh,
        in_specs=(
            tokens,
            P("fsdp"),
            P(),
            P(),
            rows,
            P(),
            rows,
            rows,
            P(),
            rows,
            P(),
            P(),
            P(),
            rows,
            P(),
            rows,
            P(),
            tokens,
        ),
        out_specs=(
            tokens,
            tokens,
            both,
            both,
            matrix,
            both,
            matrix,
            matrix,
            both,
            matrix,
            both,
            both,
            both,
            matrix,
            both,
            matrix,
            both,
        ),
        check_vma=False,
    )
```

```python
import functools
import math

import jax
import jax.numpy as jnp
from jax import lax
from jax.experimental import pallas as pl
from jax.experimental.pallas import tpu as pltpu
from jax.sharding import PartitionSpec as P

HD = 64
PAIR = 2 * HD
EPSILON = 1e-06
LOG2E = math.log2(math.e)
BF16 = jnp.bfloat16
F32 = jnp.float32
NT = (((1,), (1,)), ((), ()))
NN = (((1,), (0,)), ((), ()))
TN = (((0,), (0,)), ((), ()))
ANY = pl.BlockSpec(memory_space=pl.ANY)
SCALARS = pl.BlockSpec(memory_space=pltpu.SMEM)


def dot(a, b, dims=NN):
    return lax.dot_general(a, b, dims, preferred_element_type=F32)


def like(shape, dtype):
    return pltpu.HBM(shape, dtype)


def placed(*arrays):
    return [pltpu.with_memory_space_constraint(a, pltpu.HBM) for a in arrays]


def standard(rows):
    center = rows - jnp.mean(rows, -1, keepdims=True)
    inverse = lax.rsqrt(jnp.mean(center * center, -1, keepdims=True) + EPSILON)
    return center * inverse, inverse


def norm_grad(grad, normed, inverse, gain):
    scaled = grad * gain
    inner = (
        scaled
        - jnp.mean(scaled, -1, keepdims=True)
        - normed * jnp.mean(scaled * normed, -1, keepdims=True)
    )
    return inner * inverse


def params(mib):
    return pltpu.CompilerParams(vmem_limit_bytes=mib << 20)


def cost(flops, moved, special=0):
    return pl.CostEstimate(flops=flops // 64, bytes_accessed=moved // 64, transcendentals=0)


def piece_table(size):
    if size != 8:
        return [(None, None)]
    return [(far + near, half) for near in (0, 1) for far, half in
            ((0, None), (2, None), (4, None), (6, 0), (6, 1))]


def flip(array, bit, size):
    return lax.ppermute(array, "fsdp", [(i, i ^ (1 << bit)) for i in range(size)])


def shift(array, by, size):
    return lax.ppermute(array, "seq", [(i, (i + by) % size) for i in range(size)])


def gather_near(shard, size):
    return (flip(shard, 1, size), flip(shard, 2, size)) if size == 8 else ()


def gather_pieces(shard, near, size):
    if size != 8:
        return [lax.all_gather(shard, "fsdp", axis=0, tiled=True)]
    half = shard.shape[0] // 2
    one, two = near
    top, low = flip(one[:half], 2, size), flip(two[half:], 1, size)
    pieces = [shard, one, two, top, low]
    return pieces + [flip(piece, 0, size) for piece in pieces]


def piece_copies(table, me, refs, first, target, sems):
    width = target.shape[1]
    copies = []
    for i, ((rel, half), ref) in enumerate(zip(table, refs)):
        count = ref.shape[0]
        if rel is None:
            start = 0
        elif half is None:
            start = jnp.bitwise_xor(me, rel) * count
        else:
            start = jnp.bitwise_xor(me, rel) * (2 * count) + half * count
        source = ref.at[:, pl.ds(first, width)]
        place = target.at[pl.ds(start, count), :]
        copies.append(pltpu.make_async_copy(source, place, sems.at[i]))
    return copies


def block_copies(ref, first, target, sems):
    count = sems.shape[0]
    rows, width = target.shape[0] // count, target.shape[1]
    return [
        pltpu.make_async_copy(
            ref.at[pl.ds(i * rows, rows), pl.ds(first, width)],
            target.at[pl.ds(i * rows, rows), :],
            sems.at[i],
        )
        for i in range(count)
    ]


def last_block(me, seq):
    return jnp.where(2 * me < seq, seq - 1 - me, seq - me)


def project_kernel(seq, table, rest, where_ref, *refs):
    own_ref, down_refs, up_refs = refs[0], refs[1:seq], refs[seq : 2 * seq - 1]
    refs = refs[2 * seq - 1 :]
    w_refs, refs = refs[: len(table)], refs[len(table) :]
    gain_ref, shift_ref, bias_ref, first_ref, qkv_ref, x_sc, w_sc, x_sem, w_sem = (
        refs[:3] + refs[3 + 2 * rest :]
    )
    step = pl.program_id(0)
    me = where_ref[1]
    late = last_block(me, seq)
    copies = piece_copies(table, where_ref[0], w_refs, 0, w_sc, w_sem)

    @pl.when(step == 0)
    def _():
        for copy in copies:
            copy.start()
        if not rest:
            pltpu.make_async_copy(own_ref, x_sc.at[0], x_sem.at[0]).start()
        for j in range(1, seq):
            wanted = (late == j) if rest else (late != j)
            inside = me + j < seq
            if rest or j < seq - 1:

                @pl.when(jnp.logical_and(wanted, inside))
                def _(j=j):
                    pltpu.make_async_copy(down_refs[j - 1], x_sc.at[j], x_sem.at[j]).start()

            if rest or j > 1:

                @pl.when(jnp.logical_and(wanted, jnp.logical_not(inside)))
                def _(j=j):
                    pltpu.make_async_copy(up_refs[seq - j - 1], x_sc.at[j], x_sem.at[j]).start()

        for copy in copies:
            copy.wait()

    block = late if rest else step + jnp.where(step >= late, 1, 0)
    pltpu.make_async_copy(own_ref, x_sc.at[block], x_sem.at[block]).wait()
    hat, _ = standard(x_sc[block].astype(F32))
    first = (hat * gain_ref[...] + shift_ref[...]).astype(BF16)
    first_ref[...] = first
    qkv_ref[...] = (dot(first, w_sc[...]) + bias_ref[...]).astype(BF16)


def project(where, seq, table, tokens, pieces, gain, shift_by, bias, before=None):
    local, width = tokens[0].shape
    columns = pieces[0].shape[1]
    rest = before is not None

    def fixed(i, w):
        return (0, 0)

    def turn(i, w):
        late = last_block(w[1], seq)
        return (late if rest else i + jnp.where(i >= late, 1, 0), 0)

    vector = pl.BlockSpec((1, width), fixed)
    count = len(tokens) + len(pieces) + 4
    return pl.pallas_call(
        functools.partial(project_kernel, seq, table, rest),
        grid_spec=pltpu.PrefetchScalarGridSpec(
            num_scalar_prefetch=1,
            grid=(1 if rest else seq - 1,),
            in_specs=[ANY] * (len(tokens) + len(pieces))
            + [vector, vector, pl.BlockSpec((1, columns), fixed)]
            + [ANY] * (2 * rest),
            out_specs=[pl.BlockSpec((local, width), turn), pl.BlockSpec((local, columns), turn)],
            scratch_shapes=[
                pltpu.VMEM((seq, local, width), BF16),
                pltpu.VMEM((width, columns), BF16),
                pltpu.SemaphoreType.DMA((seq,)),
                pltpu.SemaphoreType.DMA((len(table),)),
            ],
        ),
        out_shape=[
            like((seq * local, width), BF16),
            jax.ShapeDtypeStruct((seq * local, columns), BF16),
        ],
        input_output_aliases={count: 0, count + 1: 1} if rest else {},
        compiler_params=params(32),
        cost_estimate=cost(2 * seq * local * width * columns, 6 * seq * local * width),
        name="project",
    )(
        where,
        *placed(*tokens, *pieces),
        gain[None],
        shift_by[None],
        bias[None],
        *(before if rest else ()),
    )


def forward_kernel(scale, seq, q_ref, k_ref, v_ref, *refs):
    mixed_refs, (exact_ref, lse_ref, value_sc) = refs[:seq], refs[seq:]
    step = pl.program_id(0)

    @pl.when(step == 0)
    def _():
        value_sc[:, :PAIR] = v_ref[...]
        value_sc[:, PAIR:] = jnp.ones((value_sc.shape[0], PAIR), value_sc.dtype)

    query = q_ref[...]
    keys = k_ref[...]
    first = lax.broadcasted_iota(jnp.int32, query.shape, 1) < HD
    outs, sums = [], []
    for head in range(2):
        mine = first if head == 0 else jnp.logical_not(first)
        scores = dot(jnp.where(mine, query, jnp.zeros_like(query)), keys, NT)
        peak = jnp.max(scores, -1, keepdims=True)
        expo = jnp.exp2((scores - peak) * scale).astype(BF16)
        both = dot(expo, value_sc[...])
        total = both[:, PAIR:]
        outs.append(both[:, :PAIR] / total)
        sums.append(peak * scale + jnp.log2(total[:, :1]))
    exact = jnp.where(first, outs[0], outs[1])
    exact_ref[...] = exact
    lse_ref[...] = jnp.concatenate(sums, 1)
    for j in range(seq):

        @pl.when(step == j)
        def _(j=j):
            mixed_refs[j][...] = exact.astype(BF16)


def attention_forward(qkv, pair, pairs, seq):
    length = qkv.shape[0]
    rows = length // seq
    row = pl.BlockSpec((rows, PAIR), lambda i: (i, 0))
    return pl.pallas_call(
        functools.partial(forward_kernel, HD**-0.5 * LOG2E, seq),
        grid=(seq,),
        in_specs=[
            pl.BlockSpec((rows, PAIR), lambda i: (i, pair)),
            pl.BlockSpec((length, PAIR), lambda i: (0, pairs + pair)),
            pl.BlockSpec((length, PAIR), lambda i: (0, 2 * pairs + pair)),
        ],
        out_specs=[pl.BlockSpec((rows, PAIR), lambda i: (0, 0))] * seq
        + [row, pl.BlockSpec((rows, 2), lambda i: (i, 0))],
        out_shape=[like((rows, PAIR), BF16)] * seq
        + [like((length, PAIR), F32), like((length, 2), F32)],
        scratch_shapes=[pltpu.VMEM((length, 2 * PAIR), BF16)],
        compiler_params=params(32),
        cost_estimate=cost(
            16 * length * length * PAIR, 14 * length * PAIR, 2 * length * length
        ),
        name="attention_forward",
    )(qkv, qkv, qkv)


def backward_kernel(scale, seq, q_ref, k_ref, v_ref, *refs):
    grad_refs, (exact_ref, lse_ref), refs = refs[:seq], refs[seq : seq + 2], refs[seq + 2 :]
    out_refs, (dk_sc, dv_sc, grad_sc) = refs[:seq], refs[seq:]
    step = pl.program_id(0)

    @pl.when(step == 0)
    def _():
        dk_sc[...] = jnp.zeros_like(dk_sc)
        dv_sc[...] = jnp.zeros_like(dv_sc)

    for j in range(seq):

        @pl.when(step == j)
        def _(j=j):
            grad_sc[...] = grad_refs[j][...]

    query, keys, values, grad = q_ref[...], k_ref[...], v_ref[...], grad_sc[...]
    first = lax.broadcasted_iota(jnp.int32, query.shape, 1) < HD
    product = grad.astype(F32) * exact_ref[...]
    dqs = []
    for head in range(2):
        mine = first if head == 0 else jnp.logical_not(first)
        zero = jnp.zeros_like(query)
        q_one = jnp.where(mine, query, zero)
        g_one = jnp.where(mine, grad, zero)
        inner = jnp.sum(jnp.where(mine, product, 0.0), -1, keepdims=True)
        probs = jnp.exp2(dot(q_one, keys, NT) * (scale * LOG2E) - lse_ref[:, head : head + 1])
        grad_scores = (probs * (dot(g_one, values, NT) - inner)).astype(BF16)
        dqs.append(dot(grad_scores, keys))
        dv_sc[...] += dot(g_one, probs.astype(BF16), TN)
        dk_sc[...] += dot(q_one, grad_scores, TN)
    dq = (jnp.where(first, dqs[0], dqs[1]) * scale).astype(BF16)
    for j in range(seq):

        @pl.when(step == j)
        def _(j=j):
            out_refs[j][:, :PAIR] = dq

    @pl.when(step == pl.num_programs(0) - 1)
    def _():
        dk = (dk_sc[...] * scale).T.astype(BF16)
        dv = dv_sc[...].T.astype(BF16)
        rows = dk.shape[0] // seq
        for j in range(seq):
            out_refs[j][:, PAIR : 2 * PAIR] = dk[j * rows : (j + 1) * rows]
            out_refs[j][:, 2 * PAIR :] = dv[j * rows : (j + 1) * rows]


def attention_backward(qkv, grads, exact, lse, pair, pairs, seq):
    length = qkv.shape[0]
    rows = length // seq
    row = pl.BlockSpec((rows, PAIR), lambda i: (i, 0))
    return pl.pallas_call(
        functools.partial(backward_kernel, HD**-0.5, seq),
        grid=(seq,),
        in_specs=[
            pl.BlockSpec((rows, PAIR), lambda i: (i, pair)),
            pl.BlockSpec((length, PAIR), lambda i: (0, pairs + pair)),
            pl.BlockSpec((length, PAIR), lambda i: (0, 2 * pairs + pair)),
        ]
        + [pl.BlockSpec((rows, PAIR), lambda i: (0, pair))] * seq
        + [row, pl.BlockSpec((rows, 2), lambda i: (i, 0))],
        out_specs=[pl.BlockSpec((rows, 3 * PAIR), lambda i: (0, 0))] * seq,
        out_shape=[like((rows, 3 * PAIR), BF16)] * seq,
        scratch_shapes=[pltpu.VMEM((PAIR, length), F32)] * 2 + [pltpu.VMEM((rows, PAIR), BF16)],
        compiler_params=params(32),
        cost_estimate=cost(
            40 * length * length * PAIR, 20 * length * PAIR, 2 * length * length
        ),
        name="attention_backward",
    )(qkv, qkv, qkv, *placed(*grads, exact, lse))


def block_of(where_ref, j, seq):
    return lax.rem(where_ref[1] + (seq - j), seq)


def hidden_kernel(seq, pairs, where_ref, *refs):
    count = seq * pairs
    mixed_refs, w_ref = refs[:count], refs[count]
    (x_ref, bout_ref, gain_ref, shift_ref, bfc1_ref, attended_ref, middle_ref, second_ref,
     activ_ref, slope_ref, att_sc, wout_sc, wfc1_sc, mixed_sem, wout_sem, wfc1_sem) = refs[count + 1 :]
    step = pl.program_id(0)
    width = x_ref.shape[1]

    @pl.when(step == 0)
    def _():
        out_copies = block_copies(w_ref, 0, wout_sc, wout_sem)
        for j in range(seq):
            for p in range(pairs):
                place = (block_of(where_ref, j, seq) * pairs + p) * PAIR
                out_copies.append(
                    pltpu.make_async_copy(
                        mixed_refs[j * pairs + p],
                        att_sc.at[:, pl.ds(pl.multiple_of(place, PAIR), PAIR)],
                        mixed_sem.at[j * pairs + p],
                    )
                )
        fc1_copies = block_copies(w_ref, width, wfc1_sc, wfc1_sem)
        for copy in out_copies + fc1_copies:
            copy.start()
        for copy in out_copies:
            copy.wait()
        attended = att_sc[...]
        attended_ref[...] = attended
        middle = x_ref[...].astype(F32) + (dot(attended, wout_sc[...]) + bout_ref[...])
        middle_ref[...] = middle
        hat, _ = standard(middle)
        second_ref[...] = (hat * gain_ref[...] + shift_ref[...]).astype(BF16)
        for copy in fc1_copies:
            copy.wait()

    block = bfc1_ref.shape[1]
    start = pl.multiple_of(step * block, block)
    hidden = dot(second_ref[...], wfc1_sc[:, pl.ds(start, block)]) + bfc1_ref[...]
    cdf = 0.5 * (1.0 + lax.erf(hidden * (0.5**0.5)))
    activ_ref[...] = (hidden * cdf).astype(BF16)
    slope_ref[...] = cdf + hidden * jnp.exp(-0.5 * hidden * hidden) * ((2.0 * math.pi) ** -0.5)


def hidden_layer(where, seq, mixed, weights, x, b_out, gain, shift_by, b_fc1, block):
    local, width = x.shape
    high = b_fc1.shape[0]
    pairs = len(mixed) // seq
    fixed = lambda i: (0, 0)
    tall = pl.BlockSpec((local, width), fixed)
    vector = pl.BlockSpec((1, width), fixed)
    wide = pl.BlockSpec((local, block), lambda i: (0, i))
    return pl.pallas_call(
        functools.partial(hidden_kernel, seq, pairs),
        grid=(high // block,),
        in_specs=[SCALARS] + [ANY] * (len(mixed) + 1)
        + [tall, vector, vector, vector, pl.BlockSpec((1, block), lambda i: (0, i))],
        out_specs=[tall, tall, tall, wide, wide],
        out_shape=[
            like((local, width), BF16),
            like((local, width), F32),
            like((local, width), BF16),
            like((local, high), BF16),
            like((local, high), F32),
        ],
        scratch_shapes=[
            pltpu.VMEM((local, width), BF16),
            pltpu.VMEM((width, width), BF16),
            pltpu.VMEM((width, high), BF16),
            pltpu.SemaphoreType.DMA((len(mixed),)),
            pltpu.SemaphoreType.DMA((4,)),
            pltpu.SemaphoreType.DMA((4,)),
        ],
        compiler_params=params(40),
        cost_estimate=cost(2 * local * width * (width + high), 8 * local * high, local * high),
        name="hidden_layer",
    )(where, *placed(*mixed, weights, x), b_out[None], gain[None], shift_by[None], b_fc1[None])


def output_kernel(blocks, where_ref, present_ref, w_ref, activ_ref, slope_ref, middle_ref, cot_ref,
                  bfc2_ref, out_ref, ghid_ref, sum_ref, final_sc, glow_sc, w_sc, w_sem):
    step = pl.program_id(0)
    present = present_ref[0]
    copies = block_copies(w_ref, 0, w_sc, w_sem)

    @pl.when(step == 0)
    def _():
        for copy in copies:
            copy.start()
        glow_sc[...] = (cot_ref[...].astype(F32) * present).astype(BF16)
        final_sc[...] = middle_ref[...] + bfc2_ref[...]

    for i in range(blocks):

        @pl.when(step == i)
        def _(i=i):
            copies[i].wait()

    block = activ_ref.shape[1]
    below = w_sc[pl.ds(pl.multiple_of(step * block, block), block), :]
    final_sc[...] += dot(activ_ref[...], below)
    grad_hidden = (dot(glow_sc[...], below, NT) * slope_ref[...]).astype(BF16)
    ghid_ref[...] = grad_hidden
    sum_ref[...] = jnp.sum(grad_hidden.astype(F32), 0, keepdims=True)

    @pl.when(step == blocks - 1)
    def _():
        out_ref[...] = (final_sc[...] * present).astype(BF16)


def output_layer(where, present, weights, activ, slope, middle, cot, b_fc2):
    local, width = middle.shape
    high = activ.shape[1]
    blocks = 8
    fixed = lambda i: (0, 0)
    tall = pl.BlockSpec((local, width), fixed)
    wide = pl.BlockSpec((local, high // blocks), lambda i: (0, i))
    return pl.pallas_call(
        functools.partial(output_kernel, blocks),
        grid=(blocks,),
        in_specs=[SCALARS, SCALARS, ANY, wide, wide, tall, tall, pl.BlockSpec((1, width), fixed)],
        out_specs=[tall, wide, pl.BlockSpec((1, high // blocks), lambda i: (0, i))],
        out_shape=[like((local, width), BF16), like((local, high), BF16), like((1, high), F32)],
        scratch_shapes=[
            pltpu.VMEM((local, width), F32),
            pltpu.VMEM((local, width), BF16),
            pltpu.VMEM((high, width), BF16),
            pltpu.SemaphoreType.DMA((blocks,)),
        ],
        compiler_params=params(40),
        cost_estimate=cost(4 * local * width * high, 12 * local * high),
        name="output_layer",
    )(where, present, *placed(weights, activ, slope, middle, cot), b_fc2[None])


def middle_kernel(seq, blocks, where_ref, present_ref, w_ref, ghid_ref, middle_ref, cot_ref,
                  gain_ref, gmid_ref, gbranch_ref, *refs):
    gmixed_refs, (sums_ref, gsecond_sc, wout_sc, wfc1_sc, wout_sem, wfc1_sem) = refs[:seq], refs[seq:]
    step = pl.program_id(0)
    width = middle_ref.shape[1]
    present = present_ref[0]
    upper = block_copies(w_ref, width, wfc1_sc, wfc1_sem)
    outer = block_copies(w_ref, 0, wout_sc, wout_sem)

    @pl.when(step == 0)
    def _():
        for copy in upper + outer:
            copy.start()
        gsecond_sc[...] = jnp.zeros_like(gsecond_sc)
        for copy in upper:
            copy.wait()

    block = ghid_ref.shape[1]
    start = pl.multiple_of(step * block, block)
    gsecond_sc[...] += dot(ghid_ref[...], wfc1_sc[:, pl.ds(start, block)], NT)

    @pl.when(step == blocks - 1)
    def _():
        for copy in outer:
            copy.wait()
        hat, inverse = standard(middle_ref[...])
        grad_second = gsecond_sc[...]
        grad_rows = cot_ref[...].astype(F32) * present
        grad_middle = grad_rows + norm_grad(grad_second, hat, inverse, gain_ref[...])
        gmid_ref[...] = grad_middle
        grad_branch = grad_middle.astype(BF16)
        gbranch_ref[...] = grad_branch
        sums_ref[...] = jnp.concatenate(
            [
                jnp.sum(grad_branch.astype(F32), 0, keepdims=True),
                jnp.sum(grad_second * hat, 0, keepdims=True),
                jnp.sum(grad_second, 0, keepdims=True),
                jnp.sum(grad_rows, 0, keepdims=True),
            ],
            0,
        )
        own = width // seq
        for j in range(seq):
            rows = pl.multiple_of(block_of(where_ref, j, seq) * own, own)
            gmixed_refs[j][...] = dot(grad_branch, wout_sc[pl.ds(rows, own), :], NT).astype(BF16)


def middle_layer(where, present, seq, weights, grad_hidden, middle, cot, gain):
    local, width = middle.shape
    high = grad_hidden.shape[1]
    blocks = 4
    fixed = lambda i: (0, 0)
    tall = pl.BlockSpec((local, width), fixed)
    own = width // seq
    return pl.pallas_call(
        functools.partial(middle_kernel, seq, blocks),
        grid=(blocks,),
        in_specs=[
            SCALARS,
            SCALARS,
            ANY,
            pl.BlockSpec((local, high // blocks), lambda i: (0, i)),
            tall,
            tall,
            pl.BlockSpec((1, width), fixed),
        ],
        out_specs=[tall, tall]
        + [pl.BlockSpec((local, own), fixed)] * seq
        + [pl.BlockSpec((4, width), fixed)],
        out_shape=[like((local, width), F32), like((local, width), BF16)]
        + [like((local, own), BF16)] * seq
        + [like((4, width), F32)],
        scratch_shapes=[
            pltpu.VMEM((local, width), F32),
            pltpu.VMEM((width, width), BF16),
            pltpu.VMEM((width, high), BF16),
            pltpu.SemaphoreType.DMA((4,)),
            pltpu.SemaphoreType.DMA((4,)),
        ],
        compiler_params=params(40),
        cost_estimate=cost(2 * local * width * (width + high), 12 * local * high),
        name="middle_layer",
    )(where, present, *placed(weights, grad_hidden, middle, cot), gain[None])


def last_kernel(seq, pairs, where_ref, *refs):
    count = seq * pairs
    grad_refs, w_ref = refs[:count], refs[count]
    x_ref, gmid_ref, gain_ref, out_ref, sums_ref, grad_sc, w_sc, grad_sem, w_sem = refs[count + 1 :]
    width = x_ref.shape[1]
    copies = block_copies(w_ref, 0, w_sc, w_sem)
    for j in range(seq):
        for p in range(pairs):
            place = (block_of(where_ref, j, seq) * pairs + p) * PAIR
            for t in range(3):
                copies.append(
                    pltpu.make_async_copy(
                        grad_refs[j * pairs + p].at[:, pl.ds(t * PAIR, PAIR)],
                        grad_sc.at[:, pl.ds(pl.multiple_of(t * width + place, PAIR), PAIR)],
                        grad_sem.at[(j * pairs + p) * 3 + t],
                    )
                )
    for copy in copies:
        copy.start()
    hat, inverse = standard(x_ref[...].astype(F32))
    for copy in copies:
        copy.wait()
    grad_first = dot(grad_sc[...], w_sc[...], NT)
    out_ref[...] = gmid_ref[...] + norm_grad(grad_first, hat, inverse, gain_ref[...])
    sums_ref[...] = jnp.concatenate(
        [jnp.sum(grad_first * hat, 0, keepdims=True), jnp.sum(grad_first, 0, keepdims=True)], 0
    )


def last_layer(where, seq, grads, weights, x, grad_middle, gain):
    local, width = x.shape
    pairs = len(grads) // seq
    whole = pl.BlockSpec(memory_space=pltpu.VMEM)
    return pl.pallas_call(
        functools.partial(last_kernel, seq, pairs),
        in_specs=[SCALARS] + [ANY] * (len(grads) + 1) + [whole] * 3,
        out_specs=[whole, whole],
        out_shape=[like((local, width), F32), like((2, width), F32)],
        scratch_shapes=[
            pltpu.VMEM((local, 3 * width), BF16),
            pltpu.VMEM((width, 3 * width), BF16),
            pltpu.SemaphoreType.DMA((3 * len(grads),)),
            pltpu.SemaphoreType.DMA((4,)),
        ],
        compiler_params=params(56),
        cost_estimate=cost(6 * local * width * width, 6 * width * width),
        name="last_layer",
    )(where, *placed(*grads, weights, x, grad_middle), gain[None])


def product(sides, refs):
    parts = []
    for count in sides:
        left, right_refs, refs = refs[0][...], refs[1 : 1 + count], refs[1 + count :]
        rows = right_refs[0].shape[0]
        groups = left.shape[0] // rows
        total = None
        for g in range(groups):
            blocks = [r[...] for r in right_refs[g::groups]]
            right = blocks[0] if len(blocks) == 1 else jnp.concatenate(blocks, 1)
            term = dot(left[g * rows : (g + 1) * rows], right, TN)
            total = term if total is None else total + term
        parts.append(total)
    return parts[0] if len(parts) == 1 else jnp.concatenate(parts, 1)


def away_kernel(sides, where_ref, *refs):
    refs[-1][0] = product(sides, refs[:-1]).astype(BF16)


def kept_kernel(sides, where_ref, *refs):
    refs, (arrived_ref, far1, keep1, far2, keep2) = refs[:-5], refs[-5:]
    step = pl.program_id(0)
    total = (product(sides, refs) + arrived_ref[0].astype(F32)).astype(BF16)
    half = total.shape[1] // 2

    @pl.when(step % 2 == 1)
    def _():
        far1[0] = total[:, :half]

    @pl.when(step % 2 == 0)
    def _():
        keep1[0] = total[:, :half]

    @pl.when(step >= 2)
    def _():
        far2[0] = total[:, half:]

    @pl.when(step < 2)
    def _():
        keep2[0] = total[:, half:]


def weight_shape(job):
    columns = [sum(r.shape[1] for r in rights) * rights[0].shape[0] // left.shape[0]
               for left, rights in job]
    return job[0][0].shape[1] // 8, sum(columns)


def weight_call(where, job, kernel, odd, more, out_specs, out_shape, name):
    rest, columns = weight_shape(job)
    specs, args = [], []
    for left, rights in job:
        specs.append(
            pl.BlockSpec(
                (left.shape[0], rest), lambda i, w: (0, jnp.bitwise_xor(w[0], 2 * i + odd))
            )
        )
        specs += [pl.BlockSpec(r.shape, lambda i, w: (0, 0)) for r in rights]
        args += [left, *rights]
    return pl.pallas_call(
        functools.partial(kernel, [len(rights) for _, rights in job]),
        grid_spec=pltpu.PrefetchScalarGridSpec(
            num_scalar_prefetch=1,
            grid=(4,),
            in_specs=specs
            + [pl.BlockSpec((1, rest, columns), lambda i, w: (i, 0, 0)) for _ in more],
            out_specs=out_specs,
        ),
        out_shape=out_shape,
        compiler_params=params(48),
        cost_estimate=cost(job[0][0].shape[0] * 8 * rest * columns, 8 * rest * columns),
        name=name,
    )(where, *placed(*args, *more))


def weight_away(where, job):
    rest, columns = weight_shape(job)
    return weight_call(
        where,
        job,
        away_kernel,
        1,
        [],
        pl.BlockSpec((1, rest, columns), lambda i, w: (i, 0, 0)),
        like((4, rest, columns), BF16),
        "weight_away",
    )


def weight_kept(where, job, arrived, ahead):
    rest, columns = weight_shape(job)
    two = like((2, rest, columns // 2), BF16)

    def spec(which):
        return pl.BlockSpec((1, rest, columns // 2), lambda i, w: (which(i), 0, 0))

    far1, keep1, far2, keep2 = weight_call(
        where,
        job,
        kept_kernel,
        0,
        [arrived],
        [
            spec(lambda i: i // 2),
            spec(lambda i: i // 2),
            spec(lambda i: jnp.maximum(i - 2, 0)),
            spec(lambda i: jnp.minimum(i, 1)),
        ],
        [two] * 4,
        "weight_kept",
    )
    if ahead:
        far1, far2 = after((far1, far2), ahead)
    return (keep1, flip(far1, 1, 8)), (keep2, flip(far2, 2, 8))


def second_kernel(keep1_ref, came1_ref, keep2_ref, came2_ref, *out_refs):
    far1, stay1, far2, stay2 = out_refs
    for keep_ref, came_ref, far, stay in (
        (keep1_ref, came1_ref, far1, stay1),
        (keep2_ref, came2_ref, far2, stay2),
    ):
        total = (keep_ref[...].astype(F32) + came_ref[...].astype(F32)).astype(BF16)
        stay[...] = total[0]
        far[...] = total[1]


def second_sums(first, before, ahead):
    (keep1, came1), (keep2, came2) = first
    keep1 = after(keep1, before)
    _, rest, half = keep1.shape
    rows = rest // 2
    spec = pl.BlockSpec((2, rows, half), lambda i: (0, i, 0))
    out = pl.BlockSpec((rows, half), lambda i: (i, 0))
    far1, stay1, far2, stay2 = pl.pallas_call(
        second_kernel,
        grid=(2,),
        in_specs=[spec] * 4,
        out_specs=[out] * 4,
        out_shape=[like((rest, half), BF16)] * 4,
        compiler_params=params(32),
        cost_estimate=cost(4 * rest * half, 24 * rest * half),
        name="second_sums",
    )(*placed(keep1, came1, keep2, came2))
    far1, far2 = after((far1, far2), ahead)
    return (stay1, flip(far1, 2, 8)), (stay2, flip(far2, 1, 8))


def spread_kernel(seq, where_ref, *refs):
    ins, outs = refs[:-seq], refs[-seq:]
    both = jnp.concatenate(
        [a[...].astype(F32) + b[...].astype(F32) for a, b in zip(ins[0::2], ins[1::2])], 1
    )
    for j, out_ref in enumerate(outs):

        @pl.when(pl.program_id(0) == j)
        def _(out_ref=out_ref):
            out_ref[...] = both.astype(out_ref.dtype)


def seq_spread(where, seconds, seq):
    arrays = [array for second in seconds for part in second for array in part]
    rest = arrays[0].shape[0]
    rows = rest // seq
    columns = sum(a.shape[1] for a in arrays[::2])
    blocks = [
        pl.BlockSpec((rows, a.shape[1]), lambda i, w: (lax.rem(w[1] + i, seq), 0)) for a in arrays
    ]
    out = pl.BlockSpec((rows, columns), lambda i, w: (0, 0))
    return pl.pallas_call(
        functools.partial(spread_kernel, seq),
        grid_spec=pltpu.PrefetchScalarGridSpec(
            num_scalar_prefetch=1, grid=(seq,), in_specs=blocks, out_specs=[out] * seq
        ),
        out_shape=[like((rows, columns), F32)] + [like((rows, columns), BF16)] * (seq - 1),
        compiler_params=params(32),
        cost_estimate=cost(rest * columns, 8 * rest * columns),
        name="seq_spread",
    )(where, *placed(*arrays))


def plain_sums(job, seq):
    blocks = []
    for left, rights in job:
        groups = left.shape[0] // rights[0].shape[0]
        right = jnp.concatenate([jnp.concatenate(rights[g::groups], 1) for g in range(groups)], 0)
        product = dot(left, right, TN)
        blocks.append(lax.psum_scatter(product, "fsdp", scatter_dimension=0, tiled=True))
    me = lax.axis_index("seq")
    parts = jnp.concatenate(blocks, 1)
    parts = parts.reshape(seq, parts.shape[0] // seq, parts.shape[1])
    chunks = [lax.dynamic_index_in_dim(parts, (me + j) % seq, 0, False) for j in range(seq)]
    return [chunks[0]] + [c.astype(BF16) for c in chunks[1:]]


def sum_vectors(vectors, fsdp, seq):
    me = lax.axis_index("fsdp")
    bits = fsdp.bit_length() - 1
    sizes = [v.shape[0] // (fsdp * seq) for v in vectors]
    block = jnp.concatenate([v.reshape(fsdp, seq, -1) for v in vectors], 2)
    block = block.reshape((2,) * bits + (seq, sum(sizes)))
    for bit in range(bits):
        axis = bits - 1 - bit
        mine = (me >> bit) & 1
        away = lax.dynamic_index_in_dim(block, 1 - mine, axis, False)
        block = lax.dynamic_index_in_dim(block, mine, axis, False) + flip(away, bit, fsdp)
    return block, sizes


def split_vectors(block, sizes, seq):
    place = lax.axis_index("seq")
    total = lax.dynamic_index_in_dim(block, place, 0, False)
    for by in range(1, seq):
        away = lax.dynamic_index_in_dim(block, (place + by) % seq, 0, False)
        total = total + shift(away, by, seq)
    return jnp.split(total, [sum(sizes[: i + 1]) for i in range(len(sizes) - 1)])


def after(value, *others):
    return lax.optimization_barrier((value, others))[0]


def spread_pairs(parts, seq):
    arrived = []
    for blocks in parts:
        if arrived:
            blocks = after(blocks, arrived[-1][1:])
        arrived.append([blocks[0]] + [shift(blocks[j], j, seq) for j in range(1, seq)])
    return [pair[j] for j in range(seq) for pair in arrived]


def on_device(
    fsdp,
    seq,
    inputs,
    clip_mask,
    ln1_gain,
    ln1_bias,
    w_query,
    b_query,
    w_key,
    w_value,
    b_value,
    w_out,
    b_out,
    ln2_gain,
    ln2_bias,
    w_fc1,
    b_fc1,
    w_fc2,
    b_fc2,
    cotangent,
):
    clips, local, width = inputs.shape
    assert clips == 1
    me = lax.axis_index("seq")
    where = jnp.stack([lax.axis_index("fsdp"), me]).astype(jnp.int32)
    present = clip_mask.astype(F32)
    own = width // seq
    pairs = own // PAIR
    table = piece_table(fsdp)
    x, cot = inputs[0], cotangent[0]
    grad_low = (cot.astype(F32) * present).astype(BF16)

    def columns(array, axis):
        return lax.dynamic_slice_in_dim(array, me * own, own, axis)

    shard_heads = jnp.concatenate([columns(w, 1) for w in (w_query, w_key, w_value)], 1)
    near_heads = gather_near(shard_heads, fsdp)
    down, up = [x], [x]
    for hop in range(1, seq):
        if hop == 2:
            down[-1], up[-1], near_heads = after((down[-1], up[-1], near_heads))
            w_heads = gather_pieces(shard_heads, near_heads, fsdp)
        if hop == 3:
            down[-1], up[-1] = after((down[-1], up[-1]), w_heads)
        down.append(lax.ppermute(down[-1], "seq", [(i, i - 1) for i in range(1, seq + 1 - hop)]))
        up.append(lax.ppermute(up[-1], "seq", [(i, i + 1) for i in range(hop - 1, seq - 1)]))
    b_heads = jnp.concatenate([columns(b_query, 0), jnp.zeros((own,), F32), columns(b_value, 0)])
    one = lax.all_gather(jnp.concatenate([w_out, w_fc1], 1), "fsdp", axis=0, tiled=True)
    two = lax.all_gather(after(w_fc2, down[1], up[1]), "fsdp", axis=0, tiled=True)
    shard_three = jnp.concatenate([w_query, w_key, w_value], 1)
    three = lax.all_gather(after(shard_three, down[2], up[2]), "fsdp", axis=0, tiled=True)

    norms = (ln1_gain, ln1_bias, b_heads)
    early = [x] + down[1:-1] + [x] + up[1:-1] + [x]
    first_in, qkv = project(where, seq, table, early, w_heads, *norms)
    first_in, qkv = project(
        where, seq, table, [x] + down[1:] + up[1:], w_heads, *norms, (first_in, qkv)
    )
    forward = [attention_forward(qkv, 0, pairs, seq)]
    for p in range(1, pairs):
        forward.append(attention_forward(qkv, p, pairs, seq))
    mixed = spread_pairs([part[:seq] for part in forward], seq)
    attended, middle, second_in, activ, slope = hidden_layer(
        where, seq, mixed, one, x, b_out, ln2_gain, ln2_bias, b_fc1, 512
    )
    parts = {}

    def away(name, job, before):
        if fsdp == 8:
            parts[name] = weight_away(after(where, before), job)
        else:
            parts[name] = plain_sums(job, seq)
        return parts[name]

    def kept(name, job, before, first=(), ahead=()):
        if fsdp != 8:
            return ()
        arrived = flip(after(parts[name], first), 0, 8)
        parts[name] = weight_kept(after(where, before), job, arrived, ahead)
        return parts[name][0][0]

    def second(name, before, ahead=()):
        if fsdp != 8:
            return ()
        parts[name] = second_sums(parts[name], before, ahead)
        return parts[name][0][0]

    def chunks(names, before):
        if fsdp == 8:
            return seq_spread(after(where, before), [parts[n] for n in names], seq)
        return [jnp.concatenate(blocks, 1) for blocks in zip(*[parts[n] for n in names])]

    def came(name):
        return (parts[name][0][1], parts[name][1][1]) if fsdp == 8 else ()

    def send(blocks, ahead):
        if ahead:
            blocks = after(blocks, ahead)
        return [blocks[0]] + [shift(blocks[j], j, seq) for j in range(1, seq)]

    low = [(activ, [grad_low])]
    step = away("low", low, ())
    output, grad_hidden, sum_fc1 = output_layer(
        after(where, step), present, two, activ, slope, middle, cot, b_fc2
    )
    step = kept("low", low, grad_hidden)
    high = [(second_in, [grad_hidden])]
    step = away("high", high, step)
    results = middle_layer(
        after(where, step), present, seq, one, grad_hidden, middle, cot, ln2_gain
    )
    grad_middle, grad_branch = results[:2]
    grad_mixed, sums2 = results[2 : 2 + seq], results[2 + seq]
    grads = [grad_mixed[0]] + [shift(grad_mixed[j], -j, seq) for j in range(1, seq)]
    low_came = came("low")
    step = second("low", (grad_branch, three))
    step = kept("high", high, step, (low_came, grad_branch), grads[1:])
    low_rows = chunks(["low"], step)
    step = low_rows[1]
    low_rows = send(low_rows, grads[1:])
    back, home = [], []
    for p in range(pairs):
        exact, lse = forward[p][seq:]
        back.append(attention_backward(qkv, grads, exact, after(lse, step), p, pairs, seq))
        home.append(send(back[-1], () if home else low_rows[1:]))
        step = back[-1][0]
    total_low = sum(rows.astype(F32) for rows in low_rows)
    step = second("high", step, home[0][1:])
    late = [(first_in, [b for pair in back for b in pair]), (attended, [grad_branch])]
    step = away("late", late, step)
    step = kept("late", late, step, home[0][1:], home[1][1:])
    high_rows = chunks(["high"], step)
    step = high_rows[1]
    high_rows = send(high_rows, home[1][1:])
    step = second("late", step)
    grad_inputs, sums1 = last_layer(
        after(where, step),
        seq,
        [pair[j] for j in range(seq) for pair in home],
        three,
        x,
        grad_middle,
        ln1_gain,
    )
    late_rows = chunks(["late"], sums1)

    def spread(which):
        vector = jnp.concatenate(
            [
                sum(
                    jnp.sum(block[:, which * PAIR : (which + 1) * PAIR].astype(F32), 0)
                    for block in back[p]
                )
                for p in range(pairs)
            ]
        )
        return lax.dynamic_update_slice(jnp.zeros((width,), F32), vector, (me * own,))

    sums1 = after(sums1, high_rows[1:], late_rows[1])
    block, sizes = sum_vectors(
        [sums1[0], sums1[1], spread(0), spread(2)] + [sums2[i] for i in range(4)] + [sum_fc1[0]],
        fsdp,
        seq,
    )
    split = 3 * own
    sent = send(late_rows, high_rows[1:])
    rows = after(sent, block)
    total_out = sum(part[:, split:].astype(F32) for part in rows)
    total_high = sum(part.astype(F32) for part in high_rows)
    heads = [part[:, :split].astype(F32) for part in rows[::-1]]
    grad_heads = lax.dynamic_slice_in_dim(jnp.stack(heads + heads), (seq - 1 - me) % seq, seq, 0)
    strip = grad_heads.shape[1]
    grad_heads = grad_heads.reshape(seq, strip, pairs, 3, PAIR).transpose(3, 1, 0, 2, 4)
    grad_heads = grad_heads.reshape(3, strip, width)

    sums = split_vectors(after(block, sent[1:]), sizes, seq)
    return (
        output[None],
        grad_inputs[None],
        sums[0],
        sums[1],
        grad_heads[0],
        sums[2],
        grad_heads[1],
        grad_heads[2],
        sums[3],
        total_out,
        sums[4],
        sums[5],
        sums[6],
        total_high,
        sums[8],
        total_low,
        sums[7],
    )


def solution(mesh):
    rows, both = P("fsdp", None), P(("fsdp", "seq"))
    tokens = P("fsdp", "seq", None)
    matrix = P(("fsdp", "seq"), None)
    return jax.shard_map(
        functools.partial(on_device, mesh.shape["fsdp"], mesh.shape["seq"]),
        mesh=mesh,
        in_specs=(
            tokens,
            P("fsdp"),
            P(),
            P(),
            rows,
            P(),
            rows,
            rows,
            P(),
            rows,
            P(),
            P(),
            P(),
            rows,
            P(),
            rows,
            P(),
            tokens,
        ),
        out_specs=(
            tokens,
            tokens,
            both,
            both,
            matrix,
            both,
            matrix,
            matrix,
            both,
            matrix,
            both,
            both,
            both,
            matrix,
            both,
            matrix,
            both,
        ),
        check_vma=False,
    )
```
